32 devices in a mesh: batch: 16 (over z, x, core), seq: 2 (over y).
Axes of the slice: x: 2, y: 2, z: 4, core: 2. Of those that a mesh axis runs over, the one named last changes fastest.
Arguments:
- hidden: bfloat16 [16, 448, 768], P('batch', 'seq'), may hold values from -6 to 6
- encoder: bfloat16 [16, 1536, 768], P(None, ('batch', 'seq')), may hold values from -6 to 6
- cotangent: bfloat16 [16, 448, 768], P('batch', 'seq'), may hold values from -6 to 6
- token_offsets: int32 [16], P('batch'), may hold values from 0 to 336, as said below
- token_lengths: int32 [16], P('batch'), may hold values from 112 to 448, as said below
- frame_counts: int32 [16], P('batch'), may hold values from 375 to 1500, as said below
- corpus_ids: int32 [16], P('batch'), may hold values from 0 to 8
- corpus_weights: float32 [9], replicated, may hold values from 0.25 to 4
- norm_gains: bfloat16 [768, 4], P('batch'), may hold values from 0.5 to 1.5
- norm_shifts: bfloat16 [768, 4], P('batch'), may hold values from -1 to 1
- self_in: bfloat16 [768, 2304], P('batch'), may hold values from -0.21875 to 0.21875
- self_out: bfloat16 [768, 768], P('batch'), may hold values from -0.875 to 0.875
- cross_query: bfloat16 [768, 768], P('batch'), may hold values from -0.21875 to 0.21875
- cross_kv: bfloat16 [768, 1536], P('batch'), may hold values from -0.21875 to 0.21875
- cross_out: bfloat16 [768, 768], P('batch'), may hold values from -1.25 to 1.25
- proj_bias: bfloat16 [768, 7], P('batch'), may hold values from -1 to 1
- up_weight: bfloat16 [768, 3072], P('batch'), may hold values from -0.21875 to 0.21875
- up_bias: bfloat16 [3072], P('batch'), may hold values from -1 to 1
- down_weight: bfloat16 [3072, 768], P('batch'), may hold values from -0.109375 to 0.109375
Outputs:
- layer_out: bfloat16 [16, 448, 768], P('batch', 'seq')
- grad_hidden: float32 [16, 448, 768], P('batch', 'seq')
- grad_encoder: float32 [16, 1536, 768], P(None, ('batch', 'seq'))
- grad_norm_gains: float32 [768, 4], P('batch')
- grad_norm_shifts: float32 [768, 4], P('batch')
- grad_self_in: float32 [768, 2304], P('batch')
- grad_self_out: float32 [768, 768], P('batch')
- grad_cross_query: float32 [768, 768], P('batch')
- grad_cross_kv: float32 [768, 1536], P('batch')
- grad_cross_out: float32 [768, 768], P('batch')
- grad_proj_bias: float32 [768, 7], P('batch')
- grad_up_weight: float32 [768, 3072], P('batch')
- grad_up_bias: float32 [3072], P('batch')
- grad_down_weight: float32 [3072, 768], P('batch')
The draws below stay inside these ranges and needn't reach their ends.
Inputs may be any that keep to these rules, and one draw needn't show every extreme that they name: `token_lengths`: some sequence has exactly 448 live tokens and some exactly 112. token_offsets + token_lengths <= 448 for every sequence. The valid frames of a sequence are its first frame_counts slots; some sequence has exactly 1500.
All inputs are finite; a program needn't handle non-finite values.
Results may differ from the reference program's by a relative error of at most 0.023.
Values may be sent and summed in bfloat16 or wider, within the bound.
No kernel may reach another device: no remote copies, remote signals or barrier semaphores. Data moves between devices by JAX's collectives and lax.ppermute only.
A program may use at most 192 MiB of HBM per device.

```python
import math
import jax
import jax.numpy as jnp
from jax import lax

D = 768
HEADS = 12
HEAD_DIM = 64
FF = 3072
LEN = 448
MAX_FRAMES = 1500
FRAMES = 1536
CORPORA = 9
SEQS = 16


def lengths_and_offsets(key):
    base = jax.random.fold_in(key, 11)
    lengths = jax.random.randint(jax.random.fold_in(base, 1), (SEQS,), LEN // 4, LEN + 1)
    lengths = lengths.at[0].set(LEN).at[1].set(LEN // 4)
    room = LEN - lengths + 1
    offsets = jax.random.randint(jax.random.fold_in(base, 2), (SEQS,), 0, room)
    offsets = offsets.at[1].set(LEN - LEN // 4)
    return (lengths.astype(jnp.int32), offsets.astype(jnp.int32))


def draw_token_lengths(key, part):
    return lengths_and_offsets(key)[0]


def draw_token_offsets(key, part):
    return lengths_and_offsets(key)[1]


def draw_frame_counts(key, part):
    counts = jax.random.randint(jax.random.fold_in(key, 23), (SEQS,), MAX_FRAMES // 4, MAX_FRAMES + 1)
    counts = counts.at[0].set(MAX_FRAMES).at[1].set(MAX_FRAMES // 4)
    return counts.astype(jnp.int32)


def place_ends(result, rng, smallest, top_value):
    extent = result.shape
    place = [jax.random.randint(jax.random.fold_in(rng, axis), (), 0, extent[axis]) for axis in range(len(extent))]
    result = result.at[tuple(place)].set(smallest)
    longest = extent.index(max(extent))
    place[longest] = (place[longest] + 1) % extent[longest]
    return result.at[tuple(place)].set(top_value)


def raised(result, rng, source, target, blocks, factor):
    owner, partner = [(jnp.arange(result.shape[axis_at]) // (result.shape[axis_at] // blocks)).reshape([-1 if axis == axis_at else 1 for axis in range(result.ndim)]) for axis_at in (source, target)]
    chosen = jax.random.permutation(rng, blocks)[partner]
    strong = (owner == chosen) | (owner == (partner + blocks // 2) % blocks)
    return jnp.where(strong, factor * result, result)


def block_scale(stream_key, shape, pieces, low, top_value):
    factor_of, own = 1.0, jax.random.fold_in(stream_key, 6)
    for axis_at, blocks in pieces:
        draws = jnp.exp(jax.random.uniform(jax.random.fold_in(own, axis_at), (blocks,), jnp.float32, low / len(pieces), top_value / len(pieces)))
        factor_of = factor_of * jnp.repeat(draws, shape[axis_at] // blocks).reshape([-1 if axis == axis_at else 1 for axis in range(len(shape))])
    return factor_of


def centred(stream_key, shape, scale, most, shards=(), kind=jnp.bfloat16):
    drawn = scale * jax.random.normal(stream_key, shape, jnp.float32)
    if shards:
        drawn = drawn * block_scale(stream_key, shape, shards, -0.22, 0.18)
    return jnp.clip(drawn, -most, most).astype(kind)


def gaussian_with(key, shape, deviation, bound, pieces, heavy, kind=jnp.bfloat16):
    entries = deviation * jax.random.normal(key, shape, jnp.float32)
    if pieces:
        entries = entries * block_scale(key, shape, pieces, -0.22, 0.18)
    return jnp.clip(raised(entries, jax.random.fold_in(key, 3), *heavy), -bound, bound).astype(kind)


def setup_inputs(seed: int = 0) -> dict:
    arg_keys = jax.random.split(jax.random.key(seed), 20)
    hidden = gaussian_with(arg_keys[0], (SEQS, LEN, D), 1.0, 6.0, ((0, 16), (1, 2)), (0, 2, 16, 2.0))
    encoder = centred(arg_keys[1], (SEQS, FRAMES, D), 1.0, 6.0, ((1, 32),))
    cotangent = centred(arg_keys[2], (SEQS, LEN, D), 1.0, 6.0, ((0, 16), (1, 2)))
    token_offsets = draw_token_offsets(jax.random.fold_in(arg_keys[19], 71), 0)
    token_lengths = draw_token_lengths(jax.random.fold_in(arg_keys[19], 71), 0)
    frame_counts = draw_frame_counts(jax.random.fold_in(arg_keys[19], 71), 0)
    corpus_ids = place_ends(jax.random.randint(arg_keys[6], (SEQS,), 0, CORPORA), jax.random.fold_in(arg_keys[6], 1), 0, CORPORA - 1).astype(jnp.int32)
    corpus_weights = jnp.clip(jnp.exp(jax.random.uniform(arg_keys[7], (CORPORA,), jnp.float32, math.log(0.25), math.log(4.0))), 0.25, 4.0)
    norm_gains = jnp.clip(1.0 + 0.1 * jax.random.normal(arg_keys[8], (D, 4), jnp.float32), 0.5, 1.5).astype(jnp.bfloat16)
    norm_shifts = centred(arg_keys[9], (D, 4), 0.2, 1.0, ((0, 16),))
    self_in = centred(arg_keys[10], (D, 3 * D), D ** -0.5, 0.21875, ((0, 16),))
    self_out = centred(arg_keys[11], (D, D), (D // 16) ** -0.5, 0.875, ((0, 16),))
    cross_query = centred(arg_keys[12], (D, D), D ** -0.5, 0.21875, ((0, 16),))
    cross_kv = centred(arg_keys[13], (D, 2 * D), D ** -0.5, 0.21875, ((0, 16),))
    cross_out = centred(arg_keys[14], (D, D), (D // 32) ** -0.5, 1.25, ((0, 16),))
    proj_bias = centred(arg_keys[15], (D, 7), 0.2, 1.0, ((0, 16),))
    up_weight = centred(arg_keys[16], (D, FF), D ** -0.5, 0.21875, ((0, 16),))
    up_bias = centred(arg_keys[17], (FF,), 0.2, 1.0, ((0, 16),))
    down_weight = centred(arg_keys[18], (FF, D), FF ** -0.5, 0.109375, ((0, 16),))
    return {"hidden": hidden, "encoder": encoder, "cotangent": cotangent, "token_offsets": token_offsets, "token_lengths": token_lengths, "frame_counts": frame_counts, "corpus_ids": corpus_ids, "corpus_weights": corpus_weights, "norm_gains": norm_gains, "norm_shifts": norm_shifts, "self_in": self_in, "self_out": self_out, "cross_query": cross_query, "cross_kv": cross_kv, "cross_out": cross_out, "proj_bias": proj_bias, "up_weight": up_weight, "up_bias": up_bias, "down_weight": down_weight}


EPS = 1e-05
HIGH = lax.Precision.HIGHEST

@jax.custom_vjp
def low(v):
    return lax.optimization_barrier(v.astype(jnp.bfloat16)).astype(jnp.float32)

@jax.custom_vjp
def low_back(v):
    return v

def low_keep(v):
    return (low(v), None)

def low_pass(kept, grad):
    return (grad,)

def back_keep(v):
    return (v, None)

def back_low(kept, grad):
    return (low(grad),)
low.defvjp(low_keep, low_pass)
low_back.defvjp(back_keep, back_low)

def layer_norm(values, gain, shift):
    center = values - lax.optimization_barrier(jnp.mean(values, axis=-1, keepdims=True))
    inv_std = lax.rsqrt(lax.optimization_barrier(jnp.mean(center * center, axis=-1, keepdims=True)) + EPS)
    return center * inv_std * gain + shift

def project(left_side, right_side):
    return jnp.einsum('...i,ij->...j', left_side, right_side, precision=HIGH)

def attention(queries, keys_all, values_all, key_mask):
    seq_count, row_count, model_width = queries.shape
    key_count = keys_all.shape[1]
    query_heads = queries.reshape(seq_count, row_count, HEADS, HEAD_DIM)
    key_heads = keys_all.reshape(seq_count, key_count, HEADS, HEAD_DIM)
    value_heads = values_all.reshape(seq_count, key_count, HEADS, HEAD_DIM)
    scores = low_back(jnp.einsum('bqhd,bkhd->bhqk', query_heads, key_heads, precision=HIGH) * HEAD_DIM ** (-0.5))
    scores = jnp.where(key_mask[:, None], scores, -jnp.inf)
    probability = low(jax.nn.softmax(scores, axis=-1))
    mixed_heads = jnp.einsum('bhqk,bkhd->bqhd', probability, value_heads, precision=HIGH)
    return low_back(low(mixed_heads.reshape(seq_count, row_count, model_width)))

def decoder_layer(inputs, states, weight_set, self_mask, frame_mask):
    gain_cols, shifts, self_in, self_out, cross_query, cross_kv, cross_out, biases, up_weight, up_bias, down_weight = weight_set
    model_width = inputs.shape[-1]
    zero_row = jnp.zeros((model_width,), jnp.float32)
    act_one = low(layer_norm(inputs, gain_cols[:, 0], shifts[:, 0]))
    qkv_bias = jnp.concatenate([biases[:, 0], zero_row, biases[:, 1]])
    qkv_all = low_back(low(project(act_one, self_in) + qkv_bias))
    self_mixed = attention(qkv_all[..., :model_width], qkv_all[..., model_width:2 * model_width], qkv_all[..., 2 * model_width:], self_mask)
    after_self = inputs + low_back(project(self_mixed, self_out) + biases[:, 2])
    act_two = low(layer_norm(after_self, gain_cols[:, 1], shifts[:, 1]))
    cross_queries = low_back(low(project(act_two, cross_query) + biases[:, 3]))
    kv_bias = jnp.concatenate([zero_row, biases[:, 4]])
    cross_pairs = low_back(low(project(states, cross_kv) + kv_bias))
    cross_mixed = attention(cross_queries, cross_pairs[..., :model_width], cross_pairs[..., model_width:], frame_mask)
    after_cross = after_self + low_back(project(cross_mixed, cross_out) + biases[:, 5])
    act_three = low(layer_norm(after_cross, gain_cols[:, 2], shifts[:, 2]))
    up_value = low_back(project(act_three, up_weight) + up_bias)
    hidden_act = low(jax.nn.gelu(up_value, approximate=False))
    after_mlp = after_cross + low_back(project(hidden_act, down_weight) + biases[:, 6])
    return layer_norm(after_mlp, gain_cols[:, 3], shifts[:, 3])

def reference(hidden, encoder, cotangent, token_offsets, token_lengths, frame_counts, corpus_ids, corpus_weights, norm_gains, norm_shifts, self_in, self_out, cross_query, cross_kv, cross_out, proj_bias, up_weight, up_bias, down_weight):
    weight_set = tuple((item.astype(jnp.float32) for item in (norm_gains, norm_shifts, self_in, self_out, cross_query, cross_kv, cross_out, proj_bias, up_weight, up_bias, down_weight)))
    group_size = 8
    positions = jnp.arange(LEN, dtype=jnp.int32)
    frame_slots = jnp.arange(FRAMES, dtype=jnp.int32)
    seq_weight = corpus_weights[corpus_ids]

    def group_step(totals, group_index):
        first_seq = (group_index * group_size).astype(jnp.int32)

        def take_rows(array):
            return lax.dynamic_slice_in_dim(array, first_seq, group_size, 0)
        offsets = take_rows(token_offsets)
        lengths = take_rows(token_lengths)
        key_pos = positions[None, None, :]
        query_pos = positions[None, :, None]
        self_mask = (key_pos <= query_pos) & ((key_pos >= offsets[:, None, None]) | (key_pos == query_pos))
        frame_mask = frame_slots[None, None, :] < take_rows(frame_counts)[:, None, None]
        live_rows = (positions[None, :] >= offsets[:, None]) & (positions[None, :] < (offsets + lengths)[:, None])
        grad_out = take_rows(cotangent).astype(jnp.float32) * jnp.where(live_rows, take_rows(seq_weight)[:, None], 0.0)[..., None]

        def forward(inputs, states, *weights_in):
            return decoder_layer(inputs, states, weights_in, self_mask, frame_mask)
        layer_out, pull_back = jax.vjp(forward, take_rows(hidden).astype(jnp.float32), take_rows(encoder).astype(jnp.float32), *weight_set)
        grad_list = pull_back(grad_out)
        totals = tuple((total + grad_item for total, grad_item in zip(totals, grad_list[2:])))
        return (totals, (layer_out.astype(jnp.bfloat16), grad_list[0], grad_list[1]))
    start_totals = tuple((jnp.zeros_like(item) for item in weight_set))
    totals, (outputs, grad_rows, grad_states) = lax.scan(group_step, start_totals, jnp.arange(SEQS // group_size, dtype=jnp.int32))
    return (outputs.reshape(SEQS, LEN, D), grad_rows.reshape(SEQS, LEN, D), grad_states.reshape(SEQS, FRAMES, D), totals[0], totals[1], totals[2], totals[3], totals[4], totals[5], totals[6], totals[7], totals[8], totals[9], totals[10])
```

```python
from functools import partial
import math

import jax
import jax.numpy as jnp
from jax import lax
from jax.experimental import pallas as pl
from jax.experimental.pallas import tpu as pltpu
from jax.sharding import PartitionSpec as P

HEADS = 12
HEAD_DIM = 64


EPS = 1e-05


def layer_parts(values):
    center = values - jnp.mean(values, axis=-1, keepdims=True)
    inv_std = lax.rsqrt(jnp.mean(center * center, axis=-1, keepdims=True) + EPS)
    return (center * inv_std, inv_std)


def layer_back(grad_side, normed, inv_std, gain):
    scaled = grad_side * gain
    mean_one = jnp.mean(scaled, axis=-1, keepdims=True)
    mean_two = jnp.mean(scaled * normed, axis=-1, keepdims=True)
    grad_in = inv_std * (scaled - mean_one - normed * mean_two)
    return (grad_in, jnp.sum(grad_side * normed, axis=(0, 1)), jnp.sum(grad_side, axis=(0, 1)))


def dot_right(left_side, weight):
    return jnp.dot(left_side, weight, preferred_element_type=jnp.float32)


def dot_left(grad_side, weight):
    return jnp.einsum("bcj,ij->bci", grad_side, weight, preferred_element_type=jnp.float32)


def weight_term(left_side, grad_side):
    return jnp.einsum("bci,bcj->ij", left_side, grad_side, preferred_element_type=jnp.float32)


def col_sum(grad_side):
    return jnp.sum(grad_side, axis=(0, 1), dtype=jnp.float32)


def head_step():
    return math.gcd(HEADS, 4)


def attend(queries, key_value, key_mask):
    seq_count, row_count, feat_width = queries.shape
    key_count = key_value.shape[1]
    heads_step = head_step()
    span_width = heads_step * HEAD_DIM
    score_scale = HEAD_DIM ** (-0.5)

    def head_block(group_index, state_pair):
        result, log_total = state_pair
        col_start = group_index * span_width
        query_heads = lax.dynamic_slice_in_dim(queries, col_start, span_width, 2).reshape(
            seq_count, row_count, heads_step, HEAD_DIM
        )
        key_heads = lax.dynamic_slice_in_dim(key_value, col_start, span_width, 2).reshape(
            seq_count, key_count, heads_step, HEAD_DIM
        )
        value_heads = lax.dynamic_slice_in_dim(
            key_value, feat_width + col_start, span_width, 2
        ).reshape(seq_count, key_count, heads_step, HEAD_DIM)
        scores = (
            jnp.einsum(
                "bqhd,bkhd->bhqk", query_heads, key_heads, preferred_element_type=jnp.float32
            )
            * score_scale
        )
        scores = jnp.where(key_mask[:, None], scores, -jnp.inf)
        row_top = jnp.max(scores, axis=-1, keepdims=True)
        exp_terms = jnp.exp(scores - row_top)
        row_total = jnp.sum(exp_terms, axis=-1, keepdims=True)
        probability = (exp_terms / row_total).astype(jnp.bfloat16)
        mixed_heads = jnp.einsum(
            "bhqk,bkhd->bqhd", probability, value_heads, preferred_element_type=jnp.float32
        )
        result = lax.dynamic_update_slice_in_dim(
            result,
            mixed_heads.reshape(seq_count, row_count, span_width).astype(jnp.bfloat16),
            col_start,
            2,
        )
        log_total = lax.dynamic_update_slice_in_dim(
            log_total, (row_top + jnp.log(row_total))[..., 0], group_index * heads_step, 1
        )
        return (result, log_total)

    start_state = (
        jnp.zeros((seq_count, row_count, feat_width), jnp.bfloat16),
        jnp.zeros((seq_count, HEADS, row_count), jnp.float32),
    )
    return lax.fori_loop(0, feat_width // span_width, head_block, start_state)


def attend_back(queries, key_value, key_mask, log_total, grad_mixed):
    seq_count, row_count, feat_width = queries.shape
    key_count = key_value.shape[1]
    heads_step = head_step()
    span_width = heads_step * HEAD_DIM
    score_scale = HEAD_DIM ** (-0.5)

    def head_block(group_index, state_pair):
        grad_queries, grad_pairs = state_pair
        col_start = group_index * span_width
        query_heads = lax.dynamic_slice_in_dim(queries, col_start, span_width, 2).reshape(
            seq_count, row_count, heads_step, HEAD_DIM
        )
        key_heads = lax.dynamic_slice_in_dim(key_value, col_start, span_width, 2).reshape(
            seq_count, key_count, heads_step, HEAD_DIM
        )
        value_heads = lax.dynamic_slice_in_dim(
            key_value, feat_width + col_start, span_width, 2
        ).reshape(seq_count, key_count, heads_step, HEAD_DIM)
        grad_heads = lax.dynamic_slice_in_dim(grad_mixed, col_start, span_width, 2).reshape(
            seq_count, row_count, heads_step, HEAD_DIM
        )
        block_total = lax.dynamic_slice_in_dim(log_total, group_index * heads_step, heads_step, 1)
        scores = (
            jnp.einsum(
                "bqhd,bkhd->bhqk", query_heads, key_heads, preferred_element_type=jnp.float32
            )
            * score_scale
        )
        probability = jnp.where(key_mask[:, None], jnp.exp(scores - block_total[..., None]), 0.0)
        grad_prob = jnp.einsum(
            "bqhd,bkhd->bhqk", grad_heads, value_heads, preferred_element_type=jnp.float32
        )
        grad_value = jnp.einsum(
            "bhqk,bqhd->bkhd",
            probability.astype(jnp.bfloat16),
            grad_heads,
            preferred_element_type=jnp.float32,
        )
        row_dot = jnp.sum(probability * grad_prob, axis=-1, keepdims=True)
        grad_scores = (probability * (grad_prob - row_dot)).astype(jnp.bfloat16)
        grad_query = (
            jnp.einsum(
                "bhqk,bkhd->bqhd", grad_scores, key_heads, preferred_element_type=jnp.float32
            )
            * score_scale
        )
        grad_key = (
            jnp.einsum(
                "bhqk,bqhd->bkhd", grad_scores, query_heads, preferred_element_type=jnp.float32
            )
            * score_scale
        )
        grad_queries = lax.dynamic_update_slice_in_dim(
            grad_queries, grad_query.reshape(seq_count, row_count, span_width), col_start, 2
        )
        grad_pairs = lax.dynamic_update_slice_in_dim(
            grad_pairs, grad_key.reshape(seq_count, key_count, span_width), col_start, 2
        )
        grad_pairs = lax.dynamic_update_slice_in_dim(
            grad_pairs,
            grad_value.reshape(seq_count, key_count, span_width),
            feat_width + col_start,
            2,
        )
        return (grad_queries, grad_pairs)

    start_state = (
        jnp.zeros((seq_count, row_count, feat_width), jnp.float32),
        jnp.zeros((seq_count, key_count, 2 * feat_width), jnp.float32),
    )
    return lax.fori_loop(0, feat_width // span_width, head_block, start_state)


CORES = 2
PAIR = 2
FLIP = [(0, 1), (1, 0)]


def partners(stride, radix, step):
    pairs = []
    for i in range(lax.axis_size("batch")):
        digit = i // stride % radix
        pairs.append((i, i + ((digit ^ step) - digit) * stride))
    return pairs


def swap(block, stride, radix=2, step=1):
    return lax.ppermute(block, "batch", partners(stride, radix, step))


def swap_seq(block):
    return lax.ppermute(block, "seq", FLIP)


def place_of():
    batch = lax.axis_index("batch")
    return (
        batch // (CORES * PAIR),
        batch // CORES % PAIR,
        batch % CORES,
        lax.axis_index("seq"),
    )


def splits(rows):
    depth = lax.axis_size("batch") // (CORES * PAIR)
    return rows % 48 == 0 and depth == 4 and lax.axis_size("seq") == 2


def place_kernel(where_ref, *refs, depth, rows):
    pieces, out_ref, sem = refs[:8], refs[8], refs[9]
    third = rows // 3
    deep, wide, core, seq = where_ref[0], where_ref[1], where_ref[2], where_ref[3]
    started = []
    for c in range(2):
        column, across, side, side_across = pieces[4 * c : 4 * c + 4]
        for w, (body, edge) in enumerate(((column, side), (across, side_across))):
            for k in range(depth):
                base = (((deep ^ k) * PAIR + (wide ^ w)) * CORES + (core ^ c)) * rows
                for source, start, count in (
                    (body, base + seq * third, 2 * third),
                    (edge, base + (1 - seq) * 2 * third, third),
                ):
                    copy = pltpu.make_async_copy(
                        source.at[k], out_ref.at[pl.ds(pl.multiple_of(start, 16), count)], sem
                    )
                    copy.start()
                    started.append(copy)
    for copy in started:
        copy.wait()


def gather_rows(shard):
    rows, cols = shard.shape
    if not splits(rows):
        return lax.all_gather(shard, "batch", axis=0, tiled=True)
    third = rows // 3
    size = lax.axis_size("batch")
    depth = size // (CORES * PAIR)
    deep, wide, core, seq = place_of()
    part = lax.dynamic_slice_in_dim(shard, seq * third, 2 * third, 0)
    column = jnp.stack(
        [part] + [swap(part, CORES * PAIR, depth, k) for k in range(1, depth)]
    )
    across = swap(column, CORES)
    side = swap_seq(lax.dynamic_slice_in_dim(column, seq * third, third, 1))
    side_across = swap_seq(lax.dynamic_slice_in_dim(across, seq * third, third, 1))
    mine = (column, across, side, side_across)
    other = tuple(swap(piece, 1) for piece in mine)
    total = size * rows
    return pl.pallas_call(
        partial(place_kernel, depth=depth, rows=rows),
        out_shape=jax.ShapeDtypeStruct((total, cols), shard.dtype),
        in_specs=[pl.BlockSpec(memory_space=pltpu.SMEM)]
        + [pl.BlockSpec(memory_space=pl.ANY)] * 8,
        out_specs=pl.BlockSpec(memory_space=pltpu.VMEM),
        scratch_shapes=[pltpu.SemaphoreType.DMA],
        cost_estimate=pl.CostEstimate(
            flops=0, transcendentals=0, bytes_accessed=4 * total * cols
        ),
        name="place_rows",
    )(jnp.stack([deep, wide, core, seq]).astype(jnp.int32), *mine, *other)


def narrow(values):
    return lax.reduce_precision(values, 8, 7).astype(jnp.bfloat16)


def reduce_rows(grads):
    size = lax.axis_size("batch")
    rows, cols = grads.shape[0] // size, grads.shape[1]
    grads = grads.astype(jnp.bfloat16)
    if not splits(rows):
        mine = lax.psum_scatter(grads, "batch", scatter_dimension=0, tiled=True)
        return lax.psum(mine, "seq").astype(jnp.float32)
    third = rows // 3
    depth = size // (CORES * PAIR)
    deep, wide, core, seq = place_of()
    grid = grads.reshape(depth, PAIR, CORES, rows, cols)
    pick = lax.dynamic_index_in_dim
    came = swap(pick(grid, 1 - core, 2, keepdims=False), 1)
    chip = pick(grid, core, 2, keepdims=False).astype(jnp.float32) + came.astype(jnp.float32)
    edge = lax.dynamic_slice_in_dim(chip, (1 - seq) * 2 * third, third, 2)
    came = swap_seq(edge.astype(jnp.bfloat16)).astype(jnp.float32)
    kept = lax.dynamic_slice_in_dim(chip, seq * third, 2 * third, 2)
    blank = jnp.zeros_like(came)
    kept = kept + jnp.where(
        seq == 0, jnp.concatenate([came, blank], axis=2), jnp.concatenate([blank, came], axis=2)
    )
    came = swap(pick(kept, 1 - wide, 1, keepdims=False).astype(jnp.bfloat16), CORES)
    pair = pick(kept, wide, 1, keepdims=False) + came.astype(jnp.float32)
    total = pick(pair, deep, 0, keepdims=False)
    for k in range(1, depth):
        came = swap(
            pick(pair, deep ^ k, 0, keepdims=False).astype(jnp.bfloat16), CORES * PAIR, depth, k
        )
        total = total + came.astype(jnp.float32)
    mine = narrow(total)
    came = swap_seq(mine)
    low = jnp.where(seq == 0, mine, came).astype(jnp.float32)
    high = jnp.where(seq == 0, came, mine).astype(jnp.float32)
    return jnp.concatenate([low[:third], low[third:] + high[:third], high[third:]], axis=0)


def body(
    hidden,
    encoder,
    cotangent,
    token_offsets,
    token_lengths,
    frame_counts,
    corpus_ids,
    corpus_weights,
    norm_gains,
    norm_shifts,
    self_in,
    self_out,
    cross_query,
    cross_kv,
    cross_out,
    proj_bias,
    up_weight,
    up_bias,
    down_weight,
):
    model_width = hidden.shape[2]
    shard_rows = norm_gains.shape[0]
    wide_cols = up_weight.shape[1]
    blocks = wide_cols // model_width
    size = lax.axis_size("batch")

    tail_width = 128
    small = jnp.concatenate(
        [norm_gains, norm_shifts, proj_bias, up_bias.reshape(shard_rows, blocks)], axis=1
    )
    small_cols = small.shape[1]
    small = jnp.pad(small, ((0, 0), (0, tail_width - small_cols)))
    first_all = gather_rows(jnp.concatenate([self_in, small], axis=1))
    second_all = gather_rows(
        jnp.concatenate([self_out, cross_query, cross_kv, cross_out], axis=1)
    )
    up_blocks = up_weight.reshape(shard_rows, blocks, model_width).transpose(1, 0, 2)
    third_all = lax.all_gather(
        jnp.concatenate([up_blocks.reshape(-1, model_width), down_weight], axis=1),
        "batch",
        axis=0,
        tiled=True,
    )
    frame_mine = lax.all_to_all(encoder, "batch", split_axis=0, concat_axis=1, tiled=True)
    frame_other = swap_seq(frame_mine)
    hidden_other = swap_seq(hidden)

    self_in_all = first_all[:, : 3 * model_width]
    small_all = first_all[:, 3 * model_width : 3 * model_width + small_cols]
    self_out_all = second_all[:, :model_width]
    query_all = second_all[:, model_width : 2 * model_width]
    kv_all = second_all[:, 2 * model_width : 4 * model_width]
    cross_out_all = second_all[:, 4 * model_width :]
    down_all = third_all[:, model_width:]
    up_all = (
        third_all[:, :model_width]
        .reshape(size, blocks, shard_rows, model_width)
        .transpose(0, 2, 1, 3)
        .reshape(model_width, wide_cols)
    )
    gains = small_all[:, :4].astype(jnp.float32)
    shifts = small_all[:, 4:8].astype(jnp.float32)
    biases = small_all[:, 8:15].astype(jnp.float32)
    up_bias_all = small_all[:, 15:].reshape(-1).astype(jnp.float32)

    seq_count, row_count, _ = hidden.shape
    seq_index = lax.axis_index("seq")
    slots = jnp.arange(row_count, dtype=jnp.int32)
    positions = seq_index * row_count + slots
    positions_other = (1 - seq_index) * row_count + slots
    offsets = token_offsets[:, None]
    zero_row = jnp.zeros((model_width,), jnp.float32)
    inputs = hidden.astype(jnp.float32)
    normed_one, scale_one = layer_parts(inputs)
    act_one = (normed_one * gains[:, 0] + shifts[:, 0]).astype(jnp.bfloat16)
    normed_far, _ = layer_parts(hidden_other.astype(jnp.float32))
    act_far = (normed_far * gains[:, 0] + shifts[:, 0]).astype(jnp.bfloat16)
    qkv_bias = jnp.concatenate([biases[:, 0], zero_row, biases[:, 1]])
    qkv_local = (dot_right(act_one, self_in_all) + qkv_bias).astype(jnp.bfloat16)
    self_query = qkv_local[..., :model_width]
    pair_far = (
        dot_right(act_far, self_in_all[:, model_width:]) + qkv_bias[model_width:]
    ).astype(jnp.bfloat16)
    self_pairs = jnp.concatenate([pair_far, qkv_local[..., model_width:]], axis=1)
    key_pos = jnp.concatenate([positions_other, positions])[None, None, :]
    query_pos = positions[None, :, None]
    self_mask = (key_pos <= query_pos) & ((key_pos >= offsets[:, :, None]) | (key_pos == query_pos))
    self_mixed, self_total = attend(self_query, self_pairs, self_mask)
    after_self = inputs + dot_right(self_mixed, self_out_all) + biases[:, 2]
    normed_two, scale_two = layer_parts(after_self)
    act_two = (normed_two * gains[:, 1] + shifts[:, 1]).astype(jnp.bfloat16)
    cross_queries = (dot_right(act_two, query_all) + biases[:, 3]).astype(jnp.bfloat16)
    frames = jnp.concatenate([frame_mine, frame_other], axis=1)
    kv_bias = jnp.concatenate([zero_row, biases[:, 4]])
    cross_pairs = (dot_right(frames, kv_all) + kv_bias).astype(jnp.bfloat16)
    half_slots = frame_mine.shape[1]
    owner_frames = encoder.shape[1]
    gathered = jnp.arange(2 * half_slots, dtype=jnp.int32)
    half_index = (gathered // half_slots) ^ seq_index
    within = gathered % half_slots
    frame_ids = (within // owner_frames * 2 + half_index) * owner_frames + within % owner_frames
    frame_mask = frame_ids[None, None, :] < frame_counts[:, None, None]
    cross_mixed, cross_total = attend(cross_queries, cross_pairs, frame_mask)
    after_cross = after_self + dot_right(cross_mixed, cross_out_all) + biases[:, 5]
    normed_three, scale_three = layer_parts(after_cross)
    act_three = (normed_three * gains[:, 2] + shifts[:, 2]).astype(jnp.bfloat16)
    up_value = dot_right(act_three, up_all) + up_bias_all
    gelu_value, gelu_pull = jax.vjp(partial(jax.nn.gelu, approximate=False), up_value)
    hidden_act = gelu_value.astype(jnp.bfloat16)
    after_mlp = after_cross + dot_right(hidden_act, down_all) + biases[:, 6]
    normed_last, scale_last = layer_parts(after_mlp)
    result = (normed_last * gains[:, 3] + shifts[:, 3]).astype(jnp.bfloat16)
    corpus_match = (
        corpus_ids[:, None] == jnp.arange(corpus_weights.shape[0], dtype=jnp.int32)[None, :]
    )
    seq_weight = jnp.sum(jnp.where(corpus_match, corpus_weights[None, :], 0.0), axis=1)
    live_rows = (positions[None, :] >= offsets) & (
        positions[None, :] < offsets + token_lengths[:, None]
    )
    grad_out = (
        cotangent.astype(jnp.float32) * jnp.where(live_rows, seq_weight[:, None], 0.0)[..., None]
    )
    grad_mlp, gain_last, shift_last = layer_back(grad_out, normed_last, scale_last, gains[:, 3])
    grad_down = grad_mlp.astype(jnp.bfloat16)
    down_sum = reduce_rows(weight_term(hidden_act, grad_down))
    down_bias = col_sum(grad_down)
    grad_act = dot_left(grad_down, down_all)
    grad_up = gelu_pull(grad_act)[0].astype(jnp.bfloat16)
    up_sum = reduce_rows(weight_term(act_three, grad_up))
    up_bias_term = col_sum(grad_up)
    back_three, gain_three, shift_three = layer_back(
        dot_left(grad_up, up_all), normed_three, scale_three, gains[:, 2]
    )
    grad_cross = grad_mlp + back_three
    grad_cross_in = grad_cross.astype(jnp.bfloat16)
    cross_out_term = weight_term(cross_mixed, grad_cross_in)
    cross_out_bias = col_sum(grad_cross_in)
    grad_cross_mixed = dot_left(grad_cross_in, cross_out_all).astype(jnp.bfloat16)
    grad_cross_query, grad_cross_pairs = attend_back(
        cross_queries, cross_pairs, frame_mask, cross_total, grad_cross_mixed
    )
    grad_frames_in = grad_cross_pairs.astype(jnp.bfloat16)
    kv_term = weight_term(frames, grad_frames_in)
    kv_bias_term = col_sum(grad_frames_in[..., model_width:])
    frame_grads = dot_left(grad_frames_in, kv_all)
    frame_came = swap_seq(frame_grads[:, half_slots:].astype(jnp.bfloat16))
    owner_grads = frame_grads[:, :half_slots] + frame_came.astype(jnp.float32)
    grad_encoder = lax.all_to_all(
        owner_grads.astype(jnp.bfloat16), "batch", split_axis=1, concat_axis=0, tiled=True
    ).astype(jnp.float32)
    grad_cq = grad_cross_query.astype(jnp.bfloat16)
    query_term = weight_term(act_two, grad_cq)
    query_bias = col_sum(grad_cq)
    cross_sum = reduce_rows(jnp.concatenate([cross_out_term, kv_term, query_term], axis=1))
    back_two, gain_two, shift_two = layer_back(
        dot_left(grad_cq, query_all), normed_two, scale_two, gains[:, 1]
    )
    grad_self = grad_cross + back_two
    grad_self_in = grad_self.astype(jnp.bfloat16)
    self_out_term = weight_term(self_mixed, grad_self_in)
    self_out_bias = col_sum(grad_self_in)
    grad_self_mixed = dot_left(grad_self_in, self_out_all).astype(jnp.bfloat16)
    grad_self_query, grad_self_pairs = attend_back(
        self_query, self_pairs, self_mask, self_total, grad_self_mixed
    )
    grad_pairs_in = grad_self_pairs.astype(jnp.bfloat16)
    grad_qkv = jnp.concatenate(
        [grad_self_query.astype(jnp.bfloat16), grad_pairs_in[:, row_count:]], axis=-1
    )
    grad_far = grad_pairs_in[:, :row_count]
    far_term = weight_term(act_far, grad_far)
    qkv_term = weight_term(act_one, grad_qkv)
    qkv_term = jnp.concatenate(
        [qkv_term[:, :model_width], qkv_term[:, model_width:] + far_term], axis=1
    )
    qkv_sums = col_sum(grad_qkv)
    value_sums = qkv_sums[2 * model_width :] + col_sum(grad_far[..., model_width:])
    norm_far = swap_seq(
        dot_left(grad_far, self_in_all[:, model_width:]).astype(jnp.bfloat16)
    ).astype(jnp.float32)
    back_one, gain_one, shift_one = layer_back(
        dot_left(grad_qkv, self_in_all) + norm_far, normed_one, scale_one, gains[:, 0]
    )
    grad_hidden = grad_self + back_one
    small_term = jnp.stack(
        [
            gain_one,
            gain_two,
            gain_three,
            gain_last,
            shift_one,
            shift_two,
            shift_three,
            shift_last,
            qkv_sums[:model_width],
            value_sums,
            self_out_bias,
            query_bias,
            kv_bias_term,
            cross_out_bias,
            down_bias,
        ],
        axis=1,
    )
    small_term = jnp.concatenate([small_term, up_bias_term.reshape(model_width, blocks)], axis=1)
    small_term = jnp.pad(small_term, ((0, 0), (0, tail_width - small_cols)))
    self_sum = reduce_rows(jnp.concatenate([self_out_term, qkv_term, small_term], axis=1))
    small_sum = self_sum[:, 4 * model_width :]
    return (
        result,
        grad_hidden,
        grad_encoder,
        small_sum[:, :4],
        small_sum[:, 4:8],
        self_sum[:, model_width : 4 * model_width],
        self_sum[:, :model_width],
        cross_sum[:, 3 * model_width :],
        cross_sum[:, model_width : 3 * model_width],
        cross_sum[:, :model_width],
        small_sum[:, 8:15],
        up_sum,
        small_sum[:, 15:small_cols].reshape(-1),
        down_sum,
    )


def solution(mesh):
    in_specs = (
        P("batch", "seq", None),
        P(None, ("batch", "seq"), None),
        P("batch", "seq", None),
        P("batch"),
        P("batch"),
        P("batch"),
        P("batch"),
        P(),
        P("batch", None),
        P("batch", None),
        P("batch", None),
        P("batch", None),
        P("batch", None),
        P("batch", None),
        P("batch", None),
        P("batch", None),
        P("batch", None),
        P("batch"),
        P("batch", None),
    )
    out_specs = (
        P("batch", "seq", None),
        P("batch", "seq", None),
        P(None, ("batch", "seq"), None),
        P("batch", None),
        P("batch", None),
        P("batch", None),
        P("batch", None),
        P("batch", None),
        P("batch", None),
        P("batch", None),
        P("batch", None),
        P("batch", None),
        P("batch"),
        P("batch", None),
    )
    return jax.shard_map(body, mesh=mesh, in_specs=in_specs, out_specs=out_specs, check_vma=False)
```

```python
from functools import partial

import jax
import jax.numpy as jnp
from jax import lax
from jax.experimental import pallas as pl
from jax.experimental.pallas import tpu as pltpu
from jax.sharding import PartitionSpec as P

HEAD_DIM = 64
LANES = 128


EPS = 1e-05

def layer_parts(values):
    center = values - jnp.mean(values, axis=-1, keepdims=True)
    inv_std = lax.rsqrt(jnp.mean(center * center, axis=-1, keepdims=True) + EPS)
    return (center * inv_std, inv_std)


def layer_back(grad_side, normed, inv_std, gain):
    scaled = grad_side * gain
    mean_one = jnp.mean(scaled, axis=-1, keepdims=True)
    mean_two = jnp.mean(scaled * normed, axis=-1, keepdims=True)
    grad_in = inv_std * (scaled - mean_one - normed * mean_two)
    return (grad_in, jnp.sum(grad_side * normed, axis=0), jnp.sum(grad_side, axis=0))


def dot_right(left_side, weight):
    return jnp.dot(left_side, weight, preferred_element_type=jnp.float32)


def dot_left(grad_side, weight):
    return jnp.einsum("cj,ij->ci", grad_side, weight, preferred_element_type=jnp.float32)


def weight_term(left_side, grad_side):
    return jnp.einsum(
        "ci,cj->ij", left_side, grad_side, preferred_element_type=jnp.float32
    ).astype(jnp.bfloat16)


def col_sum(grad_side):
    return jnp.sum(grad_side, axis=0, dtype=jnp.float32)


def hold(steps, values):
    return lax.optimization_barrier((steps, values))

ROWS_BY_LANES = (((1,), (1,)), ((), ()))
DOWN_BOTH = (((0,), (0,)), ((), ()))


def head_parts(block):
    lane = lax.broadcasted_iota(jnp.int32, block.shape, 1)
    zero = jnp.zeros_like(block)
    return (
        jnp.where(lane < HEAD_DIM, block, zero),
        jnp.where(lane < HEAD_DIM, zero, block),
    )


def dot_of(left, right, dims):
    return lax.dot_general(left, right, dims, preferred_element_type=jnp.float32)


def attend_kernel(query_ref, key_ref, value_ref, bias_ref, mixed_ref, total_ref):
    score_scale = HEAD_DIM ** (-0.5)
    key, value = key_ref[...], value_ref[...]
    queries = head_parts(query_ref[...] * jnp.bfloat16(score_scale))
    scores = [dot_of(key, query, ROWS_BY_LANES) + bias_ref[...] for query in queries]
    tops = [jnp.max(item, axis=0, keepdims=True) for item in scores]
    terms = [jnp.exp(item - top) for item, top in zip(scores, tops)]
    totals = [jnp.sum(item, axis=0, keepdims=True) for item in terms]
    sides = [dot_of(value, item.astype(jnp.bfloat16), DOWN_BOTH) for item in terms]
    for head in range(2):
        total_ref[0, head : head + 1, :] = tops[head] + jnp.log(totals[head])
    mixed = [
        sides[head][head * HEAD_DIM : (head + 1) * HEAD_DIM] / totals[head] for head in range(2)
    ]
    mixed_ref[...] = jnp.concatenate(mixed, axis=0).T.astype(jnp.bfloat16)


def attend_back_kernel(
    query_ref, key_ref, value_ref, bias_ref, total_ref, grad_ref, gq_ref, gk_ref, gv_ref
):
    score_scale = HEAD_DIM ** (-0.5)
    key, value = key_ref[...], value_ref[...]
    queries = head_parts(query_ref[...] * jnp.bfloat16(score_scale))
    grads = head_parts(grad_ref[...])
    scores = [dot_of(key, query, ROWS_BY_LANES) + bias_ref[...] for query in queries]
    terms = [
        jnp.exp(item - total_ref[0, head : head + 1, :]) for head, item in enumerate(scores)
    ]
    grad_terms = [
        item * dot_of(value, grad, ROWS_BY_LANES) for item, grad in zip(terms, grads)
    ]
    row_dots = [jnp.sum(item, axis=0, keepdims=True) for item in grad_terms]
    grad_scores = [
        (grad_term - term * row_dot).astype(jnp.bfloat16)
        for grad_term, term, row_dot in zip(grad_terms, terms, row_dots)
    ]
    values = [
        jnp.dot(item.astype(jnp.bfloat16), grad, preferred_element_type=jnp.float32)
        for item, grad in zip(terms, grads)
    ]
    keys = [
        jnp.dot(item, query, preferred_element_type=jnp.float32)
        for item, query in zip(grad_scores, queries)
    ]
    sides = [dot_of(key, item, DOWN_BOTH) for item in grad_scores]
    gk_ref[...] = (keys[0] + keys[1]).astype(jnp.bfloat16)
    gv_ref[...] = (values[0] + values[1]).astype(jnp.bfloat16)
    picked = [
        sides[head][head * HEAD_DIM : (head + 1) * HEAD_DIM] * score_scale for head in range(2)
    ]
    gq_ref[...] = jnp.concatenate(picked, axis=0).T.astype(jnp.bfloat16)


def head_specs(rows, keys, blocks):
    return [
        pl.BlockSpec((rows, LANES), lambda i: (0, i)),
        pl.BlockSpec((keys, LANES), lambda i: (0, i)),
        pl.BlockSpec((keys, LANES), lambda i: (0, i + blocks)),
        pl.BlockSpec((keys, rows), lambda i: (0, 0)),
    ]


def attend(queries, pairs, bias):
    rows, width = queries.shape
    keys = pairs.shape[0]
    blocks = width // LANES
    work = 4 * rows * keys * width
    return pl.pallas_call(
        attend_kernel,
        grid=(blocks,),
        out_shape=(
            jax.ShapeDtypeStruct((rows, width), jnp.bfloat16),
            jax.ShapeDtypeStruct((blocks, 2, rows), jnp.float32),
        ),
        in_specs=head_specs(rows, keys, blocks),
        out_specs=(
            pl.BlockSpec((rows, LANES), lambda i: (0, i)),
            pl.BlockSpec((1, 2, rows), lambda i: (i, 0, 0)),
        ),
        cost_estimate=pl.CostEstimate(
            flops=4 * work, transcendentals=0, bytes_accessed=4 * keys * width
        ),
        name="attend",
    )(queries, pairs, pairs, bias)


def attend_back(queries, pairs, bias, totals, grads):
    rows, width = queries.shape
    keys = pairs.shape[0]
    blocks = width // LANES
    work = 10 * rows * keys * width
    return pl.pallas_call(
        attend_back_kernel,
        grid=(blocks,),
        out_shape=(
            jax.ShapeDtypeStruct((rows, width), jnp.bfloat16),
            jax.ShapeDtypeStruct((keys, width), jnp.bfloat16),
            jax.ShapeDtypeStruct((keys, width), jnp.bfloat16),
        ),
        in_specs=head_specs(rows, keys, blocks)
        + [
            pl.BlockSpec((1, 2, rows), lambda i: (i, 0, 0)),
            pl.BlockSpec((rows, LANES), lambda i: (0, i)),
        ],
        out_specs=(
            pl.BlockSpec((rows, LANES), lambda i: (0, i)),
            pl.BlockSpec((keys, LANES), lambda i: (0, i)),
            pl.BlockSpec((keys, LANES), lambda i: (0, i)),
        ),
        cost_estimate=pl.CostEstimate(
            flops=4 * work, transcendentals=0, bytes_accessed=8 * keys * width
        ),
        name="attend_back",
    )(queries, pairs, pairs, bias, totals, grads)


CORES = 2
PAIR = 2
FLIP = [(0, 1), (1, 0)]


def partners(stride, radix, step):
    pairs = []
    for i in range(lax.axis_size("batch")):
        digit = i // stride % radix
        pairs.append((i, i + ((digit ^ step) - digit) * stride))
    return pairs


def swap(block, stride, radix=2, step=1):
    return lax.ppermute(block, "batch", partners(stride, radix, step))


def swap_seq(block):
    return lax.ppermute(block, "seq", FLIP)


def place_of():
    batch = lax.axis_index("batch")
    return (
        batch // (CORES * PAIR),
        batch // CORES % PAIR,
        batch % CORES,
        lax.axis_index("seq"),
    )


def splits(rows):
    depth = lax.axis_size("batch") // (CORES * PAIR)
    return rows % 48 == 0 and depth == 4 and lax.axis_size("seq") == 2


def place_kernel(where_ref, *refs, depth, rows, half):
    pieces, out_ref, sem = refs[:8], refs[8], refs[9]
    deep, wide, core, seq = where_ref[0], where_ref[1], where_ref[2], where_ref[3]
    started = []
    for c in range(2):
        column, across, side, side_across = pieces[4 * c : 4 * c + 4]
        for w, (near, far) in enumerate(((column, side), (across, side_across))):
            for k in range(depth):
                base = (((deep ^ k) * PAIR + (wide ^ w)) * CORES + (core ^ c)) * rows
                row_span = pl.ds(pl.multiple_of(base, 16), rows)
                for source, part in ((near, seq), (far, 1 - seq)):
                    col_span = pl.ds(pl.multiple_of(part * half, LANES), half)
                    copy = pltpu.make_async_copy(
                        source.at[k], out_ref.at[row_span, col_span], sem
                    )
                    copy.start()
                    started.append(copy)
    for copy in started:
        copy.wait()


class Gather:
    def __init__(self, shard, last):
        self.rows, self.cols = shard.shape
        self.half = self.cols // 2
        self.last = last
        self.depth = lax.axis_size("batch") // (CORES * PAIR)
        self.state = (shard,)
        self.todo = (
            [self.by_depth, self.by_both, self.by_last, self.place]
            if splits(self.rows)
            else [self.plain]
        )

    def step(self):
        if self.todo:
            self.state = self.todo.pop(0)(*self.state)
        return self

    def result(self):
        while self.todo:
            self.step()
        return self.state[0]

    def plain(self, shard):
        return (lax.all_gather(shard, "batch", axis=0, tiled=True),)

    def by_depth(self, shard):
        part = lax.dynamic_slice_in_dim(shard, lax.axis_index("seq") * self.half, self.half, 1)
        came = [swap(part, CORES * PAIR, self.depth, k) for k in range(1, self.depth)]
        return (jnp.stack([part] + came),)

    def by_both(self, column):
        return column, swap(column, CORES), swap_seq(column)

    def by_last(self, column, across, side):
        far = swap_seq(across) if self.last == "seq" else swap(side, CORES)
        return column, across, side, far

    def place(self, *mine):
        other = tuple(swap(piece, 1) for piece in mine)
        total = lax.axis_size("batch") * self.rows
        call = pl.pallas_call(
            partial(place_kernel, depth=self.depth, rows=self.rows, half=self.half),
            out_shape=jax.ShapeDtypeStruct((total, self.cols), mine[0].dtype),
            in_specs=[pl.BlockSpec(memory_space=pltpu.SMEM)]
            + [pl.BlockSpec(memory_space=pl.ANY)] * 8,
            out_specs=pl.BlockSpec(memory_space=pltpu.VMEM),
            scratch_shapes=[pltpu.SemaphoreType.DMA],
            cost_estimate=pl.CostEstimate(
                flops=0, transcendentals=0, bytes_accessed=4 * total * self.cols
            ),
            name="place_rows",
        )
        return (call(jnp.stack(place_of()).astype(jnp.int32), *mine, *other),)


def narrow(values):
    return lax.reduce_precision(values, 8, 7).astype(jnp.bfloat16)


class Reduction:
    def __init__(self, *terms):
        self.size = lax.axis_size("batch")
        self.rows = terms[0].shape[0] // self.size
        self.state = terms
        self.fast = splits(self.rows)
        self.todo = (
            [self.by_core, self.by_seq, self.by_pair, self.by_depth, self.finish, self.join]
            if self.fast
            else [self.plain]
        )

    def step(self):
        if self.todo:
            self.state = self.todo.pop(0)(*self.state)
        return self

    def result(self):
        while self.todo:
            self.step()
        return self.state[0]

    def plain(self, *terms):
        terms = jnp.concatenate(terms, axis=1)
        mine = lax.psum_scatter(terms, "batch", scatter_dimension=0, tiled=True)
        return (lax.psum(mine, "seq").astype(jnp.float32),)

    def by_core(self, *terms):
        _, _, core, _ = place_of()
        grids = [term.reshape(-1, PAIR, CORES, self.rows, term.shape[1]) for term in terms]
        return tuple(
            jnp.concatenate(
                [lax.dynamic_index_in_dim(grid, which, 2, keepdims=False) for grid in grids], axis=-1
            )
            for which in (core, 1 - core)
        )

    def by_seq(self, kept, sent):
        seq, third = lax.axis_index("seq"), self.rows // 3
        chip = kept.astype(jnp.float32) + swap(sent, 1).astype(jnp.float32)
        edge = lax.dynamic_slice_in_dim(chip, (1 - seq) * 2 * third, third, 2)
        kept = lax.dynamic_slice_in_dim(chip, seq * third, 2 * third, 2)
        return kept.astype(jnp.bfloat16), edge.astype(jnp.bfloat16)

    def by_pair(self, kept, sent):
        _, wide, _, seq = place_of()
        came = swap_seq(sent)
        blank = jnp.zeros_like(came)
        came = jnp.where(
            seq == 0,
            jnp.concatenate([came, blank], axis=2),
            jnp.concatenate([blank, came], axis=2),
        )
        kept = kept.astype(jnp.float32) + came.astype(jnp.float32)
        mine = lax.dynamic_index_in_dim(kept, wide, 1, keepdims=False)
        sent = lax.dynamic_index_in_dim(kept, 1 - wide, 1, keepdims=False)
        return mine.astype(jnp.bfloat16), sent.astype(jnp.bfloat16)

    def by_depth(self, kept, sent):
        deep, _, _, _ = place_of()
        kept = kept.astype(jnp.float32) + swap(sent, CORES).astype(jnp.float32)
        return tuple(
            lax.dynamic_index_in_dim(kept, deep ^ k, 0, keepdims=False).astype(jnp.bfloat16)
            for k in range(self.size // (CORES * PAIR))
        )

    def finish(self, kept, *sent):
        depth = self.size // (CORES * PAIR)
        total = kept.astype(jnp.float32)
        for k, block in enumerate(sent, 1):
            total = total + swap(block, CORES * PAIR, depth, k).astype(jnp.float32)
        return (narrow(total),)

    def join(self, mine):
        seq, third = lax.axis_index("seq"), self.rows // 3
        came = swap_seq(mine)
        low = jnp.where(seq == 0, mine, came).astype(jnp.float32)
        high = jnp.where(seq == 0, came, mine).astype(jnp.float32)
        return (
            jnp.concatenate([low[:third], low[third:] + high[:third], high[third:]], axis=0),
        )


def advance(works, values):
    for work in works:
        work.step()
    states, values = lax.optimization_barrier(([work.state for work in works], values))
    for work, state in zip(works, states):
        work.state = state
    return values


def body(
    hidden,
    encoder,
    cotangent,
    token_offsets,
    token_lengths,
    frame_counts,
    corpus_ids,
    corpus_weights,
    norm_gains,
    norm_shifts,
    self_in,
    self_out,
    cross_query,
    cross_kv,
    cross_out,
    proj_bias,
    up_weight,
    up_bias,
    down_weight,
):
    hidden, cotangent = hidden[0], cotangent[0]
    row_count, model_width = hidden.shape
    shard_rows = norm_gains.shape[0]
    wide_cols = up_weight.shape[1]
    blocks = wide_cols // model_width
    size = lax.axis_size("batch")

    tail_width = 2 * LANES
    small = jnp.concatenate(
        [norm_gains, norm_shifts, proj_bias, up_bias.reshape(shard_rows, blocks)], axis=1
    )
    small_cols = small.shape[1]
    small = jnp.pad(small, ((0, 0), (0, tail_width - small_cols)))
    first = Gather(jnp.concatenate([self_in, small], axis=1), "seq")
    second = Gather(jnp.concatenate([self_out, cross_query, cross_kv, cross_out], axis=1), "pair")
    up_blocks = up_weight.reshape(shard_rows, blocks, model_width).transpose(1, 0, 2)
    third = jnp.concatenate([up_blocks.reshape(-1, model_width), down_weight], axis=1)
    hidden_other = swap_seq(hidden)
    first.step()
    second.state, encoder, first.state = lax.optimization_barrier(
        (second.state, encoder, first.state)
    )
    second.step()
    first.step()
    frame_mine = lax.all_to_all(encoder, "batch", split_axis=0, concat_axis=0, tiled=True)
    frame_mine = frame_mine.reshape(-1, model_width)
    third, second.state = lax.optimization_barrier((third, second.state))
    third_all = lax.all_gather(third, "batch", axis=0, tiled=True)
    first.step()
    second.step()
    frame_other = swap_seq(frame_mine)
    first_all, second_all = first.result(), second.result()

    self_in_all = first_all[:, : 3 * model_width]
    small_all = first_all[:, 3 * model_width : 3 * model_width + small_cols]
    self_out_all = second_all[:, :model_width]
    query_all = second_all[:, model_width : 2 * model_width]
    kv_all = second_all[:, 2 * model_width : 4 * model_width]
    cross_out_all = second_all[:, 4 * model_width :]
    down_all = third_all[:, model_width:]
    up_all = (
        third_all[:, :model_width]
        .reshape(size, blocks, shard_rows, model_width)
        .transpose(0, 2, 1, 3)
        .reshape(model_width, wide_cols)
    )
    gains = small_all[:, :4].astype(jnp.float32)
    shifts = small_all[:, 4:8].astype(jnp.float32)
    biases = small_all[:, 8:15].astype(jnp.float32)
    up_bias_all = small_all[:, 15:].reshape(-1).astype(jnp.float32)

    offset, length, frame_count = token_offsets[0], token_lengths[0], frame_counts[0]
    seq_index = lax.axis_index("seq")
    slots = jnp.arange(row_count, dtype=jnp.int32)
    positions = seq_index * row_count + slots
    positions_other = (1 - seq_index) * row_count + slots
    zero_row = jnp.zeros((model_width,), jnp.float32)
    inputs = hidden.astype(jnp.float32)
    normed_one, scale_one = layer_parts(inputs)
    act_one = (normed_one * gains[:, 0] + shifts[:, 0]).astype(jnp.bfloat16)
    normed_far, _ = layer_parts(hidden_other.astype(jnp.float32))
    act_far = (normed_far * gains[:, 0] + shifts[:, 0]).astype(jnp.bfloat16)
    qkv_bias = jnp.concatenate([biases[:, 0], zero_row, biases[:, 1]])
    qkv_local = (dot_right(act_one, self_in_all) + qkv_bias).astype(jnp.bfloat16)
    self_query = qkv_local[:, :model_width]
    pair_far = (
        dot_right(act_far, self_in_all[:, model_width:]) + qkv_bias[model_width:]
    ).astype(jnp.bfloat16)
    self_pairs = jnp.concatenate([pair_far, qkv_local[:, model_width:]], axis=0)
    key_pos = jnp.concatenate([positions_other, positions])[:, None]
    query_pos = positions[None, :]
    self_mask = (key_pos <= query_pos) & ((key_pos >= offset) | (key_pos == query_pos))
    self_bias = jnp.where(self_mask, 0.0, -jnp.inf)
    self_mixed, self_total = attend(self_query, self_pairs, self_bias)
    after_self = inputs + dot_right(self_mixed, self_out_all) + biases[:, 2]
    normed_two, scale_two = layer_parts(after_self)
    act_two = (normed_two * gains[:, 1] + shifts[:, 1]).astype(jnp.bfloat16)
    cross_queries = (dot_right(act_two, query_all) + biases[:, 3]).astype(jnp.bfloat16)
    frames = jnp.concatenate([frame_mine, frame_other], axis=0)
    kv_bias = jnp.concatenate([zero_row, biases[:, 4]])
    cross_pairs = (dot_right(frames, kv_all) + kv_bias).astype(jnp.bfloat16)
    half_slots = frame_mine.shape[0]
    owner_frames = encoder.shape[1]
    gathered = jnp.arange(2 * half_slots, dtype=jnp.int32)
    half_index = (gathered // half_slots) ^ seq_index
    within = gathered % half_slots
    frame_ids = (within // owner_frames * 2 + half_index) * owner_frames + within % owner_frames
    frame_bias = jnp.broadcast_to(
        jnp.where(frame_ids < frame_count, 0.0, -jnp.inf)[:, None], (2 * half_slots, row_count)
    )
    cross_mixed, cross_total = attend(cross_queries, cross_pairs, frame_bias)
    after_cross = after_self + dot_right(cross_mixed, cross_out_all) + biases[:, 5]
    normed_three, scale_three = layer_parts(after_cross)
    act_three = (normed_three * gains[:, 2] + shifts[:, 2]).astype(jnp.bfloat16)
    up_value = dot_right(act_three, up_all) + up_bias_all
    gelu_value, gelu_pull = jax.vjp(partial(jax.nn.gelu, approximate=False), up_value)
    hidden_act = gelu_value.astype(jnp.bfloat16)
    after_mlp = after_cross + dot_right(hidden_act, down_all) + biases[:, 6]
    normed_last, scale_last = layer_parts(after_mlp)
    result = (normed_last * gains[:, 3] + shifts[:, 3]).astype(jnp.bfloat16)
    corpus_match = corpus_ids[0] == jnp.arange(corpus_weights.shape[0], dtype=jnp.int32)
    seq_weight = jnp.sum(jnp.where(corpus_match, corpus_weights, 0.0))
    live_rows = (positions >= offset) & (positions < offset + length)
    grad_out = cotangent.astype(jnp.float32) * jnp.where(live_rows, seq_weight, 0.0)[:, None]
    grad_mlp, gain_last, shift_last = layer_back(grad_out, normed_last, scale_last, gains[:, 3])
    grad_down = grad_mlp.astype(jnp.bfloat16)
    down_bias = col_sum(grad_down)
    grad_act = dot_left(grad_down, down_all)
    grad_up = gelu_pull(grad_act)[0].astype(jnp.bfloat16)
    up_bias_term = col_sum(grad_up)
    wide_term = jnp.concatenate(
        [weight_term(hidden_act, grad_down).reshape(size, -1, model_width)]
        + [
            weight_term(act_three, part).reshape(size, shard_rows, model_width)
            for part in jnp.split(grad_up, blocks, axis=1)
        ],
        axis=1,
    )
    wide_term, grad_up = lax.optimization_barrier((wide_term, grad_up))
    wide_sum = lax.psum_scatter(wide_term, "batch", scatter_dimension=0, tiled=True)[0]
    back_three, gain_three, shift_three = layer_back(
        dot_left(grad_up, up_all), normed_three, scale_three, gains[:, 2]
    )
    grad_cross = grad_mlp + back_three
    grad_cross_in = grad_cross.astype(jnp.bfloat16)
    cross_out_term = weight_term(cross_mixed, grad_cross_in)
    cross_out_bias = col_sum(grad_cross_in)
    grad_cross_mixed = dot_left(grad_cross_in, cross_out_all).astype(jnp.bfloat16)
    grad_cq, grad_frame_key, grad_frame_value = attend_back(
        cross_queries, cross_pairs, frame_bias, cross_total, grad_cross_mixed
    )
    kv_bias_term = col_sum(grad_cross_mixed)
    frame_grads = dot_left(grad_frame_key, kv_all[:, :model_width]) + dot_left(
        grad_frame_value, kv_all[:, model_width:]
    )
    frame_mine_grads = frame_grads[:half_slots]
    frame_sent = frame_grads[half_slots:].astype(jnp.bfloat16)
    grad_cq, (frame_sent, frame_mine_grads) = hold(grad_cq, (frame_sent, frame_mine_grads))
    query_term = weight_term(act_two, grad_cq)
    query_bias = col_sum(grad_cq)
    back_two, gain_two, shift_two = layer_back(
        dot_left(grad_cq, query_all), normed_two, scale_two, gains[:, 1]
    )
    grad_self = grad_cross + back_two
    grad_self_in = grad_self.astype(jnp.bfloat16)
    self_out_term = weight_term(self_mixed, grad_self_in)
    self_out_bias = col_sum(grad_self_in)
    grad_self_mixed = dot_left(grad_self_in, self_out_all).astype(jnp.bfloat16)
    cross_sum = Reduction(
        cross_out_term,
        weight_term(frames, grad_frame_key),
        weight_term(frames, grad_frame_value),
        query_term,
    )
    grad_self_mixed = advance([cross_sum], grad_self_mixed)
    grad_self_query, grad_self_key, grad_self_value = attend_back(
        self_query, self_pairs, self_bias, self_total, grad_self_mixed
    )
    owner_grads = (frame_mine_grads + swap_seq(frame_sent).astype(jnp.float32)).astype(
        jnp.bfloat16
    )
    grad_self_query, grad_self_key, grad_self_value, owner_grads = advance(
        [cross_sum],
        (grad_self_query, grad_self_key, grad_self_value, owner_grads),
    )
    grad_encoder = lax.all_to_all(
        owner_grads.reshape(size, owner_frames, model_width),
        "batch",
        split_axis=0,
        concat_axis=0,
        tiled=True,
    ).astype(jnp.float32)
    grad_pairs = jnp.concatenate([grad_self_key, grad_self_value], axis=1)
    grad_qkv = jnp.concatenate([grad_self_query, grad_pairs[row_count:]], axis=1)
    grad_far = grad_pairs[:row_count]
    both_acts = jnp.concatenate([act_far, act_one], axis=0)
    small_now = [
        weight_term(act_one, grad_self_query),
        weight_term(both_acts, grad_self_key),
        weight_term(both_acts, grad_self_value),
    ]
    query_sums = col_sum(grad_self_query)
    value_sums = col_sum(grad_self_mixed)
    norm_far = dot_left(grad_far, self_in_all[:, model_width:]).astype(jnp.bfloat16)
    back_side = dot_left(grad_qkv, self_in_all) + swap_seq(norm_far).astype(jnp.float32)
    back_one, gain_one, shift_one = layer_back(back_side, normed_one, scale_one, gains[:, 0])
    grad_hidden = grad_self + back_one
    small_term = jnp.stack(
        [
            gain_one,
            gain_two,
            gain_three,
            gain_last,
            shift_one,
            shift_two,
            shift_three,
            shift_last,
            query_sums,
            value_sums,
            self_out_bias,
            query_bias,
            kv_bias_term,
            cross_out_bias,
            down_bias,
        ],
        axis=1,
    )
    small_term = jnp.concatenate([small_term, up_bias_term.reshape(model_width, blocks)], axis=1)
    small_term = jnp.pad(small_term, ((0, 0), (0, tail_width - small_cols))).astype(jnp.bfloat16)
    self_sum = Reduction(self_out_term, *small_now, small_term)
    wide_sum = wide_sum.astype(jnp.float32) + swap_seq(wide_sum).astype(jnp.float32)
    inner_rows = down_weight.shape[0]
    up_sum = (
        wide_sum[inner_rows:]
        .reshape(blocks, shard_rows, model_width)
        .transpose(1, 0, 2)
        .reshape(shard_rows, wide_cols)
    )
    cross_sum, self_sum = cross_sum.result(), self_sum.result()
    small_sum = self_sum[:, 4 * model_width :]
    return (
        result[None],
        grad_hidden[None],
        grad_encoder,
        small_sum[:, :4],
        small_sum[:, 4:8],
        self_sum[:, model_width : 4 * model_width],
        self_sum[:, :model_width],
        cross_sum[:, 3 * model_width :],
        cross_sum[:, model_width : 3 * model_width],
        cross_sum[:, :model_width],
        small_sum[:, 8:15],
        up_sum,
        small_sum[:, 15:small_cols].reshape(-1),
        wide_sum[:inner_rows],
    )


def solution(mesh):
    in_specs = (
        P("batch", "seq", None),
        P(None, ("batch", "seq"), None),
        P("batch", "seq", None),
        P("batch"),
        P("batch"),
        P("batch"),
        P("batch"),
        P(),
        P("batch", None),
        P("batch", None),
        P("batch", None),
        P("batch", None),
        P("batch", None),
        P("batch", None),
        P("batch", None),
        P("batch", None),
        P("batch", None),
        P("batch"),
        P("batch", None),
    )
    out_specs = (
        P("batch", "seq", None),
        P("batch", "seq", None),
        P(None, ("batch", "seq"), None),
        P("batch", None),
        P("batch", None),
        P("batch", None),
        P("batch", None),
        P("batch", None),
        P("batch", None),
        P("batch", None),
        P("batch", None),
        P("batch", None),
        P("batch"),
        P("batch", None),
    )
    return jax.shard_map(body, mesh=mesh, in_specs=in_specs, out_specs=out_specs, check_vma=False)
```

```python
from functools import partial

import jax
import jax.numpy as jnp
from jax import lax
from jax.experimental import pallas as pl
from jax.experimental.pallas import tpu as pltpu
from jax.sharding import PartitionSpec as P

HEAD_DIM = 64
LANES = 128


EPS = 1e-05

def layer_parts(values):
    center = values - jnp.mean(values, axis=-1, keepdims=True)
    inv_std = lax.rsqrt(jnp.mean(center * center, axis=-1, keepdims=True) + EPS)
    return (center * inv_std, inv_std)


def layer_back(grad_side, normed, inv_std, gain):
    scaled = grad_side * gain
    mean_one = jnp.mean(scaled, axis=-1, keepdims=True)
    mean_two = jnp.mean(scaled * normed, axis=-1, keepdims=True)
    grad_in = inv_std * (scaled - mean_one - normed * mean_two)
    return (grad_in, jnp.sum(grad_side * normed, axis=0), jnp.sum(grad_side, axis=0))


def dot_right(left_side, weight):
    return jnp.dot(left_side, weight, preferred_element_type=jnp.float32)


def dot_left(grad_side, weight):
    return jnp.einsum("cj,ij->ci", grad_side, weight, preferred_element_type=jnp.float32)


def weight_term(left_side, grad_side):
    return jnp.einsum(
        "ci,cj->ij", left_side, grad_side, preferred_element_type=jnp.float32
    ).astype(jnp.bfloat16)


def col_sum(grad_side):
    return jnp.sum(grad_side, axis=0, dtype=jnp.float32)


def hold(steps, values):
    return lax.optimization_barrier((steps, values))

ROWS_BY_LANES = (((1,), (1,)), ((), ()))
DOWN_BOTH = (((0,), (0,)), ((), ()))


def head_parts(block):
    lane = lax.broadcasted_iota(jnp.int32, block.shape, 1)
    zero = jnp.zeros_like(block)
    return (
        jnp.where(lane < HEAD_DIM, block, zero),
        jnp.where(lane < HEAD_DIM, zero, block),
    )


def dot_of(left, right, dims):
    return lax.dot_general(left, right, dims, preferred_element_type=jnp.float32)


def attend_kernel(query_ref, key_ref, value_ref, bias_ref, mixed_ref, total_ref):
    score_scale = HEAD_DIM ** (-0.5)
    key, value = key_ref[...], value_ref[...]
    queries = head_parts(query_ref[...] * jnp.bfloat16(score_scale))
    scores = [dot_of(key, query, ROWS_BY_LANES) + bias_ref[...] for query in queries]
    tops = [jnp.max(item, axis=0, keepdims=True) for item in scores]
    terms = [jnp.exp(item - top) for item, top in zip(scores, tops)]
    totals = [jnp.sum(item, axis=0, keepdims=True) for item in terms]
    sides = [dot_of(value, item.astype(jnp.bfloat16), DOWN_BOTH) for item in terms]
    for head in range(2):
        total_ref[0, head : head + 1, :] = tops[head] + jnp.log(totals[head])
    mixed = [
        sides[head][head * HEAD_DIM : (head + 1) * HEAD_DIM] / totals[head] for head in range(2)
    ]
    mixed_ref[...] = jnp.concatenate(mixed, axis=0).T.astype(jnp.bfloat16)


def attend_back_kernel(
    query_ref, key_ref, value_ref, bias_ref, total_ref, grad_ref, gq_ref, pair_ref
):
    score_scale = HEAD_DIM ** (-0.5)
    key, value = key_ref[...], value_ref[...]
    queries = head_parts(query_ref[...] * jnp.bfloat16(score_scale))
    grads = head_parts(grad_ref[...])
    scores = [dot_of(key, query, ROWS_BY_LANES) + bias_ref[...] for query in queries]
    terms = [
        jnp.exp(item - total_ref[0, head : head + 1, :]) for head, item in enumerate(scores)
    ]
    grad_terms = [
        item * dot_of(value, grad, ROWS_BY_LANES) for item, grad in zip(terms, grads)
    ]
    row_dots = [jnp.sum(item, axis=0, keepdims=True) for item in grad_terms]
    grad_scores = [
        (grad_term - term * row_dot).astype(jnp.bfloat16)
        for grad_term, term, row_dot in zip(grad_terms, terms, row_dots)
    ]
    values = [
        jnp.dot(item.astype(jnp.bfloat16), grad, preferred_element_type=jnp.float32)
        for item, grad in zip(terms, grads)
    ]
    keys = [
        jnp.dot(item, query, preferred_element_type=jnp.float32)
        for item, query in zip(grad_scores, queries)
    ]
    sides = [dot_of(key, item, DOWN_BOTH) for item in grad_scores]
    pair_ref[0] = (keys[0] + keys[1]).astype(jnp.bfloat16)
    pair_ref[1] = (values[0] + values[1]).astype(jnp.bfloat16)
    picked = [
        sides[head][head * HEAD_DIM : (head + 1) * HEAD_DIM] * score_scale for head in range(2)
    ]
    gq_ref[...] = jnp.concatenate(picked, axis=0).T.astype(jnp.bfloat16)


def head_specs(rows, keys, blocks):
    return [
        pl.BlockSpec((rows, LANES), lambda i: (0, i)),
        pl.BlockSpec((keys, LANES), lambda i: (0, i)),
        pl.BlockSpec((keys, LANES), lambda i: (0, i + blocks)),
        pl.BlockSpec((keys, rows), lambda i: (0, 0)),
    ]


def attend(queries, pairs, bias):
    rows, width = queries.shape
    keys = pairs.shape[0]
    blocks = width // LANES
    return pl.pallas_call(
        attend_kernel,
        grid=(blocks,),
        out_shape=(
            jax.ShapeDtypeStruct((rows, width), jnp.bfloat16),
            jax.ShapeDtypeStruct((blocks, 2, rows), jnp.float32),
        ),
        in_specs=head_specs(rows, keys, blocks),
        out_specs=(
            pl.BlockSpec((rows, LANES), lambda i: (0, i)),
            pl.BlockSpec((1, 2, rows), lambda i: (i, 0, 0)),
        ),
        cost_estimate=pl.CostEstimate(flops=0, transcendentals=0, bytes_accessed=0),
        name="attend",
    )(queries, pairs, pairs, bias)


def attend_back(queries, pairs, bias, totals, grads):
    rows, width = queries.shape
    keys = pairs.shape[0]
    blocks = width // LANES
    return pl.pallas_call(
        attend_back_kernel,
        grid=(blocks,),
        out_shape=(
            jax.ShapeDtypeStruct((rows, width), jnp.bfloat16),
            jax.ShapeDtypeStruct((2, keys, width), jnp.bfloat16),
        ),
        in_specs=head_specs(rows, keys, blocks)
        + [
            pl.BlockSpec((1, 2, rows), lambda i: (i, 0, 0)),
            pl.BlockSpec((rows, LANES), lambda i: (0, i)),
        ],
        out_specs=(
            pl.BlockSpec((rows, LANES), lambda i: (0, i)),
            pl.BlockSpec((2, keys, LANES), lambda i: (0, 0, i)),
        ),
        cost_estimate=pl.CostEstimate(flops=0, transcendentals=0, bytes_accessed=0),
        name="attend_back",
    )(queries, pairs, pairs, bias, totals, grads)


CORES = 2
PAIR = 2
FLIP = [(0, 1), (1, 0)]


def partners(stride, radix, step):
    pairs = []
    for i in range(lax.axis_size("batch")):
        digit = i // stride % radix
        pairs.append((i, i + ((digit ^ step) - digit) * stride))
    return pairs


def swap(block, stride, radix=2, step=1):
    return lax.ppermute(block, "batch", partners(stride, radix, step))


def swap_seq(block):
    return lax.ppermute(block, "seq", FLIP)


def place_of():
    batch = lax.axis_index("batch")
    return (
        batch // (CORES * PAIR),
        batch // CORES % PAIR,
        batch % CORES,
        lax.axis_index("seq"),
    )


def splits(rows):
    depth = lax.axis_size("batch") // (CORES * PAIR)
    return rows % 48 == 0 and depth == 4 and lax.axis_size("seq") == 2


def place_kernel(where_ref, *refs, depth, rows, half):
    pieces, out_ref, sem = refs[:8], refs[8], refs[9]
    deep, wide, core, seq = where_ref[0], where_ref[1], where_ref[2], where_ref[3]
    started = []
    for c in range(2):
        column, across, side, side_across = pieces[4 * c : 4 * c + 4]
        for w, (near, far) in enumerate(((column, side), (across, side_across))):
            for k in range(depth):
                base = (((deep ^ k) * PAIR + (wide ^ w)) * CORES + (core ^ c)) * rows
                row_span = pl.ds(pl.multiple_of(base, 16), rows)
                for source, part in ((near, seq), (far, 1 - seq)):
                    col_span = pl.ds(pl.multiple_of(part * half, LANES), half)
                    copy = pltpu.make_async_copy(
                        source.at[k], out_ref.at[row_span, col_span], sem
                    )
                    copy.start()
                    started.append(copy)
    for copy in started:
        copy.wait()


class Gather:
    def __init__(self, shard, last):
        self.rows, self.cols = shard.shape
        self.half = self.cols // 2
        self.last = last
        self.depth = lax.axis_size("batch") // (CORES * PAIR)
        self.state = (shard,)
        self.todo = (
            [self.by_depth, self.by_both, self.by_last, self.place]
            if splits(self.rows)
            else [self.plain]
        )

    def step(self):
        if self.todo:
            self.state = self.todo.pop(0)(*self.state)
        return self

    def result(self):
        while self.todo:
            self.step()
        return self.state[0]

    def plain(self, shard):
        return (lax.all_gather(shard, "batch", axis=0, tiled=True),)

    def by_depth(self, shard):
        part = lax.dynamic_slice_in_dim(shard, lax.axis_index("seq") * self.half, self.half, 1)
        came = [swap(part, CORES * PAIR, self.depth, k) for k in range(1, self.depth)]
        return (jnp.stack([part] + came),)

    def by_both(self, column):
        return column, swap(column, CORES), swap_seq(column)

    def by_last(self, column, across, side):
        far = swap_seq(across) if self.last == "seq" else swap(side, CORES)
        return column, across, side, far

    def place(self, *mine):
        other = tuple(swap(piece, 1) for piece in mine)
        total = lax.axis_size("batch") * self.rows
        call = pl.pallas_call(
            partial(place_kernel, depth=self.depth, rows=self.rows, half=self.half),
            out_shape=jax.ShapeDtypeStruct((total, self.cols), mine[0].dtype),
            in_specs=[pl.BlockSpec(memory_space=pltpu.SMEM)]
            + [pl.BlockSpec(memory_space=pl.ANY)] * 8,
            out_specs=pl.BlockSpec(memory_space=pltpu.VMEM),
            scratch_shapes=[pltpu.SemaphoreType.DMA],
            cost_estimate=pl.CostEstimate(flops=0, transcendentals=0, bytes_accessed=0),
            name="place_rows",
        )
        return (call(jnp.stack(place_of()).astype(jnp.int32), *mine, *other),)


def narrow(values):
    return lax.reduce_precision(values, 8, 7).astype(jnp.bfloat16)


def grad_kernel(where_ref, *refs, count, first, rows, blend):
    terms, refs = [refs[4 * i : 4 * i + 4] for i in range(count)], refs[4 * count :]
    extras, (kept_ref, sent_ref, total_ref) = refs[:blend], refs[blend:]
    wide, core, seq = where_ref[1], where_ref[2], where_ref[3]
    height = total_ref.shape[0]
    groups = CORES * kept_ref.shape[0] * rows // height

    def group_step(group, carry):
        start = 0
        for left_ref, far_left_ref, right_ref, far_right_ref in terms:
            width = far_right_ref.shape[1]
            span = pl.ds(pl.multiple_of(group * height, LANES), height)
            if len(right_ref.shape) == 3:
                right = right_ref[core]
            else:
                right = right_ref[:, pl.ds(pl.multiple_of(core * width, LANES), width)]
            total_ref[:, :width] = dot_of(left_ref[:, span], right, DOWN_BOTH) + dot_of(
                far_left_ref[:, span], far_right_ref[...], DOWN_BOTH
            )
            cols = slice(start, start + width)
            for place, near, far in routes(group, height, first, rows, wide, seq):
                for out_ref, base in ((kept_ref, near), (sent_ref, far)):
                    picked = total_ref[pl.ds(pl.multiple_of(base, 16), rows), :width]
                    out_ref[place, :, cols] = picked.astype(jnp.bfloat16)
            start += width
        if blend:
            cols = slice(start, start + LANES)
            for place, near, far in routes(group, height, first, rows, wide, seq):
                for out_ref, base in ((kept_ref, near), (sent_ref, far)):
                    picked = pl.ds(pl.multiple_of(group * height + base, 16), rows)
                    out_ref[place, :, cols] = (
                        extras[0][picked, :].astype(jnp.float32)
                        + extras[1][picked, :].astype(jnp.float32)
                    ).astype(jnp.bfloat16)
        return carry

    lax.fori_loop(0, groups, group_step, 0)


def routes(group, height, first, rows, wide, seq):
    if first == "seq":
        pairs = height // (2 * rows)
        return [
            (group * pairs + i, (2 * i + seq) * rows, (2 * i + 1 - seq) * rows)
            for i in range(pairs)
        ]
    quads = height // (4 * rows)
    return [
        (
            (group * quads + i) * 2 + j,
            (4 * i + 2 * wide + j) * rows,
            (4 * i + 2 * (1 - wide) + j) * rows,
        )
        for i in range(quads)
        for j in range(2)
    ]


def self_tail_kernel(query_ref, pair_ref, weight_ref, near_ref, far_ref, *refs):
    vectors, base_ref, (side_ref, sent_ref, column_ref) = refs[:-4], refs[-4], refs[-3:]
    rows, width = query_ref.shape
    both = dot_of(pair_ref[0], weight_ref[:, width : 2 * width], ROWS_BY_LANES) + dot_of(
        pair_ref[1], weight_ref[:, 2 * width : 3 * width], ROWS_BY_LANES
    )
    far = both[:rows]
    side = both[rows:] + dot_of(query_ref[...], weight_ref[:, :width], ROWS_BY_LANES)
    side_ref[...] = side
    sent_ref[...] = far.astype(jnp.bfloat16)
    sums = [
        jnp.sum(side * near_ref[...] + far * far_ref[...], axis=0, keepdims=True),
        jnp.sum(side + far, axis=0, keepdims=True),
        jnp.sum(query_ref[...].astype(jnp.float32), axis=0, keepdims=True),
    ]
    count = len(sums) + len(vectors)
    lane = lax.broadcasted_iota(jnp.int32, (LANES, LANES), 1)
    blank = jnp.zeros((LANES - count, LANES), jnp.float32)
    for i in range(width // LANES):
        here = slice(i * LANES, (i + 1) * LANES)
        block = jnp.concatenate(
            [item[:, here] for item in sums] + [row[i : i + 1, :] for row in vectors] + [blank],
            axis=0,
        )
        column_ref[here, :] = jnp.where(
            lane < count, block.T, base_ref[here, :].astype(jnp.float32)
        ).astype(jnp.bfloat16)


def self_tail(query, pairs, weight, near, far, vectors, base):
    rows, width = query.shape
    return pl.pallas_call(
        self_tail_kernel,
        out_shape=(
            jax.ShapeDtypeStruct((rows, width), jnp.float32),
            jax.ShapeDtypeStruct((rows, width), jnp.bfloat16),
            jax.ShapeDtypeStruct(base.shape, jnp.bfloat16),
        ),
        cost_estimate=pl.CostEstimate(flops=0, transcendentals=0, bytes_accessed=0),
        name="self_tail",
    )(query, pairs, weight, near, far, *[vector.reshape(-1, LANES) for vector in vectors], base)


def half_of(right, which):
    if right.ndim == 3:
        return lax.dynamic_index_in_dim(right, which, 0, keepdims=False)
    width = right.shape[1] // CORES
    return lax.dynamic_slice_in_dim(right, which * width, width, 1)


class Reduction:
    def __init__(self, terms, first, extra=None):
        self.size = lax.axis_size("batch")
        self.depth = self.size // (CORES * PAIR)
        self.rows = terms[0][0].shape[1] // self.size
        self.first = first
        self.terms, self.extra = terms, extra
        self.fast = splits(self.rows)
        self.widths = [
            right.shape[2] if right.ndim == 3 else right.shape[1] // CORES for _, _, right in terms
        ]
        self.state = ()
        self.todo = (
            [self.begin, self.by_first, self.by_second, self.by_depth, self.by_seq, self.finish]
            if self.fast
            else [self.plain]
        )

    def step(self):
        if self.todo:
            self.state = self.todo.pop(0)(*self.state)
        return self

    def result(self):
        while self.todo:
            self.step()
            self.state = self.launch(*self.state)
        return self.state

    def plain(self):
        whole = [
            weight_term(left, jnp.concatenate(list(right), axis=1) if right.ndim == 3 else right)
            for left, _, right in self.terms
        ] + ([] if self.extra is None else [self.extra])
        mine = lax.psum_scatter(
            jnp.concatenate(whole, axis=1), "batch", scatter_dimension=0, tiled=True
        )
        mine = lax.psum(mine, "seq").astype(jnp.float32)
        ends = [0]
        for item in whole:
            ends.append(ends[-1] + item.shape[1])
        return tuple(mine[:, i:j] for i, j in zip(ends, ends[1:]))

    def begin(self):
        self.sender = self.along_seq if self.first == "seq" else self.along_pair
        where = jnp.stack(place_of()).astype(jnp.int32)
        operands = [where]
        for left, far_left, right in self.terms:
            operands += [left, far_left, right, swap(half_of(right, 1 - where[2]), 1)]
        if self.extra is not None:
            operands += [self.extra, swap(self.extra, 1)]
        blend = 0 if self.extra is None else 2
        total = sum(self.widths) + (LANES if blend else 0)
        shape = jax.ShapeDtypeStruct((self.depth * PAIR, self.rows, total), jnp.bfloat16)
        height = 3 * LANES
        return tuple(
            pl.pallas_call(
                partial(
                    grad_kernel,
                    count=len(self.terms),
                    first=self.first,
                    rows=self.rows,
                    blend=blend,
                ),
                out_shape=(shape, shape),
                in_specs=[pl.BlockSpec(memory_space=pltpu.SMEM)]
                + [pl.BlockSpec(memory_space=pltpu.VMEM)] * (len(operands) - 1),
                out_specs=(pl.BlockSpec(memory_space=pltpu.VMEM),) * 2,
                scratch_shapes=[pltpu.VMEM((height, max(self.widths)), jnp.float32)],
                cost_estimate=pl.CostEstimate(flops=0, transcendentals=0, bytes_accessed=0),
                name="grad_blocks",
            )(*operands)
        )

    def launch(self, kept, *sent):
        if not self.fast:
            return (kept, *sent)
        return (kept, *self.sender(*sent))

    def along_seq(self, block):
        return (swap_seq(block),)

    def along_pair(self, block):
        return (swap(block, CORES),)

    def along_depth(self, *blocks):
        return tuple(
            swap(block, CORES * PAIR, self.depth, k) for k, block in enumerate(blocks, 1)
        )

    def along_core(self, block):
        return (swap(block, 1),)

    def by_first(self, kept, came):
        _, wide, _, seq = place_of()
        self.sender = self.along_pair if self.first == "seq" else self.along_seq
        kept = kept.astype(jnp.float32) + came.astype(jnp.float32)
        kept = kept.reshape(self.depth, 2, self.rows, -1)
        which = wide if self.first == "seq" else seq
        return tuple(
            lax.dynamic_index_in_dim(kept, i, 1, keepdims=False).astype(jnp.bfloat16)
            for i in (which, 1 - which)
        )

    def by_second(self, kept, came):
        deep, _, _, _ = place_of()
        self.sender = self.along_depth
        kept = kept.astype(jnp.float32) + came.astype(jnp.float32)
        return tuple(
            lax.dynamic_index_in_dim(kept, deep ^ k, 0, keepdims=False).astype(jnp.bfloat16)
            for k in range(self.depth)
        )

    def by_depth(self, kept, *came):
        total = kept.astype(jnp.float32)
        for block in came:
            total = total + block.astype(jnp.float32)
        self.sender = self.along_seq
        total = narrow(total)
        return total, total

    def by_seq(self, mine, came):
        _, _, core, seq = place_of()
        same = seq == core
        self.sender = self.along_core
        return jnp.where(same, mine, came), jnp.where(same, came, mine)

    def finish(self, mine, came):
        _, _, core, _ = place_of()
        self.fast = False
        low = jnp.where(core == 0, mine, came).astype(jnp.float32)
        high = jnp.where(core == 0, came, mine).astype(jnp.float32)
        results, start = [], 0
        for width in self.widths:
            cols = slice(start, start + width)
            results.append(jnp.concatenate([low[:, cols], high[:, cols]], axis=1))
            start += width
        if self.extra is not None:
            results.append(mine[:, start:].astype(jnp.float32))
        return tuple(results)


def advance(works, values=(), after=()):
    for work in works:
        work.step()
    states = [work.state for work in works]
    heads = [work.state[0] for work in after]
    states, heads, values = lax.optimization_barrier((states, heads, values))
    for work, state in zip(works, states):
        work.state = work.launch(*state)
    for work, head in zip(after, heads):
        work.state = (head, *work.state[1:])
    return values


def body(
    hidden,
    encoder,
    cotangent,
    token_offsets,
    token_lengths,
    frame_counts,
    corpus_ids,
    corpus_weights,
    norm_gains,
    norm_shifts,
    self_in,
    self_out,
    cross_query,
    cross_kv,
    cross_out,
    proj_bias,
    up_weight,
    up_bias,
    down_weight,
):
    hidden, cotangent = hidden[0], cotangent[0]
    row_count, model_width = hidden.shape
    shard_rows = norm_gains.shape[0]
    wide_cols = up_weight.shape[1]
    blocks = wide_cols // model_width
    size = lax.axis_size("batch")

    tail_width = 2 * LANES
    far = lambda block: swap(block, 1)
    small = jnp.concatenate(
        [norm_gains, norm_shifts, proj_bias, up_bias.reshape(shard_rows, blocks)], axis=1
    )
    small_cols = small.shape[1]
    small = jnp.pad(small, ((0, 0), (0, tail_width - small_cols)))
    first = Gather(jnp.concatenate([self_in, small], axis=1), "seq")
    second = Gather(jnp.concatenate([self_out, cross_query, cross_kv, cross_out], axis=1), "pair")
    up_blocks = up_weight.reshape(shard_rows, blocks, model_width).transpose(1, 0, 2)
    third = jnp.concatenate([up_blocks.reshape(-1, model_width), down_weight], axis=1)
    hidden_other = swap_seq(hidden)
    first.step()
    second.state, encoder, first.state, hidden_other = lax.optimization_barrier(
        (second.state, encoder, first.state, hidden_other)
    )
    first.step()
    second.step()
    first.state, second.state, third, encoder = lax.optimization_barrier(
        (first.state, second.state, third, encoder)
    )
    first.step()
    second.step()
    frame_mine = lax.all_to_all(encoder, "batch", split_axis=0, concat_axis=0, tiled=True)
    frame_mine = frame_mine.reshape(-1, model_width)
    third_all = lax.all_gather(third, "batch", axis=0, tiled=True)
    frame_other = swap_seq(frame_mine)
    first_all = first.result()

    self_in_all = first_all[:, : 3 * model_width]
    small_all = first_all[:, 3 * model_width : 3 * model_width + small_cols]
    gains = small_all[:, :4].astype(jnp.float32)
    shifts = small_all[:, 4:8].astype(jnp.float32)
    biases = small_all[:, 8:15].astype(jnp.float32)
    up_bias_all = small_all[:, 15:].reshape(-1).astype(jnp.float32)

    offset, length, frame_count = token_offsets[0], token_lengths[0], frame_counts[0]
    seq_index = lax.axis_index("seq")
    slots = jnp.arange(row_count, dtype=jnp.int32)
    positions = seq_index * row_count + slots
    positions_other = (1 - seq_index) * row_count + slots
    zero_row = jnp.zeros((model_width,), jnp.float32)
    inputs = hidden.astype(jnp.float32)
    normed_one, scale_one = layer_parts(inputs)
    act_one = (normed_one * gains[:, 0] + shifts[:, 0]).astype(jnp.bfloat16)
    normed_far, _ = layer_parts(hidden_other.astype(jnp.float32))
    act_far = (normed_far * gains[:, 0] + shifts[:, 0]).astype(jnp.bfloat16)
    qkv_bias = jnp.concatenate([biases[:, 0], zero_row, biases[:, 1]])
    qkv_local = (dot_right(act_one, self_in_all) + qkv_bias).astype(jnp.bfloat16)
    self_query = qkv_local[:, :model_width]
    pair_far = (
        dot_right(act_far, self_in_all[:, model_width:]) + qkv_bias[model_width:]
    ).astype(jnp.bfloat16)
    self_pairs = jnp.concatenate([pair_far, qkv_local[:, model_width:]], axis=0)
    key_pos = jnp.concatenate([positions_other, positions])[:, None]
    query_pos = positions[None, :]
    self_mask = (key_pos <= query_pos) & ((key_pos >= offset) | (key_pos == query_pos))
    self_bias = jnp.where(self_mask, 0.0, -jnp.inf)
    self_query, self_pairs, second.state = lax.optimization_barrier(
        (self_query, self_pairs, second.state)
    )
    second.step()
    self_mixed, self_total = attend(self_query, self_pairs, self_bias)
    self_mixed, second.state = lax.optimization_barrier((self_mixed, second.state))
    second_all = second.result()
    self_out_all = second_all[:, :model_width]
    query_all = second_all[:, model_width : 2 * model_width]
    kv_all = second_all[:, 2 * model_width : 4 * model_width]
    cross_out_all = second_all[:, 4 * model_width :]
    down_all = third_all[:, model_width:]
    up_all = (
        third_all[:, :model_width]
        .reshape(size, blocks, shard_rows, model_width)
        .transpose(0, 2, 1, 3)
        .reshape(model_width, wide_cols)
    )
    after_self = inputs + dot_right(self_mixed, self_out_all) + biases[:, 2]
    normed_two, scale_two = layer_parts(after_self)
    act_two = (normed_two * gains[:, 1] + shifts[:, 1]).astype(jnp.bfloat16)
    cross_queries = (dot_right(act_two, query_all) + biases[:, 3]).astype(jnp.bfloat16)
    frames = jnp.concatenate([frame_mine, frame_other], axis=0)
    kv_bias = jnp.concatenate([zero_row, biases[:, 4]])
    cross_pairs = (dot_right(frames, kv_all) + kv_bias).astype(jnp.bfloat16)
    half_slots = frame_mine.shape[0]
    owner_frames = encoder.shape[1]
    gathered = jnp.arange(2 * half_slots, dtype=jnp.int32)
    half_index = (gathered // half_slots) ^ seq_index
    within = gathered % half_slots
    frame_ids = (within // owner_frames * 2 + half_index) * owner_frames + within % owner_frames
    frame_bias = jnp.broadcast_to(
        jnp.where(frame_ids < frame_count, 0.0, -jnp.inf)[:, None], (2 * half_slots, row_count)
    )
    cross_mixed, cross_total = attend(cross_queries, cross_pairs, frame_bias)
    after_cross = after_self + dot_right(cross_mixed, cross_out_all) + biases[:, 5]
    normed_three, scale_three = layer_parts(after_cross)
    act_three = (normed_three * gains[:, 2] + shifts[:, 2]).astype(jnp.bfloat16)
    up_value = dot_right(act_three, up_all) + up_bias_all
    gelu_value, gelu_pull = jax.vjp(partial(jax.nn.gelu, approximate=False), up_value)
    hidden_act = gelu_value.astype(jnp.bfloat16)
    after_mlp = after_cross + dot_right(hidden_act, down_all) + biases[:, 6]
    normed_last, scale_last = layer_parts(after_mlp)
    result = (normed_last * gains[:, 3] + shifts[:, 3]).astype(jnp.bfloat16)
    corpus_match = corpus_ids[0] == jnp.arange(corpus_weights.shape[0], dtype=jnp.int32)
    seq_weight = jnp.sum(jnp.where(corpus_match, corpus_weights, 0.0))
    live_rows = (positions >= offset) & (positions < offset + length)
    grad_out = cotangent.astype(jnp.float32) * jnp.where(live_rows, seq_weight, 0.0)[:, None]
    grad_mlp, gain_last, shift_last = layer_back(grad_out, normed_last, scale_last, gains[:, 3])
    grad_down = grad_mlp.astype(jnp.bfloat16)
    down_bias = col_sum(grad_down)
    grad_act = dot_left(grad_down, down_all)
    grad_up = gelu_pull(grad_act)[0].astype(jnp.bfloat16)
    up_bias_columns = jnp.pad(
        col_sum(grad_up).astype(jnp.bfloat16).reshape(model_width, blocks),
        ((0, 0), (small_cols - blocks, LANES - small_cols)),
    )
    wide_term = jnp.concatenate(
        [weight_term(hidden_act, grad_down).reshape(size, -1, model_width)]
        + [
            weight_term(act_three, part).reshape(size, shard_rows, model_width)
            for part in jnp.split(grad_up, blocks, axis=1)
        ],
        axis=1,
    )
    wide_term, grad_up = lax.optimization_barrier((wide_term, grad_up))
    wide_sum = lax.psum_scatter(wide_term, "batch", scatter_dimension=0, tiled=True)[0]
    back_three, gain_three, shift_three = layer_back(
        dot_left(grad_up, up_all), normed_three, scale_three, gains[:, 2]
    )
    grad_cross = grad_mlp + back_three
    grad_cross_in = grad_cross.astype(jnp.bfloat16)
    cross_out_bias = col_sum(grad_cross_in)
    grad_cross_mixed = dot_left(grad_cross_in, cross_out_all).astype(jnp.bfloat16)
    grad_cq, grad_frame_pairs = attend_back(
        cross_queries, cross_pairs, frame_bias, cross_total, grad_cross_mixed
    )
    frame_grads = dot_left(grad_frame_pairs[0], kv_all[:, :model_width]) + dot_left(
        grad_frame_pairs[1], kv_all[:, model_width:]
    )
    frame_grads = frame_grads.astype(jnp.bfloat16)
    grad_cq, frame_kept, frame_sent = lax.optimization_barrier(
        (grad_cq, frame_grads[:half_slots], frame_grads[half_slots:])
    )
    frame_came = swap_seq(frame_sent)
    kv_bias_term = col_sum(grad_cross_mixed)
    query_bias = col_sum(grad_cq)
    back_two, gain_two, shift_two = layer_back(
        dot_left(grad_cq, query_all), normed_two, scale_two, gains[:, 1]
    )
    grad_self = grad_cross + back_two
    grad_self_in = grad_self.astype(jnp.bfloat16)
    self_out_bias = col_sum(grad_self_in)
    grad_self_mixed = dot_left(grad_self_in, self_out_all).astype(jnp.bfloat16)
    cross_sum = Reduction(
        [
            (frames, far(frames), grad_frame_pairs),
            (cross_mixed, far(cross_mixed), grad_cross_in),
            (act_two, far(act_two), grad_cq),
            (self_mixed, far(self_mixed), grad_self_in),
        ],
        "seq",
    )
    grad_self_mixed = advance([cross_sum], grad_self_mixed)
    grad_self_query, grad_self_pairs = attend_back(
        self_query, self_pairs, self_bias, self_total, grad_self_mixed
    )
    both_acts = jnp.concatenate([act_far, act_one], axis=0)
    self_pair_sum = Reduction([(both_acts, far(both_acts), grad_self_pairs)], "pair")
    grad_self_query, grad_self_pairs = advance(
        [self_pair_sum], (grad_self_query, grad_self_pairs)
    )
    value_sums = col_sum(grad_self_mixed)
    norm_side, norm_far, small_term = self_tail(
        grad_self_query,
        grad_self_pairs,
        first_all,
        normed_one,
        normed_far,
        [
            value_sums,
            self_out_bias,
            query_bias,
            kv_bias_term,
            cross_out_bias,
            down_bias,
            gain_two,
            gain_three,
            gain_last,
            shift_two,
            shift_three,
            shift_last,
        ],
        up_bias_columns,
    )
    self_sum = Reduction([(act_one, far(act_one), grad_self_query)], "seq", small_term)
    owner_grads = frame_kept.astype(jnp.float32) + frame_came.astype(jnp.float32)
    norm_far, owner_grads = advance([self_sum], (norm_far, owner_grads.astype(jnp.bfloat16)))
    norm_came = swap_seq(norm_far)
    grad_encoder = lax.all_to_all(
        owner_grads.reshape(size, owner_frames, model_width),
        "batch",
        split_axis=0,
        concat_axis=0,
        tiled=True,
    )
    advance([cross_sum, self_pair_sum], after=[self_sum])
    norm_came = advance([self_sum], norm_came, after=[cross_sum, self_pair_sum])
    advance([cross_sum, self_pair_sum], after=[self_sum])
    grad_encoder, wide_sum = advance(
        [self_sum], (grad_encoder, wide_sum), after=[cross_sum, self_pair_sum]
    )
    grad_encoder = grad_encoder.astype(jnp.float32)
    back_one, _, _ = layer_back(
        norm_side + norm_came.astype(jnp.float32), normed_one, scale_one, gains[:, 0]
    )
    grad_hidden = grad_self + back_one
    wide_sum = wide_sum.astype(jnp.float32) + swap_seq(wide_sum).astype(jnp.float32)
    inner_rows = down_weight.shape[0]
    grad_up_weight = (
        wide_sum[inner_rows:]
        .reshape(blocks, shard_rows, model_width)
        .transpose(1, 0, 2)
        .reshape(shard_rows, wide_cols)
    )
    grad_cross_kv, grad_cross_out, grad_cross_query, grad_self_out = cross_sum.result()
    grad_self_keys = self_pair_sum.result()[0]
    grad_self_queries, small_sum = self_sum.result()
    return (
        result[None],
        grad_hidden[None],
        grad_encoder,
        jnp.concatenate([small_sum[:, :1], small_sum[:, 9:12]], axis=1),
        jnp.concatenate([small_sum[:, 1:2], small_sum[:, 12:15]], axis=1),
        jnp.concatenate([grad_self_queries, grad_self_keys], axis=1),
        grad_self_out,
        grad_cross_query,
        grad_cross_kv,
        grad_cross_out,
        small_sum[:, 2:9],
        grad_up_weight,
        small_sum[:, 15:small_cols].reshape(-1),
        wide_sum[:inner_rows],
    )


def solution(mesh):
    in_specs = (
        P("batch", "seq", None),
        P(None, ("batch", "seq"), None),
        P("batch", "seq", None),
        P("batch"),
        P("batch"),
        P("batch"),
        P("batch"),
        P(),
        P("batch", None),
        P("batch", None),
        P("batch", None),
        P("batch", None),
        P("batch", None),
        P("batch", None),
        P("batch", None),
        P("batch", None),
        P("batch", None),
        P("batch"),
        P("batch", None),
    )
    out_specs = (
        P("batch", "seq", None),
        P("batch", "seq", None),
        P(None, ("batch", "seq"), None),
        P("batch", None),
        P("batch", None),
        P("batch", None),
        P("batch", None),
        P("batch", None),
        P("batch", None),
        P("batch", None),
        P("batch", None),
        P("batch", None),
        P("batch"),
        P("batch", None),
    )
    return jax.shard_map(body, mesh=mesh, in_specs=in_specs, out_specs=out_specs, check_vma=False)
```

```python
from functools import partial

import math

import jax
import jax.numpy as jnp
from jax import lax
from jax.experimental import pallas as pl
from jax.experimental.pallas import tpu as pltpu
from jax.sharding import PartitionSpec as P

HEAD_DIM = 64
LANES = 128


EPS = 1e-05

def layer_parts(values):
    center = values - jnp.mean(values, axis=-1, keepdims=True)
    inv_std = lax.rsqrt(jnp.mean(center * center, axis=-1, keepdims=True) + EPS)
    return (center * inv_std, inv_std)


def layer_back(grad_side, normed, inv_std, gain):
    scaled = grad_side * gain
    mean_one = jnp.mean(scaled, axis=-1, keepdims=True)
    mean_two = jnp.mean(scaled * normed, axis=-1, keepdims=True)
    grad_in = inv_std * (scaled - mean_one - normed * mean_two)
    return (grad_in, jnp.sum(grad_side * normed, axis=0), jnp.sum(grad_side, axis=0))


def dot_right(left_side, weight):
    return jnp.dot(left_side, weight, preferred_element_type=jnp.float32)


def dot_left(grad_side, weight):
    return jnp.einsum("cj,ij->ci", grad_side, weight, preferred_element_type=jnp.float32)


def weight_term(left_side, grad_side):
    return jnp.einsum(
        "ci,cj->ij", left_side, grad_side, preferred_element_type=jnp.float32
    ).astype(jnp.bfloat16)


def col_sum(grad_side):
    return jnp.sum(grad_side, axis=0, dtype=jnp.float32)


def hold(steps, values):
    return lax.optimization_barrier((steps, values))

ROWS_BY_LANES = (((1,), (1,)), ((), ()))
DOWN_BOTH = (((0,), (0,)), ((), ()))


def head_parts(block):
    lane = lax.broadcasted_iota(jnp.int32, block.shape, 1)
    zero = jnp.zeros_like(block)
    return (
        jnp.where(lane < HEAD_DIM, block, zero),
        jnp.where(lane < HEAD_DIM, zero, block),
    )


def dot_of(left, right, dims):
    return lax.dot_general(left, right, dims, preferred_element_type=jnp.float32)


def attend_kernel(query_ref, key_ref, value_ref, bias_ref, mixed_ref, total_ref):
    score_scale = HEAD_DIM ** (-0.5)
    key, value = key_ref[...], value_ref[...]
    queries = head_parts(query_ref[...] * jnp.bfloat16(score_scale))
    scores = [dot_of(key, query, ROWS_BY_LANES) + bias_ref[...] for query in queries]
    tops = [jnp.max(item, axis=0, keepdims=True) for item in scores]
    terms = [jnp.exp(item - top) for item, top in zip(scores, tops)]
    totals = [jnp.sum(item, axis=0, keepdims=True) for item in terms]
    sides = [dot_of(value, item.astype(jnp.bfloat16), DOWN_BOTH) for item in terms]
    for head in range(2):
        total_ref[0, head : head + 1, :] = tops[head] + jnp.log(totals[head])
    mixed = [
        sides[head][head * HEAD_DIM : (head + 1) * HEAD_DIM] / totals[head] for head in range(2)
    ]
    mixed_ref[...] = jnp.concatenate(mixed, axis=0).T.astype(jnp.bfloat16)


def attend_back_kernel(
    query_ref, key_ref, value_ref, bias_ref, total_ref, grad_ref, gq_ref, pair_ref
):
    score_scale = HEAD_DIM ** (-0.5)
    key, value = key_ref[...], value_ref[...]
    queries = head_parts(query_ref[...] * jnp.bfloat16(score_scale))
    grads = head_parts(grad_ref[...])
    scores = [dot_of(key, query, ROWS_BY_LANES) + bias_ref[...] for query in queries]
    terms = [
        jnp.exp(item - total_ref[0, head : head + 1, :]) for head, item in enumerate(scores)
    ]
    grad_terms = [
        item * dot_of(value, grad, ROWS_BY_LANES) for item, grad in zip(terms, grads)
    ]
    row_dots = [jnp.sum(item, axis=0, keepdims=True) for item in grad_terms]
    grad_scores = [
        (grad_term - term * row_dot).astype(jnp.bfloat16)
        for grad_term, term, row_dot in zip(grad_terms, terms, row_dots)
    ]
    values = [
        jnp.dot(item.astype(jnp.bfloat16), grad, preferred_element_type=jnp.float32)
        for item, grad in zip(terms, grads)
    ]
    keys = [
        jnp.dot(item, query, preferred_element_type=jnp.float32)
        for item, query in zip(grad_scores, queries)
    ]
    sides = [dot_of(key, item, DOWN_BOTH) for item in grad_scores]
    pair_ref[0] = (keys[0] + keys[1]).astype(jnp.bfloat16)
    pair_ref[1] = (values[0] + values[1]).astype(jnp.bfloat16)
    picked = [
        sides[head][head * HEAD_DIM : (head + 1) * HEAD_DIM] * score_scale for head in range(2)
    ]
    gq_ref[...] = jnp.concatenate(picked, axis=0).T.astype(jnp.bfloat16)


def head_specs(rows, keys, blocks):
    return [
        pl.BlockSpec((rows, LANES), lambda i: (0, i)),
        pl.BlockSpec((keys, LANES), lambda i: (0, i)),
        pl.BlockSpec((keys, LANES), lambda i: (0, i + blocks)),
        pl.BlockSpec((keys, rows), lambda i: (0, 0)),
    ]


def attend(queries, pairs, bias):
    rows, width = queries.shape
    keys = pairs.shape[0]
    blocks = width // LANES
    return pl.pallas_call(
        attend_kernel,
        grid=(blocks,),
        out_shape=(
            jax.ShapeDtypeStruct((rows, width), jnp.bfloat16),
            jax.ShapeDtypeStruct((blocks, 2, rows), jnp.float32),
        ),
        in_specs=head_specs(rows, keys, blocks),
        out_specs=(
            pl.BlockSpec((rows, LANES), lambda i: (0, i)),
            pl.BlockSpec((1, 2, rows), lambda i: (i, 0, 0)),
        ),
        cost_estimate=pl.CostEstimate(flops=0, transcendentals=0, bytes_accessed=0),
        name="attend",
    )(queries, pairs, pairs, bias)


def attend_back(queries, pairs, bias, totals, grads):
    rows, width = queries.shape
    keys = pairs.shape[0]
    blocks = width // LANES
    return pl.pallas_call(
        attend_back_kernel,
        grid=(blocks,),
        out_shape=(
            jax.ShapeDtypeStruct((rows, width), jnp.bfloat16),
            jax.ShapeDtypeStruct((2, keys, width), jnp.bfloat16),
        ),
        in_specs=head_specs(rows, keys, blocks)
        + [
            pl.BlockSpec((1, 2, rows), lambda i: (i, 0, 0)),
            pl.BlockSpec((rows, LANES), lambda i: (0, i)),
        ],
        out_specs=(
            pl.BlockSpec((rows, LANES), lambda i: (0, i)),
            pl.BlockSpec((2, keys, LANES), lambda i: (0, 0, i)),
        ),
        cost_estimate=pl.CostEstimate(flops=0, transcendentals=0, bytes_accessed=0),
        name="attend_back",
    )(queries, pairs, pairs, bias, totals, grads)


CORES = 2
PAIR = 2
FLIP = [(0, 1), (1, 0)]


def partners(stride, radix, step):
    pairs = []
    for i in range(lax.axis_size("batch")):
        digit = i // stride % radix
        pairs.append((i, i + ((digit ^ step) - digit) * stride))
    return pairs


def swap(block, stride, radix=2, step=1):
    return lax.ppermute(block, "batch", partners(stride, radix, step))


def swap_seq(block):
    return lax.ppermute(block, "seq", FLIP)


def place_of():
    batch = lax.axis_index("batch")
    return (
        batch // (CORES * PAIR),
        batch // CORES % PAIR,
        batch % CORES,
        lax.axis_index("seq"),
    )


def splits(rows):
    depth = lax.axis_size("batch") // (CORES * PAIR)
    return rows % 48 == 0 and depth == 4 and lax.axis_size("seq") == 2


def place_kernel(where_ref, *refs, depth, rows, half):
    pieces, out_ref, sem = refs[:8], refs[8], refs[9]
    deep, wide, core, seq = where_ref[0], where_ref[1], where_ref[2], where_ref[3]
    started = []
    for c in range(2):
        column, across, side, side_across = pieces[4 * c : 4 * c + 4]
        for w, (near, far) in enumerate(((column, side), (across, side_across))):
            for k in range(depth):
                base = (((deep ^ k) * PAIR + (wide ^ w)) * CORES + (core ^ c)) * rows
                row_span = pl.ds(pl.multiple_of(base, 16), rows)
                for source, part in ((near, seq), (far, 1 - seq)):
                    col_span = pl.ds(pl.multiple_of(part * half, LANES), half)
                    copy = pltpu.make_async_copy(
                        source.at[k], out_ref.at[row_span, col_span], sem
                    )
                    copy.start()
                    started.append(copy)
    for copy in started:
        copy.wait()


class Gather:
    def __init__(self, shard, last):
        self.rows, self.cols = shard.shape
        self.half = self.cols // 2
        self.last = last
        self.depth = lax.axis_size("batch") // (CORES * PAIR)
        self.state = (shard,)
        self.todo = (
            [self.by_depth, self.by_both, self.by_last, self.place]
            if splits(self.rows)
            else [self.plain]
        )

    def step(self):
        if self.todo:
            self.state = self.todo.pop(0)(*self.state)
        return self

    def result(self):
        while self.todo:
            self.step()
        return self.state[0]

    def plain(self, shard):
        return (lax.all_gather(shard, "batch", axis=0, tiled=True),)

    def by_depth(self, shard):
        part = lax.dynamic_slice_in_dim(shard, lax.axis_index("seq") * self.half, self.half, 1)
        came = [swap(part, CORES * PAIR, self.depth, k) for k in range(1, self.depth)]
        return (jnp.stack([part] + came),)

    def by_both(self, column):
        return column, swap(column, CORES), swap_seq(column)

    def by_last(self, column, across, side):
        far = swap_seq(across) if self.last == "seq" else swap(side, CORES)
        return column, across, side, far

    def place(self, *mine):
        other = tuple(swap(piece, 1) for piece in mine)
        total = lax.axis_size("batch") * self.rows
        call = pl.pallas_call(
            partial(place_kernel, depth=self.depth, rows=self.rows, half=self.half),
            out_shape=jax.ShapeDtypeStruct((total, self.cols), mine[0].dtype),
            in_specs=[pl.BlockSpec(memory_space=pltpu.SMEM)]
            + [pl.BlockSpec(memory_space=pl.ANY)] * 8,
            out_specs=pl.BlockSpec(memory_space=pltpu.VMEM),
            scratch_shapes=[pltpu.SemaphoreType.DMA],
            cost_estimate=pl.CostEstimate(flops=0, transcendentals=0, bytes_accessed=0),
            name="place_rows",
        )
        return (call(jnp.stack(place_of()).astype(jnp.int32), *mine, *other),)


def narrow(values):
    return lax.reduce_precision(values, 8, 7).astype(jnp.bfloat16)


def grad_kernel(where_ref, *refs, count, first, rows, blend):
    terms, refs = [refs[4 * i : 4 * i + 4] for i in range(count)], refs[4 * count :]
    extras, (kept_ref, sent_ref, total_ref) = refs[:blend], refs[blend:]
    wide, core, seq = where_ref[1], where_ref[2], where_ref[3]
    height = total_ref.shape[0]
    groups = CORES * kept_ref.shape[0] * rows // height

    def group_step(group, carry):
        start = 0
        for left_ref, far_left_ref, right_ref, far_right_ref in terms:
            width = far_right_ref.shape[1]
            span = pl.ds(pl.multiple_of(group * height, LANES), height)
            if len(right_ref.shape) == 3:
                right = right_ref[core]
            else:
                right = right_ref[:, pl.ds(pl.multiple_of(core * width, LANES), width)]
            total_ref[:, :width] = dot_of(left_ref[:, span], right, DOWN_BOTH) + dot_of(
                far_left_ref[:, span], far_right_ref[...], DOWN_BOTH
            )
            cols = slice(start, start + width)
            for place, near, far in routes(group, height, first, rows, wide, seq):
                for out_ref, base in ((kept_ref, near), (sent_ref, far)):
                    picked = total_ref[pl.ds(pl.multiple_of(base, 16), rows), :width]
                    out_ref[place, :, cols] = picked.astype(jnp.bfloat16)
            start += width
        if blend:
            cols = slice(start, start + LANES)
            for place, near, far in routes(group, height, first, rows, wide, seq):
                for out_ref, base in ((kept_ref, near), (sent_ref, far)):
                    picked = pl.ds(pl.multiple_of(group * height + base, 16), rows)
                    out_ref[place, :, cols] = (
                        extras[0][picked, :].astype(jnp.float32)
                        + extras[1][picked, :].astype(jnp.float32)
                    ).astype(jnp.bfloat16)
        return carry

    lax.fori_loop(0, groups, group_step, 0)


def routes(group, height, first, rows, wide, seq):
    if first == "seq":
        pairs = height // (2 * rows)
        return [
            (group * pairs + i, (2 * i + seq) * rows, (2 * i + 1 - seq) * rows)
            for i in range(pairs)
        ]
    quads = height // (4 * rows)
    return [
        (
            (group * quads + i) * 2 + j,
            (4 * i + 2 * wide + j) * rows,
            (4 * i + 2 * (1 - wide) + j) * rows,
        )
        for i in range(quads)
        for j in range(2)
    ]


def back_by_norm(grad_side, normed, inv_std, gain):
    scaled = grad_side * gain
    mean_one = jnp.mean(scaled, axis=-1, keepdims=True)
    mean_two = jnp.mean(scaled * normed, axis=-1, keepdims=True)
    return inv_std * (scaled - mean_one - normed * mean_two)


def sum_rows(values):
    return jnp.sum(values, axis=0, keepdims=True)


def feed_forward_kernel(
    act_ref,
    after_ref,
    grad_ref,
    live_ref,
    gain_ref,
    shift_ref,
    bias_ref,
    up_bias_ref,
    weight_ref,
    result_ref,
    cross_ref,
    sums_ref,
    up_sums_ref,
    wide_ref,
    up_ref,
    down_ref,
    hidden_ref,
    slope_ref,
    side_ref,
    term_ref,
    in_sem,
    out_sem,
):
    blocks, width, _ = up_ref.shape
    size = wide_ref.shape[0]
    piece = width // size
    inner = blocks * piece
    per = size // blocks
    copies = []
    for j in range(blocks):
        for b in range(size):
            copies.append(
                (
                    weight_ref.at[pl.ds(b * inner + j * piece, piece), pl.ds(0, width)],
                    up_ref.at[j, pl.ds(b * piece, piece)],
                    in_sem.at[j],
                )
            )
        copies.append(
            (
                weight_ref.at[pl.ds(j * width, width), pl.ds(width, width)],
                down_ref.at[j],
                in_sem.at[blocks + j],
            )
        )
    started = [pltpu.make_async_copy(*copy) for copy in copies]
    for copy in started:
        copy.start()

    def wait_up(j):
        pltpu.make_async_copy(down_ref.at[j], up_ref.at[j], in_sem.at[j]).wait()

    def wait_down(j):
        pltpu.make_async_copy(up_ref.at[j], down_ref.at[j], in_sem.at[blocks + j]).wait()

    act = act_ref[...]
    half_root, slope_scale = math.sqrt(0.5), 1.0 / math.sqrt(2.0 * math.pi)

    def rise(j, total):
        wait_up(j)
        up = dot_of(act, up_ref[j], (((1,), (0,)), ((), ()))) + up_bias_ref[j]
        level = 0.5 * (1.0 + lax.erf(up * half_root))
        hidden_ref[j] = (up * level).astype(jnp.bfloat16)
        slope_ref[j] = level + up * (slope_scale * jnp.exp(-0.5 * up * up))
        wait_down(j)
        return total + dot_of(hidden_ref[j], down_ref[j], (((1,), (0,)), ((), ())))

    after = after_ref[...]
    mlp = lax.fori_loop(0, blocks, rise, after + bias_ref[...])
    normed, inv_std = layer_parts(mlp)
    result_ref[...] = (normed * gain_ref[1:2] + shift_ref[...]).astype(jnp.bfloat16)
    grad_out = grad_ref[...].astype(jnp.float32) * live_ref[...]
    grad_mlp = back_by_norm(grad_out, normed, inv_std, gain_ref[1:2])
    grad_down = grad_mlp.astype(jnp.bfloat16)

    def fall(j, total):
        grad_act = dot_of(grad_down, down_ref[j], ROWS_BY_LANES)
        grad_up = slope_ref[j] * grad_act
        side_ref[j] = grad_up.astype(jnp.bfloat16)
        up_sums_ref[j] = sum_rows(grad_up)
        return total + dot_of(side_ref[j], up_ref[j], ROWS_BY_LANES)

    grad_three = lax.fori_loop(0, blocks, fall, jnp.zeros_like(mlp))

    def outward(j):
        return (
            pltpu.make_async_copy(
                term_ref.at[pl.ds(j * per, per), pl.ds(0, inner)],
                wide_ref.at[pl.ds(j * per, per), pl.ds(0, inner)],
                out_sem.at[j],
            ),
            pltpu.make_async_copy(
                term_ref.at[:, pl.ds(pl.multiple_of(inner + j * piece, 16), piece)],
                wide_ref.at[:, pl.ds(pl.multiple_of(inner + j * piece, 16), piece)],
                out_sem.at[blocks + j],
            ),
        )

    def weigh(j, carry):
        down = dot_of(hidden_ref[j], grad_down, DOWN_BOTH).astype(jnp.bfloat16)
        for t in range(per):
            term_ref[j * per + t, :inner] = down[t * inner : (t + 1) * inner]
        up = dot_of(act, side_ref[j], DOWN_BOTH).astype(jnp.bfloat16)
        span = pl.ds(pl.multiple_of(inner + j * piece, 16), piece)
        for b in range(size):
            term_ref[b, span] = up[b * piece : (b + 1) * piece]
        for copy in outward(j):
            copy.start()
        return carry

    lax.fori_loop(0, blocks, weigh, 0)
    normed_three, scale_three = layer_parts(after)
    cross_ref[...] = grad_mlp + back_by_norm(
        grad_three, normed_three, scale_three, gain_ref[0:1]
    )
    rows = [
        grad_three * normed_three,
        grad_three,
        grad_out * normed,
        grad_out,
        grad_down.astype(jnp.float32),
    ]
    for i, item in enumerate(rows):
        sums_ref[i : i + 1] = sum_rows(item)

    def finish(j, carry):
        for copy in outward(j):
            copy.wait()
        return carry

    lax.fori_loop(0, blocks, finish, 0)


def feed_forward(act, after, grad, live, gains, shift, bias, up_bias, weight, size):
    rows, width = act.shape
    blocks = up_bias.shape[0]
    inner = blocks * width // size
    shape = jax.ShapeDtypeStruct
    vmem = pl.BlockSpec(memory_space=pltpu.VMEM)
    return pl.pallas_call(
        feed_forward_kernel,
        out_shape=(
            shape((rows, width), jnp.bfloat16),
            shape((rows, width), jnp.float32),
            shape((8, width), jnp.float32),
            shape((blocks, 1, width), jnp.float32),
            shape((size, 2 * inner, width), jnp.bfloat16),
        ),
        in_specs=[vmem] * 8 + [pl.BlockSpec(memory_space=pl.ANY)],
        out_specs=(vmem,) * 4 + (pl.BlockSpec(memory_space=pl.ANY),),
        scratch_shapes=[
            pltpu.VMEM((blocks, width, width), jnp.bfloat16),
            pltpu.VMEM((blocks, width, width), jnp.bfloat16),
            pltpu.VMEM((blocks, rows, width), jnp.bfloat16),
            pltpu.VMEM((blocks, rows, width), jnp.float32),
            pltpu.VMEM((blocks, rows, width), jnp.bfloat16),
            pltpu.VMEM((size, 2 * inner, width), jnp.bfloat16),
            pltpu.SemaphoreType.DMA((2 * blocks,)),
            pltpu.SemaphoreType.DMA((2 * blocks,)),
        ],
        cost_estimate=pl.CostEstimate(flops=0, transcendentals=0, bytes_accessed=0),
        name="feed_forward",
    )(act, after, grad, live, gains, shift, bias, up_bias, weight)


def self_tail_kernel(query_ref, pair_ref, weight_ref, near_ref, far_ref, *refs):
    vectors, base_ref, (side_ref, sent_ref, column_ref) = refs[:-4], refs[-4], refs[-3:]
    rows, width = query_ref.shape
    both = dot_of(pair_ref[0], weight_ref[:, width : 2 * width], ROWS_BY_LANES) + dot_of(
        pair_ref[1], weight_ref[:, 2 * width : 3 * width], ROWS_BY_LANES
    )
    far = both[:rows]
    side = both[rows:] + dot_of(query_ref[...], weight_ref[:, :width], ROWS_BY_LANES)
    side_ref[...] = side
    sent_ref[...] = far.astype(jnp.bfloat16)
    sums = [
        jnp.sum(side * near_ref[...] + far * far_ref[...], axis=0, keepdims=True),
        jnp.sum(side + far, axis=0, keepdims=True),
        jnp.sum(query_ref[...].astype(jnp.float32), axis=0, keepdims=True),
    ]
    count = len(sums) + len(vectors)
    lane = lax.broadcasted_iota(jnp.int32, (LANES, LANES), 1)
    blank = jnp.zeros((LANES - count, LANES), jnp.float32)
    for i in range(width // LANES):
        here = slice(i * LANES, (i + 1) * LANES)
        block = jnp.concatenate(
            [item[:, here] for item in sums] + [row[i : i + 1, :] for row in vectors] + [blank],
            axis=0,
        )
        column_ref[here, :] = jnp.where(
            lane < count, block.T, base_ref[here, :].astype(jnp.float32)
        ).astype(jnp.bfloat16)


def self_tail(query, pairs, weight, near, far, vectors, base):
    rows, width = query.shape
    return pl.pallas_call(
        self_tail_kernel,
        out_shape=(
            jax.ShapeDtypeStruct((rows, width), jnp.float32),
            jax.ShapeDtypeStruct((rows, width), jnp.bfloat16),
            jax.ShapeDtypeStruct(base.shape, jnp.bfloat16),
        ),
        cost_estimate=pl.CostEstimate(flops=0, transcendentals=0, bytes_accessed=0),
        name="self_tail",
    )(query, pairs, weight, near, far, *[vector.reshape(-1, LANES) for vector in vectors], base)


def half_of(right, which):
    if right.ndim == 3:
        return lax.dynamic_index_in_dim(right, which, 0, keepdims=False)
    width = right.shape[1] // CORES
    return lax.dynamic_slice_in_dim(right, which * width, width, 1)


class Reduction:
    def __init__(self, terms, first, extra=None):
        self.size = lax.axis_size("batch")
        self.depth = self.size // (CORES * PAIR)
        self.rows = terms[0][0].shape[1] // self.size
        self.first = first
        self.terms, self.extra = terms, extra
        self.fast = splits(self.rows)
        self.widths = [
            right.shape[2] if right.ndim == 3 else right.shape[1] // CORES for _, _, right in terms
        ]
        self.state = ()
        self.todo = (
            [self.begin, self.by_first, self.by_second, self.by_depth, self.by_seq, self.finish]
            if self.fast
            else [self.plain]
        )

    def step(self):
        if self.todo:
            self.state = self.todo.pop(0)(*self.state)
        return self

    def result(self):
        while self.todo:
            self.step()
            self.state = self.launch(*self.state)
        return self.state

    def plain(self):
        whole = [
            weight_term(left, jnp.concatenate(list(right), axis=1) if right.ndim == 3 else right)
            for left, _, right in self.terms
        ] + ([] if self.extra is None else [self.extra])
        mine = lax.psum_scatter(
            jnp.concatenate(whole, axis=1), "batch", scatter_dimension=0, tiled=True
        )
        mine = lax.psum(mine, "seq").astype(jnp.float32)
        ends = [0]
        for item in whole:
            ends.append(ends[-1] + item.shape[1])
        return tuple(mine[:, i:j] for i, j in zip(ends, ends[1:]))

    def begin(self):
        self.sender = self.along_seq if self.first == "seq" else self.along_pair
        where = jnp.stack(place_of()).astype(jnp.int32)
        operands = [where]
        for left, far_left, right in self.terms:
            operands += [left, far_left, right, swap(half_of(right, 1 - where[2]), 1)]
        if self.extra is not None:
            operands += [self.extra, swap(self.extra, 1)]
        blend = 0 if self.extra is None else 2
        total = sum(self.widths) + (LANES if blend else 0)
        shape = jax.ShapeDtypeStruct((self.depth * PAIR, self.rows, total), jnp.bfloat16)
        height = 3 * LANES
        return tuple(
            pl.pallas_call(
                partial(
                    grad_kernel,
                    count=len(self.terms),
                    first=self.first,
                    rows=self.rows,
                    blend=blend,
                ),
                out_shape=(shape, shape),
                in_specs=[pl.BlockSpec(memory_space=pltpu.SMEM)]
                + [pl.BlockSpec(memory_space=pltpu.VMEM)] * (len(operands) - 1),
                out_specs=(pl.BlockSpec(memory_space=pltpu.VMEM),) * 2,
                scratch_shapes=[pltpu.VMEM((height, max(self.widths)), jnp.float32)],
                cost_estimate=pl.CostEstimate(flops=0, transcendentals=0, bytes_accessed=0),
                name="grad_blocks",
            )(*operands)
        )

    def launch(self, kept, *sent):
        if not self.fast:
            return (kept, *sent)
        return (kept, *self.sender(*sent))

    def along_seq(self, block):
        return (swap_seq(block),)

    def along_pair(self, block):
        return (swap(block, CORES),)

    def along_depth(self, *blocks):
        return tuple(
            swap(block, CORES * PAIR, self.depth, k) for k, block in enumerate(blocks, 1)
        )

    def along_core(self, block):
        return (swap(block, 1),)

    def by_first(self, kept, came):
        _, wide, _, seq = place_of()
        self.sender = self.along_pair if self.first == "seq" else self.along_seq
        kept = kept.astype(jnp.float32) + came.astype(jnp.float32)
        kept = kept.reshape(self.depth, 2, self.rows, -1)
        which = wide if self.first == "seq" else seq
        return tuple(
            lax.dynamic_index_in_dim(kept, i, 1, keepdims=False).astype(jnp.bfloat16)
            for i in (which, 1 - which)
        )

    def by_second(self, kept, came):
        deep, _, _, _ = place_of()
        self.sender = self.along_depth
        kept = kept.astype(jnp.float32) + came.astype(jnp.float32)
        return tuple(
            lax.dynamic_index_in_dim(kept, deep ^ k, 0, keepdims=False).astype(jnp.bfloat16)
            for k in range(self.depth)
        )

    def by_depth(self, kept, *came):
        total = kept.astype(jnp.float32)
        for block in came:
            total = total + block.astype(jnp.float32)
        self.sender = self.along_seq
        total = narrow(total)
        return total, total

    def by_seq(self, mine, came):
        _, _, core, seq = place_of()
        same = seq == core
        self.sender = self.along_core
        return jnp.where(same, mine, came), jnp.where(same, came, mine)

    def finish(self, mine, came):
        _, _, core, _ = place_of()
        self.fast = False
        low = jnp.where(core == 0, mine, came).astype(jnp.float32)
        high = jnp.where(core == 0, came, mine).astype(jnp.float32)
        results, start = [], 0
        for width in self.widths:
            cols = slice(start, start + width)
            results.append(jnp.concatenate([low[:, cols], high[:, cols]], axis=1))
            start += width
        if self.extra is not None:
            results.append(mine[:, start:].astype(jnp.float32))
        return tuple(results)


def advance(works, values=(), after=()):
    for work in works:
        work.step()
    states = [work.state for work in works]
    heads = [work.state[0] for work in after]
    states, heads, values = lax.optimization_barrier((states, heads, values))
    for work, state in zip(works, states):
        work.state = work.launch(*state)
    for work, head in zip(after, heads):
        work.state = (head, *work.state[1:])
    return values


def body(
    hidden,
    encoder,
    cotangent,
    token_offsets,
    token_lengths,
    frame_counts,
    corpus_ids,
    corpus_weights,
    norm_gains,
    norm_shifts,
    self_in,
    self_out,
    cross_query,
    cross_kv,
    cross_out,
    proj_bias,
    up_weight,
    up_bias,
    down_weight,
):
    hidden, cotangent = hidden[0], cotangent[0]
    row_count, model_width = hidden.shape
    shard_rows = norm_gains.shape[0]
    wide_cols = up_weight.shape[1]
    blocks = wide_cols // model_width
    size = lax.axis_size("batch")

    tail_width = 2 * LANES
    far = lambda block: swap(block, 1)
    small = jnp.concatenate(
        [norm_gains, norm_shifts, proj_bias, up_bias.reshape(shard_rows, blocks)], axis=1
    )
    small_cols = small.shape[1]
    small = jnp.pad(small, ((0, 0), (0, tail_width - small_cols)))
    first = Gather(jnp.concatenate([self_in, small], axis=1), "seq")
    second = Gather(jnp.concatenate([self_out, cross_query, cross_kv, cross_out], axis=1), "pair")
    up_blocks = up_weight.reshape(shard_rows, blocks, model_width).transpose(1, 0, 2)
    third = jnp.concatenate([up_blocks.reshape(-1, model_width), down_weight], axis=1)
    hidden_other = swap_seq(hidden)
    first.step()
    second.state, encoder, first.state, hidden_other = lax.optimization_barrier(
        (second.state, encoder, first.state, hidden_other)
    )
    frame_mine = lax.all_to_all(encoder, "batch", split_axis=0, concat_axis=0, tiled=True)
    frame_mine = frame_mine.reshape(-1, model_width)
    first.step()
    second.step()
    first.state, second.state, third = lax.optimization_barrier(
        (first.state, second.state, third)
    )
    first.step()
    second.step()
    third_all = lax.all_gather(third, "batch", axis=0, tiled=True)
    first_all = first.result()

    self_in_all = first_all[:, : 3 * model_width]
    small_all = first_all[:, 3 * model_width : 3 * model_width + small_cols]
    gains = small_all[:, :4].astype(jnp.float32)
    shifts = small_all[:, 4:8].astype(jnp.float32)
    biases = small_all[:, 8:15].astype(jnp.float32)
    up_bias_all = small_all[:, 15:].reshape(-1).astype(jnp.float32)

    offset, length, frame_count = token_offsets[0], token_lengths[0], frame_counts[0]
    seq_index = lax.axis_index("seq")
    slots = jnp.arange(row_count, dtype=jnp.int32)
    positions = seq_index * row_count + slots
    positions_other = (1 - seq_index) * row_count + slots
    zero_row = jnp.zeros((model_width,), jnp.float32)
    inputs = hidden.astype(jnp.float32)
    normed_one, scale_one = layer_parts(inputs)
    act_one = (normed_one * gains[:, 0] + shifts[:, 0]).astype(jnp.bfloat16)
    normed_far, _ = layer_parts(hidden_other.astype(jnp.float32))
    act_far = (normed_far * gains[:, 0] + shifts[:, 0]).astype(jnp.bfloat16)
    qkv_bias = jnp.concatenate([biases[:, 0], zero_row, biases[:, 1]])
    qkv_local = (dot_right(act_one, self_in_all) + qkv_bias).astype(jnp.bfloat16)
    self_query = qkv_local[:, :model_width]
    pair_far = (
        dot_right(act_far, self_in_all[:, model_width:]) + qkv_bias[model_width:]
    ).astype(jnp.bfloat16)
    self_pairs = jnp.concatenate([pair_far, qkv_local[:, model_width:]], axis=0)
    key_pos = jnp.concatenate([positions_other, positions])[:, None]
    query_pos = positions[None, :]
    self_mask = (key_pos <= query_pos) & ((key_pos >= offset) | (key_pos == query_pos))
    self_bias = jnp.where(self_mask, 0.0, -jnp.inf)
    self_query, self_pairs, second.state, frame_mine = lax.optimization_barrier(
        (self_query, self_pairs, second.state, frame_mine)
    )
    frame_other = swap_seq(frame_mine)
    second.step()
    self_mixed, self_total = attend(self_query, self_pairs, self_bias)
    self_mixed, second.state, frame_other = lax.optimization_barrier(
        (self_mixed, second.state, frame_other)
    )
    second_all = second.result()
    self_out_all = second_all[:, :model_width]
    query_all = second_all[:, model_width : 2 * model_width]
    kv_all = second_all[:, 2 * model_width : 4 * model_width]
    cross_out_all = second_all[:, 4 * model_width :]
    after_self = inputs + dot_right(self_mixed, self_out_all) + biases[:, 2]
    normed_two, scale_two = layer_parts(after_self)
    act_two = (normed_two * gains[:, 1] + shifts[:, 1]).astype(jnp.bfloat16)
    cross_queries = (dot_right(act_two, query_all) + biases[:, 3]).astype(jnp.bfloat16)
    frames = jnp.concatenate([frame_mine, frame_other], axis=0)
    kv_bias = jnp.concatenate([zero_row, biases[:, 4]])
    cross_pairs = (dot_right(frames, kv_all) + kv_bias).astype(jnp.bfloat16)
    half_slots = frame_mine.shape[0]
    owner_frames = encoder.shape[1]
    gathered = jnp.arange(2 * half_slots, dtype=jnp.int32)
    half_index = (gathered // half_slots) ^ seq_index
    within = gathered % half_slots
    frame_ids = (within // owner_frames * 2 + half_index) * owner_frames + within % owner_frames
    frame_bias = jnp.broadcast_to(
        jnp.where(frame_ids < frame_count, 0.0, -jnp.inf)[:, None], (2 * half_slots, row_count)
    )
    cross_mixed, cross_total = attend(cross_queries, cross_pairs, frame_bias)
    after_cross = after_self + dot_right(cross_mixed, cross_out_all) + biases[:, 5]
    normed_three, scale_three = layer_parts(after_cross)
    act_three = (normed_three * gains[:, 2] + shifts[:, 2]).astype(jnp.bfloat16)
    corpus_match = corpus_ids[0] == jnp.arange(corpus_weights.shape[0], dtype=jnp.int32)
    seq_weight = jnp.sum(jnp.where(corpus_match, corpus_weights, 0.0))
    live_rows = (positions >= offset) & (positions < offset + length)
    live_weight = jnp.where(live_rows, seq_weight, 0.0)[:, None]
    if splits(shard_rows):
        result, grad_cross, norm_sums, up_sums, wide_term = feed_forward(
            act_three,
            after_cross,
            cotangent,
            live_weight,
            gains[:, 2:].T,
            shifts[:, 3:].T,
            biases[:, 6:].T,
            up_bias_all.reshape(blocks, 1, model_width),
            third_all,
            size,
        )
        gain_three, shift_three, gain_last, shift_last, down_bias = list(norm_sums[:5])
        up_bias_sum = up_sums.reshape(-1)
    else:
        down_all = third_all[:, model_width:]
        up_all = (
            third_all[:, :model_width]
            .reshape(size, blocks, shard_rows, model_width)
            .transpose(0, 2, 1, 3)
            .reshape(model_width, wide_cols)
        )
        up_value = dot_right(act_three, up_all) + up_bias_all
        gelu_value, gelu_pull = jax.vjp(partial(jax.nn.gelu, approximate=False), up_value)
        hidden_act = gelu_value.astype(jnp.bfloat16)
        after_mlp = after_cross + dot_right(hidden_act, down_all) + biases[:, 6]
        normed_last, scale_last = layer_parts(after_mlp)
        result = (normed_last * gains[:, 3] + shifts[:, 3]).astype(jnp.bfloat16)
        grad_out = cotangent.astype(jnp.float32) * live_weight
        grad_mlp, gain_last, shift_last = layer_back(grad_out, normed_last, scale_last, gains[:, 3])
        grad_down = grad_mlp.astype(jnp.bfloat16)
        down_bias = col_sum(grad_down)
        grad_act = dot_left(grad_down, down_all)
        grad_up = gelu_pull(grad_act)[0].astype(jnp.bfloat16)
        up_bias_sum = col_sum(grad_up)
        wide_term = jnp.concatenate(
            [weight_term(hidden_act, grad_down).reshape(size, -1, model_width)]
            + [
                weight_term(act_three, part).reshape(size, shard_rows, model_width)
                for part in jnp.split(grad_up, blocks, axis=1)
            ],
            axis=1,
        )
        back_three, gain_three, shift_three = layer_back(
            dot_left(grad_up, up_all), normed_three, scale_three, gains[:, 2]
        )
        grad_cross = grad_mlp + back_three
    up_bias_columns = jnp.pad(
        up_bias_sum.astype(jnp.bfloat16).reshape(model_width, blocks),
        ((0, 0), (small_cols - blocks, LANES - small_cols)),
    )
    wide_term, grad_cross = lax.optimization_barrier((wide_term, grad_cross))
    wide_sum = lax.psum_scatter(wide_term, "batch", scatter_dimension=0, tiled=True)[0]
    grad_cross_in = grad_cross.astype(jnp.bfloat16)
    cross_out_bias = col_sum(grad_cross_in)
    grad_cross_mixed = dot_left(grad_cross_in, cross_out_all).astype(jnp.bfloat16)
    grad_cq, grad_frame_pairs = attend_back(
        cross_queries, cross_pairs, frame_bias, cross_total, grad_cross_mixed
    )
    frame_grads = dot_left(grad_frame_pairs[0], kv_all[:, :model_width]) + dot_left(
        grad_frame_pairs[1], kv_all[:, model_width:]
    )
    frame_grads = frame_grads.astype(jnp.bfloat16)
    grad_cq, frame_kept, frame_sent = lax.optimization_barrier(
        (grad_cq, frame_grads[:half_slots], frame_grads[half_slots:])
    )
    frame_came = swap_seq(frame_sent)
    kv_bias_term = col_sum(grad_cross_mixed)
    query_bias = col_sum(grad_cq)
    back_two, gain_two, shift_two = layer_back(
        dot_left(grad_cq, query_all), normed_two, scale_two, gains[:, 1]
    )
    grad_self = grad_cross + back_two
    grad_self_in = grad_self.astype(jnp.bfloat16)
    self_out_bias = col_sum(grad_self_in)
    grad_self_mixed = dot_left(grad_self_in, self_out_all).astype(jnp.bfloat16)
    cross_sum = Reduction(
        [
            (frames, far(frames), grad_frame_pairs),
            (cross_mixed, far(cross_mixed), grad_cross_in),
            (act_two, far(act_two), grad_cq),
            (self_mixed, far(self_mixed), grad_self_in),
        ],
        "seq",
    )
    grad_self_mixed = advance([cross_sum], grad_self_mixed)
    grad_self_query, grad_self_pairs = attend_back(
        self_query, self_pairs, self_bias, self_total, grad_self_mixed
    )
    both_acts = jnp.concatenate([act_far, act_one], axis=0)
    self_pair_sum = Reduction([(both_acts, far(both_acts), grad_self_pairs)], "pair")
    grad_self_query, grad_self_pairs = advance(
        [self_pair_sum], (grad_self_query, grad_self_pairs)
    )
    value_sums = col_sum(grad_self_mixed)
    norm_side, norm_far, small_term = self_tail(
        grad_self_query,
        grad_self_pairs,
        first_all,
        normed_one,
        normed_far,
        [
            value_sums,
            self_out_bias,
            query_bias,
            kv_bias_term,
            cross_out_bias,
            down_bias,
            gain_two,
            gain_three,
            gain_last,
            shift_two,
            shift_three,
            shift_last,
        ],
        up_bias_columns,
    )
    self_sum = Reduction([(act_one, far(act_one), grad_self_query)], "seq", small_term)
    owner_grads = frame_kept.astype(jnp.float32) + frame_came.astype(jnp.float32)
    norm_far, owner_grads = advance([self_sum], (norm_far, owner_grads.astype(jnp.bfloat16)))
    norm_came = swap_seq(norm_far)
    grad_encoder = lax.all_to_all(
        owner_grads.reshape(size, owner_frames, model_width),
        "batch",
        split_axis=0,
        concat_axis=0,
        tiled=True,
    )
    advance([cross_sum, self_pair_sum], after=[self_sum])
    advance([self_sum], after=[cross_sum, self_pair_sum])
    norm_came = advance([cross_sum, self_pair_sum], norm_came, after=[self_sum])
    grad_encoder, wide_sum = advance(
        [self_sum], (grad_encoder, wide_sum), after=[cross_sum, self_pair_sum]
    )
    grad_encoder = grad_encoder.astype(jnp.float32)
    back_one, _, _ = layer_back(
        norm_side + norm_came.astype(jnp.float32), normed_one, scale_one, gains[:, 0]
    )
    grad_hidden = grad_self + back_one
    wide_sum = wide_sum.astype(jnp.float32) + swap_seq(wide_sum).astype(jnp.float32)
    inner_rows = down_weight.shape[0]
    grad_up_weight = (
        wide_sum[inner_rows:]
        .reshape(blocks, shard_rows, model_width)
        .transpose(1, 0, 2)
        .reshape(shard_rows, wide_cols)
    )
    grad_cross_kv, grad_cross_out, grad_cross_query, grad_self_out = cross_sum.result()
    grad_self_keys = self_pair_sum.result()[0]
    grad_self_queries, small_sum = self_sum.result()
    return (
        result[None],
        grad_hidden[None],
        grad_encoder,
        jnp.concatenate([small_sum[:, :1], small_sum[:, 9:12]], axis=1),
        jnp.concatenate([small_sum[:, 1:2], small_sum[:, 12:15]], axis=1),
        jnp.concatenate([grad_self_queries, grad_self_keys], axis=1),
        grad_self_out,
        grad_cross_query,
        grad_cross_kv,
        grad_cross_out,
        small_sum[:, 2:9],
        grad_up_weight,
        small_sum[:, 15:small_cols].reshape(-1),
        wide_sum[:inner_rows],
    )


def solution(mesh):
    in_specs = (
        P("batch", "seq", None),
        P(None, ("batch", "seq"), None),
        P("batch", "seq", None),
        P("batch"),
        P("batch"),
        P("batch"),
        P("batch"),
        P(),
        P("batch", None),
        P("batch", None),
        P("batch", None),
        P("batch", None),
        P("batch", None),
        P("batch", None),
        P("batch", None),
        P("batch", None),
        P("batch", None),
        P("batch"),
        P("batch", None),
    )
    out_specs = (
        P("batch", "seq", None),
        P("batch", "seq", None),
        P(None, ("batch", "seq"), None),
        P("batch", None),
        P("batch", None),
        P("batch", None),
        P("batch", None),
        P("batch", None),
        P("batch", None),
        P("batch", None),
        P("batch", None),
        P("batch", None),
        P("batch"),
        P("batch", None),
    )
    return jax.shard_map(body, mesh=mesh, in_specs=in_specs, out_specs=out_specs, check_vma=False)
```

```python
from functools import partial

import math

import jax
import jax.numpy as jnp
from jax import lax
from jax.experimental import pallas as pl
from jax.experimental.pallas import tpu as pltpu
from jax.sharding import PartitionSpec as P

HEAD_DIM = 64
LANES = 128


EPS = 1e-05

def layer_parts(values):
    center = values - jnp.mean(values, axis=-1, keepdims=True)
    inv_std = lax.rsqrt(jnp.mean(center * center, axis=-1, keepdims=True) + EPS)
    return (center * inv_std, inv_std)


def layer_back(grad_side, normed, inv_std, gain):
    scaled = grad_side * gain
    mean_one = jnp.mean(scaled, axis=-1, keepdims=True)
    mean_two = jnp.mean(scaled * normed, axis=-1, keepdims=True)
    grad_in = inv_std * (scaled - mean_one - normed * mean_two)
    return (grad_in, jnp.sum(grad_side * normed, axis=0), jnp.sum(grad_side, axis=0))


def dot_right(left_side, weight):
    return jnp.dot(left_side, weight, preferred_element_type=jnp.float32)


def dot_left(grad_side, weight):
    return jnp.einsum("cj,ij->ci", grad_side, weight, preferred_element_type=jnp.float32)


def weight_term(left_side, grad_side):
    return jnp.einsum(
        "ci,cj->ij", left_side, grad_side, preferred_element_type=jnp.float32
    ).astype(jnp.bfloat16)


def col_sum(grad_side):
    return jnp.sum(grad_side, axis=0, dtype=jnp.float32)


def hold(steps, values):
    return lax.optimization_barrier((steps, values))

ROWS_BY_LANES = (((1,), (1,)), ((), ()))
DOWN_BOTH = (((0,), (0,)), ((), ()))
ROWS_BY_ROWS = (((1,), (0,)), ((), ()))


def head_parts(block):
    lane = lax.broadcasted_iota(jnp.int32, block.shape, 1)
    zero = jnp.zeros_like(block)
    return (
        jnp.where(lane < HEAD_DIM, block, zero),
        jnp.where(lane < HEAD_DIM, zero, block),
    )


def dot_of(left, right, dims):
    return lax.dot_general(left, right, dims, preferred_element_type=jnp.float32)


def attend_kernel(query_ref, key_ref, value_ref, bias_ref, mixed_ref, total_ref):
    score_scale = HEAD_DIM ** (-0.5)
    key, value = key_ref[...], value_ref[...]
    queries = head_parts(query_ref[...] * jnp.bfloat16(score_scale))
    scores = [dot_of(key, query, ROWS_BY_LANES) + bias_ref[...] for query in queries]
    tops = [jnp.max(item, axis=0, keepdims=True) for item in scores]
    terms = [jnp.exp(item - top) for item, top in zip(scores, tops)]
    totals = [jnp.sum(item, axis=0, keepdims=True) for item in terms]
    sides = [dot_of(value, item.astype(jnp.bfloat16), DOWN_BOTH) for item in terms]
    for head in range(2):
        total_ref[0, head : head + 1, :] = tops[head] + jnp.log(totals[head])
    mixed = [
        sides[head][head * HEAD_DIM : (head + 1) * HEAD_DIM] / totals[head] for head in range(2)
    ]
    mixed_ref[...] = jnp.concatenate(mixed, axis=0).T.astype(jnp.bfloat16)


def attend_back_kernel(
    core_ref,
    query_ref,
    key_ref,
    value_ref,
    bias_ref,
    total_ref,
    grad_ref,
    gq_ref,
    kept_ref,
    sent_ref,
):
    score_scale = HEAD_DIM ** (-0.5)
    key, value = key_ref[...], value_ref[...]
    queries = head_parts(query_ref[...] * jnp.bfloat16(score_scale))
    grads = head_parts(grad_ref[...])
    scores = [dot_of(key, query, ROWS_BY_LANES) + bias_ref[...] for query in queries]
    terms = [
        jnp.exp(item - total_ref[0, head : head + 1, :]) for head, item in enumerate(scores)
    ]
    grad_terms = [
        item * dot_of(value, grad, ROWS_BY_LANES) for item, grad in zip(terms, grads)
    ]
    row_dots = [jnp.sum(item, axis=0, keepdims=True) for item in grad_terms]
    grad_scores = [
        (grad_term - term * row_dot).astype(jnp.bfloat16)
        for grad_term, term, row_dot in zip(grad_terms, terms, row_dots)
    ]
    values = [
        jnp.dot(item.astype(jnp.bfloat16), grad, preferred_element_type=jnp.float32)
        for item, grad in zip(terms, grads)
    ]
    keys = [
        jnp.dot(item, query, preferred_element_type=jnp.float32)
        for item, query in zip(grad_scores, queries)
    ]
    sides = [dot_of(key, item, DOWN_BOTH) for item in grad_scores]
    grad_key = (keys[0] + keys[1]).astype(jnp.bfloat16)
    grad_value = (values[0] + values[1]).astype(jnp.bfloat16)

    @pl.when(core_ref[0] == 0)
    def _():
        kept_ref[...] = grad_key
        sent_ref[...] = grad_value

    @pl.when(core_ref[0] == 1)
    def _():
        kept_ref[...] = grad_value
        sent_ref[...] = grad_key

    picked = [
        sides[head][head * HEAD_DIM : (head + 1) * HEAD_DIM] * score_scale for head in range(2)
    ]
    gq_ref[...] = jnp.concatenate(picked, axis=0).T.astype(jnp.bfloat16)


def head_specs(rows, keys, blocks):
    return [
        pl.BlockSpec((rows, LANES), lambda i: (0, i)),
        pl.BlockSpec((keys, LANES), lambda i: (0, i)),
        pl.BlockSpec((keys, LANES), lambda i: (0, i + blocks)),
        pl.BlockSpec((keys, rows), lambda i: (0, 0)),
    ]


def attend(queries, pairs, bias):
    rows, width = queries.shape
    keys = pairs.shape[0]
    blocks = width // LANES
    return pl.pallas_call(
        attend_kernel,
        grid=(blocks,),
        out_shape=(
            jax.ShapeDtypeStruct((rows, width), jnp.bfloat16),
            jax.ShapeDtypeStruct((blocks, 2, rows), jnp.float32),
        ),
        in_specs=head_specs(rows, keys, blocks),
        out_specs=(
            pl.BlockSpec((rows, LANES), lambda i: (0, i)),
            pl.BlockSpec((1, 2, rows), lambda i: (i, 0, 0)),
        ),
        cost_estimate=pl.CostEstimate(flops=0, transcendentals=0, bytes_accessed=0),
        name="attend",
    )(queries, pairs, pairs, bias)


def attend_back(core, queries, pairs, bias, totals, grads):
    rows, width = queries.shape
    keys = pairs.shape[0]
    blocks = width // LANES
    return pl.pallas_call(
        attend_back_kernel,
        grid=(blocks,),
        out_shape=(
            jax.ShapeDtypeStruct((rows, width), jnp.bfloat16),
            jax.ShapeDtypeStruct((keys, width), jnp.bfloat16),
            jax.ShapeDtypeStruct((keys, width), jnp.bfloat16),
        ),
        in_specs=[pl.BlockSpec(memory_space=pltpu.SMEM)]
        + head_specs(rows, keys, blocks)
        + [
            pl.BlockSpec((1, 2, rows), lambda i: (i, 0, 0)),
            pl.BlockSpec((rows, LANES), lambda i: (0, i)),
        ],
        out_specs=(
            pl.BlockSpec((rows, LANES), lambda i: (0, i)),
            pl.BlockSpec((keys, LANES), lambda i: (0, i)),
            pl.BlockSpec((keys, LANES), lambda i: (0, i)),
        ),
        cost_estimate=pl.CostEstimate(flops=0, transcendentals=0, bytes_accessed=0),
        name="attend_back",
    )(core.reshape(1), queries, pairs, pairs, bias, totals, grads)


CORES = 2
PAIR = 2
FLIP = [(0, 1), (1, 0)]


def partners(stride, radix, step):
    pairs = []
    for i in range(lax.axis_size("batch")):
        digit = i // stride % radix
        pairs.append((i, i + ((digit ^ step) - digit) * stride))
    return pairs


def swap(block, stride, radix=2, step=1):
    return lax.ppermute(block, "batch", partners(stride, radix, step))


def swap_seq(block):
    return lax.ppermute(block, "seq", FLIP)


def place_of():
    batch = lax.axis_index("batch")
    return (
        batch // (CORES * PAIR),
        batch // CORES % PAIR,
        batch % CORES,
        lax.axis_index("seq"),
    )


def splits(rows):
    depth = lax.axis_size("batch") // (CORES * PAIR)
    return rows % 48 == 0 and depth == 4 and lax.axis_size("seq") == 2


def place_kernel(where_ref, *refs, depth, rows, half):
    pieces, out_ref, sem = refs[:8], refs[8], refs[9]
    deep, wide, core, seq = where_ref[0], where_ref[1], where_ref[2], where_ref[3]
    started = []
    for c in range(2):
        column, across, side, side_across = pieces[4 * c : 4 * c + 4]
        for w, (near, far) in enumerate(((column, side), (across, side_across))):
            for k in range(depth):
                base = (((deep ^ k) * PAIR + (wide ^ w)) * CORES + (core ^ c)) * rows
                row_span = pl.ds(pl.multiple_of(base, 16), rows)
                for source, part in ((near, seq), (far, 1 - seq)):
                    col_span = pl.ds(pl.multiple_of(part * half, LANES), half)
                    copy = pltpu.make_async_copy(
                        source.at[k], out_ref.at[row_span, col_span], sem
                    )
                    copy.start()
                    started.append(copy)
    for copy in started:
        copy.wait()


class Gather:
    def __init__(self, shard, last):
        self.rows, self.cols = shard.shape
        self.half = self.cols // 2
        self.last = last
        self.depth = lax.axis_size("batch") // (CORES * PAIR)
        self.state = (shard,)
        self.todo = (
            [self.by_depth, self.by_both, self.by_last, self.place]
            if splits(self.rows)
            else [self.plain]
        )

    def step(self):
        if self.todo:
            self.state = self.todo.pop(0)(*self.state)
        return self

    def result(self):
        while self.todo:
            self.step()
        return self.state[0]

    def plain(self, shard):
        return (lax.all_gather(shard, "batch", axis=0, tiled=True),)

    def by_depth(self, shard):
        part = lax.dynamic_slice_in_dim(shard, lax.axis_index("seq") * self.half, self.half, 1)
        came = [swap(part, CORES * PAIR, self.depth, k) for k in range(1, self.depth)]
        return (jnp.stack([part] + came),)

    def by_both(self, column):
        return column, swap(column, CORES), swap_seq(column)

    def by_last(self, column, across, side):
        far = swap_seq(across) if self.last == "seq" else swap(side, CORES)
        return column, across, side, far

    def place(self, *mine):
        other = tuple(swap(piece, 1) for piece in mine)
        total = lax.axis_size("batch") * self.rows
        call = pl.pallas_call(
            partial(place_kernel, depth=self.depth, rows=self.rows, half=self.half),
            out_shape=jax.ShapeDtypeStruct((total, self.cols), mine[0].dtype),
            in_specs=[pl.BlockSpec(memory_space=pltpu.SMEM)]
            + [pl.BlockSpec(memory_space=pl.ANY)] * 8,
            out_specs=pl.BlockSpec(memory_space=pltpu.VMEM),
            scratch_shapes=[pltpu.SemaphoreType.DMA],
            cost_estimate=pl.CostEstimate(flops=0, transcendentals=0, bytes_accessed=0),
            name="place_rows",
        )
        return (call(jnp.stack(place_of()).astype(jnp.int32), *mine, *other),)


def narrow(values):
    return lax.reduce_precision(values, 8, 7).astype(jnp.bfloat16)


def grad_kernel(where_ref, *refs, parts, split, first, rows, blend):
    terms = []
    for count in parts:
        terms.append((refs[:count], refs[count : 2 * count], *refs[2 * count : 2 * count + 2]))
        refs = refs[2 * count + 2 :]
    extras, (kept_ref, sent_ref, total_ref) = refs[:blend], refs[blend:]
    wide, core, seq = where_ref[1], where_ref[2], where_ref[3]
    height = total_ref.shape[0]
    groups = CORES * kept_ref.shape[0] * rows // height

    def group_step(group, carry):
        start = 0
        for (lefts, far_lefts, right_ref, far_right_ref), whole in zip(terms, split):
            width = far_right_ref.shape[1]
            span = pl.ds(pl.multiple_of(group * height, LANES), height)
            if whole:
                picked = slice(None)
            else:
                picked = pl.ds(pl.multiple_of(core * width, LANES), width)
            total, at = 0.0, 0
            for left_ref, far_left_ref in zip(lefts, far_lefts):
                tokens = slice(at, at + left_ref.shape[0])
                at += left_ref.shape[0]
                total = total + dot_of(left_ref[:, span], right_ref[tokens, picked], DOWN_BOTH)
                total = total + dot_of(
                    far_left_ref[:, span], far_right_ref[tokens, :], DOWN_BOTH
                )
            total_ref[:, :width] = total
            cols = slice(start, start + width)
            for place, near, far in routes(group, height, first, rows, wide, seq):
                for out_ref, base in ((kept_ref, near), (sent_ref, far)):
                    picked = total_ref[pl.ds(pl.multiple_of(base, 16), rows), :width]
                    out_ref[place, :, cols] = picked.astype(jnp.bfloat16)
            start += width
        if blend:
            cols = slice(start, start + LANES)
            for place, near, far in routes(group, height, first, rows, wide, seq):
                for out_ref, base in ((kept_ref, near), (sent_ref, far)):
                    picked = pl.ds(pl.multiple_of(group * height + base, 16), rows)
                    out_ref[place, :, cols] = (
                        extras[0][picked, :].astype(jnp.float32)
                        + extras[1][picked, :].astype(jnp.float32)
                    ).astype(jnp.bfloat16)
        return carry

    lax.fori_loop(0, groups, group_step, 0)


def routes(group, height, first, rows, wide, seq):
    if first == "seq":
        pairs = height // (2 * rows)
        return [
            (group * pairs + i, (2 * i + seq) * rows, (2 * i + 1 - seq) * rows)
            for i in range(pairs)
        ]
    quads = height // (4 * rows)
    return [
        (
            (group * quads + i) * 2 + j,
            (4 * i + 2 * wide + j) * rows,
            (4 * i + 2 * (1 - wide) + j) * rows,
        )
        for i in range(quads)
        for j in range(2)
    ]


def back_by_norm(grad_side, normed, inv_std, gain):
    scaled = grad_side * gain
    mean_one = jnp.mean(scaled, axis=-1, keepdims=True)
    mean_two = jnp.mean(scaled * normed, axis=-1, keepdims=True)
    return inv_std * (scaled - mean_one - normed * mean_two)


def sum_rows(values):
    return jnp.sum(values, axis=0, keepdims=True)


def feed_forward_kernel(
    act_ref,
    after_ref,
    grad_ref,
    live_ref,
    gain_ref,
    shift_ref,
    bias_ref,
    up_bias_ref,
    out_weight_ref,
    weight_ref,
    result_ref,
    cross_ref,
    cross_in_ref,
    mixed_ref,
    sums_ref,
    up_sums_ref,
    wide_ref,
    up_ref,
    down_ref,
    hidden_ref,
    slope_ref,
    side_ref,
    term_ref,
    project_ref,
    in_sem,
    out_sem,
):
    blocks, width, _ = up_ref.shape
    project = pltpu.make_async_copy(
        out_weight_ref.at[:, pl.ds(out_weight_ref.shape[1] - width, width)],
        project_ref,
        in_sem.at[2 * blocks],
    )
    size = wide_ref.shape[0]
    piece = width // size
    inner = blocks * piece
    per = size // blocks
    copies = []
    for j in range(blocks):
        for b in range(size):
            copies.append(
                (
                    weight_ref.at[pl.ds(b * inner + j * piece, piece), pl.ds(0, width)],
                    up_ref.at[j, pl.ds(b * piece, piece)],
                    in_sem.at[j],
                )
            )
        copies.append(
            (
                weight_ref.at[pl.ds(j * width, width), pl.ds(width, width)],
                down_ref.at[j],
                in_sem.at[blocks + j],
            )
        )
    started = [pltpu.make_async_copy(*copy) for copy in copies]
    for copy in started:
        copy.start()
    project.start()

    def wait_up(j):
        pltpu.make_async_copy(down_ref.at[j], up_ref.at[j], in_sem.at[j]).wait()

    def wait_down(j):
        pltpu.make_async_copy(up_ref.at[j], down_ref.at[j], in_sem.at[blocks + j]).wait()

    act = act_ref[...]
    half_root, slope_scale = math.sqrt(0.5), 1.0 / math.sqrt(2.0 * math.pi)

    def rise(j, total):
        wait_up(j)
        up = dot_of(act, up_ref[j], (((1,), (0,)), ((), ()))) + up_bias_ref[j]
        level = 0.5 * (1.0 + lax.erf(up * half_root))
        hidden_ref[j] = (up * level).astype(jnp.bfloat16)
        slope_ref[j] = level + up * (slope_scale * jnp.exp(-0.5 * up * up))
        wait_down(j)
        return total + dot_of(hidden_ref[j], down_ref[j], (((1,), (0,)), ((), ())))

    after = after_ref[...]
    mlp = lax.fori_loop(0, blocks, rise, after + bias_ref[...])
    normed, inv_std = layer_parts(mlp)
    result_ref[...] = (normed * gain_ref[1:2] + shift_ref[...]).astype(jnp.bfloat16)
    grad_out = grad_ref[...].astype(jnp.float32) * live_ref[...]
    grad_mlp = back_by_norm(grad_out, normed, inv_std, gain_ref[1:2])
    grad_down = grad_mlp.astype(jnp.bfloat16)

    def fall(j, total):
        grad_act = dot_of(grad_down, down_ref[j], ROWS_BY_LANES)
        grad_up = slope_ref[j] * grad_act
        side_ref[j] = grad_up.astype(jnp.bfloat16)
        up_sums_ref[j] = sum_rows(grad_up)
        return total + dot_of(side_ref[j], up_ref[j], ROWS_BY_LANES)

    grad_three = lax.fori_loop(0, blocks, fall, jnp.zeros_like(mlp))

    def outward(j):
        return (
            pltpu.make_async_copy(
                term_ref.at[pl.ds(j * per, per), pl.ds(0, inner)],
                wide_ref.at[pl.ds(j * per, per), pl.ds(0, inner)],
                out_sem.at[j],
            ),
            pltpu.make_async_copy(
                term_ref.at[:, pl.ds(pl.multiple_of(inner + j * piece, 16), piece)],
                wide_ref.at[:, pl.ds(pl.multiple_of(inner + j * piece, 16), piece)],
                out_sem.at[blocks + j],
            ),
        )

    def weigh(j, carry):
        down = dot_of(hidden_ref[j], grad_down, DOWN_BOTH).astype(jnp.bfloat16)
        for t in range(per):
            term_ref[j * per + t, :inner] = down[t * inner : (t + 1) * inner]
        up = dot_of(act, side_ref[j], DOWN_BOTH).astype(jnp.bfloat16)
        span = pl.ds(pl.multiple_of(inner + j * piece, 16), piece)
        for b in range(size):
            term_ref[b, span] = up[b * piece : (b + 1) * piece]
        for copy in outward(j):
            copy.start()
        return carry

    lax.fori_loop(0, blocks, weigh, 0)
    normed_three, scale_three = layer_parts(after)
    grad_cross = grad_mlp + back_by_norm(grad_three, normed_three, scale_three, gain_ref[0:1])
    cross_ref[...] = grad_cross
    grad_cross_in = grad_cross.astype(jnp.bfloat16)
    cross_in_ref[...] = grad_cross_in
    project.wait()
    grad_mixed = dot_of(grad_cross_in, project_ref[...], ROWS_BY_LANES).astype(jnp.bfloat16)
    mixed_ref[...] = grad_mixed
    rows = [
        grad_three * normed_three,
        grad_three,
        grad_out * normed,
        grad_out,
        grad_down.astype(jnp.float32),
        grad_cross_in.astype(jnp.float32),
        grad_mixed.astype(jnp.float32),
    ]
    for i, item in enumerate(rows):
        sums_ref[i : i + 1] = sum_rows(item)

    def finish(j, carry):
        for copy in outward(j):
            copy.wait()
        return carry

    lax.fori_loop(0, blocks, finish, 0)


def feed_forward(act, after, grad, live, gains, shift, bias, up_bias, out_weight, weight, size):
    rows, width = act.shape
    blocks = up_bias.shape[0]
    inner = blocks * width // size
    shape = jax.ShapeDtypeStruct
    vmem = pl.BlockSpec(memory_space=pltpu.VMEM)
    return pl.pallas_call(
        feed_forward_kernel,
        out_shape=(
            shape((rows, width), jnp.bfloat16),
            shape((rows, width), jnp.float32),
            shape((rows, width), jnp.bfloat16),
            shape((rows, width), jnp.bfloat16),
            shape((8, width), jnp.float32),
            shape((blocks, 1, width), jnp.float32),
            shape((size, 2 * inner, width), jnp.bfloat16),
        ),
        in_specs=[vmem] * 8 + [pl.BlockSpec(memory_space=pl.ANY)] * 2,
        out_specs=(vmem,) * 6 + (pl.BlockSpec(memory_space=pl.ANY),),
        scratch_shapes=[
            pltpu.VMEM((blocks, width, width), jnp.bfloat16),
            pltpu.VMEM((blocks, width, width), jnp.bfloat16),
            pltpu.VMEM((blocks, rows, width), jnp.bfloat16),
            pltpu.VMEM((blocks, rows, width), jnp.float32),
            pltpu.VMEM((blocks, rows, width), jnp.bfloat16),
            pltpu.VMEM((size, 2 * inner, width), jnp.bfloat16),
            pltpu.VMEM((width, width), jnp.bfloat16),
            pltpu.SemaphoreType.DMA((2 * blocks + 1,)),
            pltpu.SemaphoreType.DMA((2 * blocks,)),
        ],
        cost_estimate=pl.CostEstimate(flops=0, transcendentals=0, bytes_accessed=0),
        name="feed_forward",
    )(act, after, grad, live, gains, shift, bias, up_bias, out_weight, weight)


def frame_pairs_kernel(near_ref, far_ref, weight_ref, bias_ref, pair_ref):
    half = pl.num_programs(0) // 2

    @pl.when(pl.program_id(0) < half)
    def _():
        pair_ref[...] = (
            dot_of(near_ref[...], weight_ref[...], ROWS_BY_ROWS) + bias_ref[...]
        ).astype(jnp.bfloat16)

    @pl.when(pl.program_id(0) >= half)
    def _():
        pair_ref[...] = (
            dot_of(far_ref[...], weight_ref[...], ROWS_BY_ROWS) + bias_ref[...]
        ).astype(jnp.bfloat16)


def frame_pairs(near, far, weight, bias):
    half, width = near.shape
    steps = half // (2 * LANES)
    return pl.pallas_call(
        frame_pairs_kernel,
        grid=(2 * steps,),
        out_shape=jax.ShapeDtypeStruct((2 * half, 2 * width), jnp.bfloat16),
        in_specs=[
            pl.BlockSpec((2 * LANES, width), lambda i: (jnp.minimum(i, steps - 1), 0)),
            pl.BlockSpec((2 * LANES, width), lambda i: (jnp.maximum(i - steps, 0), 0)),
            pl.BlockSpec((width, 2 * width), lambda i: (0, 1)),
            pl.BlockSpec((1, 2 * width), lambda i: (0, 0)),
        ],
        out_specs=pl.BlockSpec((2 * LANES, 2 * width), lambda i: (i, 0)),
        cost_estimate=pl.CostEstimate(flops=0, transcendentals=0, bytes_accessed=0),
        name="frame_pairs",
    )(near, far, weight, bias)


def frame_back_kernel(core_ref, kept_ref, sent_ref, weight_ref, far_weight_ref, near_ref, far_ref):
    half = pl.num_programs(0) // 2
    grad = dot_of(kept_ref[...], weight_ref[...], ROWS_BY_LANES) + dot_of(
        sent_ref[...], far_weight_ref[...], ROWS_BY_LANES
    )

    @pl.when(pl.program_id(0) < half)
    def _():
        near_ref[...] = grad.astype(jnp.bfloat16)

    @pl.when(pl.program_id(0) >= half)
    def _():
        far_ref[...] = grad.astype(jnp.bfloat16)


def frame_back(core, kept, sent, weight):
    keys, width = kept.shape
    steps = keys // (4 * LANES)
    shape = jax.ShapeDtypeStruct((keys // 2, width), jnp.bfloat16)
    return pl.pallas_call(
        frame_back_kernel,
        grid_spec=pltpu.PrefetchScalarGridSpec(
            num_scalar_prefetch=1,
            grid=(2 * steps,),
            in_specs=[
                pl.BlockSpec((2 * LANES, width), lambda i, core: (i, 0)),
                pl.BlockSpec((2 * LANES, width), lambda i, core: (i, 0)),
                pl.BlockSpec((width, width), lambda i, core: (0, 2 + core[0])),
                pl.BlockSpec((width, width), lambda i, core: (0, 3 - core[0])),
            ],
            out_specs=(
                pl.BlockSpec((2 * LANES, width), lambda i, core: (jnp.minimum(i, steps - 1), 0)),
                pl.BlockSpec((2 * LANES, width), lambda i, core: (jnp.maximum(i - steps, 0), 0)),
            ),
        ),
        out_shape=(shape, shape),
        cost_estimate=pl.CostEstimate(flops=0, transcendentals=0, bytes_accessed=0),
        name="frame_back",
    )(core.reshape(1), kept, sent, weight, weight)


def self_head_kernel(
    near_ref, far_ref, gain_ref, shift_ref, bias_ref, weight_ref, act_ref, far_act_ref, query_ref, pair_ref
):
    rows, width = near_ref.shape
    tile = width // 2
    for source_ref, out_ref in ((far_ref, far_act_ref), (near_ref, act_ref)):
        normed, _ = layer_parts(source_ref[...].astype(jnp.float32))
        out_ref[...] = (normed * gain_ref[...] + shift_ref[...]).astype(jnp.bfloat16)

    def project(source_ref, t):
        span = pl.ds(pl.multiple_of(t * tile, LANES), tile)
        return (
            dot_of(source_ref[...], weight_ref[:, span], ROWS_BY_ROWS) + bias_ref[:, span]
        ).astype(jnp.bfloat16)

    def query(t, carry):
        query_ref[:, pl.ds(pl.multiple_of(t * tile, LANES), tile)] = project(act_ref, t)
        return carry

    def pair(t, carry):
        span = pl.ds(pl.multiple_of(t * tile, LANES), tile)
        pair_ref[:rows, span] = project(far_act_ref, t + 2)
        pair_ref[rows:, span] = project(act_ref, t + 2)
        return carry

    lax.fori_loop(0, 2, query, 0)
    lax.fori_loop(0, 4, pair, 0)


def self_head(near, far, gain, shift, bias, weight):
    rows, width = near.shape
    shape = jax.ShapeDtypeStruct((rows, width), jnp.bfloat16)
    return pl.pallas_call(
        self_head_kernel,
        out_shape=(
            shape,
            shape,
            shape,
            jax.ShapeDtypeStruct((2 * rows, 2 * width), jnp.bfloat16),
        ),
        cost_estimate=pl.CostEstimate(flops=0, transcendentals=0, bytes_accessed=0),
        name="self_head",
    )(near, far, gain, shift, bias, weight)


def hidden_back_kernel(side_ref, came_ref, hidden_ref, gain_ref, self_ref, out_ref):
    normed, inv_std = layer_parts(hidden_ref[...].astype(jnp.float32))
    side = side_ref[...] + came_ref[...].astype(jnp.float32)
    out_ref[...] = self_ref[...] + back_by_norm(side, normed, inv_std, gain_ref[...])


def hidden_back(side, came, hidden, gain, grad_self):
    return pl.pallas_call(
        hidden_back_kernel,
        out_shape=jax.ShapeDtypeStruct(side.shape, jnp.float32),
        cost_estimate=pl.CostEstimate(flops=0, transcendentals=0, bytes_accessed=0),
        name="hidden_back",
    )(side, came, hidden, gain, grad_self)


def query_back_kernel(
    grad_ref,
    cross_ref,
    after_ref,
    gain_ref,
    weight_ref,
    self_ref,
    self_in_ref,
    mixed_ref,
    sums_ref,
    held_ref,
    sem,
):
    width = grad_ref.shape[1]
    copies = [
        pltpu.make_async_copy(
            weight_ref.at[:, pl.ds(i * width, width)], held_ref.at[i], sem.at[i]
        )
        for i in (1, 0)
    ]
    for copy in copies:
        copy.start()
    copies[0].wait()
    side = dot_of(grad_ref[...], held_ref[1], ROWS_BY_LANES)
    normed, inv_std = layer_parts(after_ref[...])
    grad_self = cross_ref[...] + back_by_norm(side, normed, inv_std, gain_ref[...])
    self_ref[...] = grad_self
    grad_self_in = grad_self.astype(jnp.bfloat16)
    self_in_ref[...] = grad_self_in
    copies[1].wait()
    grad_mixed = dot_of(grad_self_in, held_ref[0], ROWS_BY_LANES).astype(jnp.bfloat16)
    mixed_ref[...] = grad_mixed
    rows = [
        side * normed,
        side,
        grad_ref[...].astype(jnp.float32),
        grad_self_in.astype(jnp.float32),
        grad_mixed.astype(jnp.float32),
    ]
    for i, item in enumerate(rows):
        sums_ref[i : i + 1] = sum_rows(item)


def query_back(grad, cross, after, gain, weight):
    shape = jax.ShapeDtypeStruct
    rows, width = grad.shape
    return pl.pallas_call(
        query_back_kernel,
        out_shape=(
            shape((rows, width), jnp.float32),
            shape((rows, width), jnp.bfloat16),
            shape((rows, width), jnp.bfloat16),
            shape((8, width), jnp.float32),
        ),
        in_specs=[pl.BlockSpec(memory_space=pltpu.VMEM)] * 4 + [pl.BlockSpec(memory_space=pl.ANY)],
        out_specs=(pl.BlockSpec(memory_space=pltpu.VMEM),) * 4,
        scratch_shapes=[
            pltpu.VMEM((2, width, width), jnp.bfloat16),
            pltpu.SemaphoreType.DMA((2,)),
        ],
        cost_estimate=pl.CostEstimate(flops=0, transcendentals=0, bytes_accessed=0),
        name="query_back",
    )(grad, cross, after, gain, weight)


def self_tail_kernel(
    core_ref,
    query_ref,
    kept_ref,
    sent_ref,
    weight_ref,
    near_ref,
    far_ref,
    query_table_ref,
    table_ref,
    base_ref,
    side_ref,
    moved_ref,
    column_ref,
):
    rows, width = query_ref.shape
    core = core_ref[0]
    near_span = pl.ds(pl.multiple_of((1 + core) * width, LANES), width)
    far_span = pl.ds(pl.multiple_of((2 - core) * width, LANES), width)
    both = dot_of(kept_ref[...], weight_ref[:, near_span], ROWS_BY_LANES) + dot_of(
        sent_ref[...], weight_ref[:, far_span], ROWS_BY_LANES
    )
    far = both[:rows]
    side = both[rows:] + dot_of(query_ref[...], weight_ref[:, :width], ROWS_BY_LANES)
    side_ref[...] = side
    moved_ref[...] = far.astype(jnp.bfloat16)
    normed, _ = layer_parts(near_ref[...].astype(jnp.float32))
    normed_far, _ = layer_parts(far_ref[...].astype(jnp.float32))
    gain_one = sum_rows(side * normed + far * normed_far)
    shift_one = sum_rows(side + far)
    query_bias = sum_rows(query_ref[...].astype(jnp.float32))
    gain_two, shift_two, cross_query, self_out, value = [
        query_table_ref[i : i + 1] for i in range(5)
    ]
    gain_three, shift_three, gain_last, shift_last, down, cross_out, cross_value = [
        table_ref[i : i + 1] for i in range(7)
    ]
    sums = [gain_one, gain_two, gain_three, gain_last]
    sums += [shift_one, shift_two, shift_three, shift_last]
    sums += [query_bias, value, self_out, cross_query, cross_value, cross_out, down]
    lane = lax.broadcasted_iota(jnp.int32, (LANES, LANES), 1)
    blank = jnp.zeros((LANES - len(sums), LANES), jnp.float32)
    for i in range(width // LANES):
        here = slice(i * LANES, (i + 1) * LANES)
        block = jnp.concatenate([item[:, here] for item in sums] + [blank], axis=0)
        column_ref[here, :] = jnp.where(
            lane < len(sums), block.T, base_ref[here, :].astype(jnp.float32)
        ).astype(jnp.bfloat16)


def self_tail(core, query, kept, sent, weight, near, far, query_table, table, base):
    rows, width = query.shape
    return pl.pallas_call(
        self_tail_kernel,
        out_shape=(
            jax.ShapeDtypeStruct((rows, width), jnp.float32),
            jax.ShapeDtypeStruct((rows, width), jnp.bfloat16),
            jax.ShapeDtypeStruct(base.shape, jnp.bfloat16),
        ),
        in_specs=[pl.BlockSpec(memory_space=pltpu.SMEM)]
        + [pl.BlockSpec(memory_space=pltpu.VMEM)] * 9,
        cost_estimate=pl.CostEstimate(flops=0, transcendentals=0, bytes_accessed=0),
        name="self_tail",
    )(core.reshape(1), query, kept, sent, weight, near, far, query_table, table, base)


def half_of(right, which):
    width = right.shape[1] // CORES
    return lax.dynamic_slice_in_dim(right, which * width, width, 1)


class Reduction:
    def __init__(self, terms, first, extra=None):
        self.size = lax.axis_size("batch")
        self.depth = self.size // (CORES * PAIR)
        self.rows = terms[0][0][0].shape[1] // self.size
        self.first = first
        self.terms, self.extra = terms, extra
        self.fast = splits(self.rows)
        self.widths = [
            right[0].shape[1] if isinstance(right, tuple) else right.shape[1] // CORES
            for _, right in terms
        ]
        self.state = ()
        self.todo = (
            [self.begin, self.by_first, self.by_second, self.by_depth, self.by_seq, self.finish]
            if self.fast
            else [self.plain]
        )

    def step(self):
        if self.todo:
            self.state = self.todo.pop(0)(*self.state)
        return self

    def result(self):
        while self.todo:
            self.step()
            self.state = self.launch(*self.state)
        return self.state

    def plain(self):
        _, _, core, _ = place_of()
        whole = [] if self.extra is None else [self.extra]
        for left, right in reversed(self.terms):
            if isinstance(right, tuple):
                kept, sent = right
                right = jnp.concatenate(
                    [jnp.where(core == 0, kept, sent), jnp.where(core == 0, sent, kept)], axis=1
                )
            whole.insert(0, weight_term(jnp.concatenate(left, axis=0), right))
        mine = lax.psum_scatter(
            jnp.concatenate(whole, axis=1), "batch", scatter_dimension=0, tiled=True
        )
        mine = lax.psum(mine, "seq").astype(jnp.float32)
        ends = [0]
        for item in whole:
            ends.append(ends[-1] + item.shape[1])
        return tuple(mine[:, i:j] for i, j in zip(ends, ends[1:]))

    def begin(self):
        self.sender = self.along_seq if self.first == "seq" else self.along_pair
        where = jnp.stack(place_of()).astype(jnp.int32)
        operands = [where]
        for left, right in self.terms:
            if isinstance(right, tuple):
                kept, sent = right
            else:
                kept, sent = right, half_of(right, 1 - where[2])
            operands += [*left, *[swap(part, 1) for part in left], kept, swap(sent, 1)]
        if self.extra is not None:
            operands += [self.extra, swap(self.extra, 1)]
        blend = 0 if self.extra is None else 2
        total = sum(self.widths) + (LANES if blend else 0)
        shape = jax.ShapeDtypeStruct((self.depth * PAIR, self.rows, total), jnp.bfloat16)
        height = 3 * LANES
        return tuple(
            pl.pallas_call(
                partial(
                    grad_kernel,
                    parts=[len(left) for left, _ in self.terms],
                    split=[isinstance(right, tuple) for _, right in self.terms],
                    first=self.first,
                    rows=self.rows,
                    blend=blend,
                ),
                out_shape=(shape, shape),
                in_specs=[pl.BlockSpec(memory_space=pltpu.SMEM)]
                + [pl.BlockSpec(memory_space=pltpu.VMEM)] * (len(operands) - 1),
                out_specs=(pl.BlockSpec(memory_space=pltpu.VMEM),) * 2,
                scratch_shapes=[pltpu.VMEM((height, max(self.widths)), jnp.float32)],
                cost_estimate=pl.CostEstimate(flops=0, transcendentals=0, bytes_accessed=0),
                name="grad_blocks",
            )(*operands)
        )

    def launch(self, kept, *sent):
        if not self.fast:
            return (kept, *sent)
        return (kept, *self.sender(*sent))

    def along_seq(self, block):
        return (swap_seq(block),)

    def along_pair(self, block):
        return (swap(block, CORES),)

    def along_depth(self, *blocks):
        return tuple(
            swap(block, CORES * PAIR, self.depth, k) for k, block in enumerate(blocks, 1)
        )

    def along_core(self, block):
        return (swap(block, 1),)

    def by_first(self, kept, came):
        _, wide, _, seq = place_of()
        self.sender = self.along_pair if self.first == "seq" else self.along_seq
        kept = kept.astype(jnp.float32) + came.astype(jnp.float32)
        kept = kept.reshape(self.depth, 2, self.rows, -1)
        which = wide if self.first == "seq" else seq
        return tuple(
            lax.dynamic_index_in_dim(kept, i, 1, keepdims=False).astype(jnp.bfloat16)
            for i in (which, 1 - which)
        )

    def by_second(self, kept, came):
        deep, _, _, _ = place_of()
        self.sender = self.along_depth
        kept = kept.astype(jnp.float32) + came.astype(jnp.float32)
        return tuple(
            lax.dynamic_index_in_dim(kept, deep ^ k, 0, keepdims=False).astype(jnp.bfloat16)
            for k in range(self.depth)
        )

    def by_depth(self, kept, *came):
        total = kept.astype(jnp.float32)
        for block in came:
            total = total + block.astype(jnp.float32)
        self.sender = self.along_seq
        total = narrow(total)
        return total, total

    def by_seq(self, mine, came):
        _, _, core, seq = place_of()
        same = seq == core
        self.sender = self.along_core
        return jnp.where(same, mine, came), jnp.where(same, came, mine)

    def finish(self, mine, came):
        _, _, core, _ = place_of()
        self.fast = False
        low = jnp.where(core == 0, mine, came).astype(jnp.float32)
        high = jnp.where(core == 0, came, mine).astype(jnp.float32)
        results, start = [], 0
        for width in self.widths:
            cols = slice(start, start + width)
            results.append(jnp.concatenate([low[:, cols], high[:, cols]], axis=1))
            start += width
        if self.extra is not None:
            results.append(mine[:, start:].astype(jnp.float32))
        return tuple(results)


def advance(works, values=(), after=()):
    for work in works:
        work.step()
    states = [work.state for work in works]
    heads = [work.state[0] for work in after]
    states, heads, values = lax.optimization_barrier((states, heads, values))
    for work, state in zip(works, states):
        work.state = work.launch(*state)
    for work, head in zip(after, heads):
        work.state = (head, *work.state[1:])
    return values


def body(
    hidden,
    encoder,
    cotangent,
    token_offsets,
    token_lengths,
    frame_counts,
    corpus_ids,
    corpus_weights,
    norm_gains,
    norm_shifts,
    self_in,
    self_out,
    cross_query,
    cross_kv,
    cross_out,
    proj_bias,
    up_weight,
    up_bias,
    down_weight,
):
    hidden, cotangent = hidden[0], cotangent[0]
    row_count, model_width = hidden.shape
    shard_rows = norm_gains.shape[0]
    wide_cols = up_weight.shape[1]
    blocks = wide_cols // model_width
    size = lax.axis_size("batch")

    tail_width = 2 * LANES
    core = place_of()[2].astype(jnp.int32)
    small = jnp.concatenate(
        [norm_gains, norm_shifts, proj_bias, up_bias.reshape(shard_rows, blocks)], axis=1
    )
    small_cols = small.shape[1]
    small = jnp.pad(small, ((0, 0), (0, tail_width - small_cols)))
    first = Gather(jnp.concatenate([self_in, small], axis=1), "seq")
    second = Gather(jnp.concatenate([self_out, cross_query, cross_kv, cross_out], axis=1), "pair")
    up_blocks = up_weight.reshape(shard_rows, blocks, model_width).transpose(1, 0, 2)
    third = jnp.concatenate([up_blocks.reshape(-1, model_width), down_weight], axis=1)
    hidden_other = swap_seq(hidden)
    first.step()
    second.state, encoder, first.state, hidden_other = lax.optimization_barrier(
        (second.state, encoder, first.state, hidden_other)
    )
    frame_mine = lax.all_to_all(encoder, "batch", split_axis=0, concat_axis=0, tiled=True)
    frame_mine = frame_mine.reshape(-1, model_width)
    first.step()
    second.step()
    first.state, second.state, third = lax.optimization_barrier(
        (first.state, second.state, third)
    )
    first.step()
    second.step()
    third_all = lax.all_gather(third, "batch", axis=0, tiled=True)
    first_all = first.result()

    small_all = first_all[:, 3 * model_width : 3 * model_width + small_cols]
    gains = small_all[:, :4].astype(jnp.float32)
    shifts = small_all[:, 4:8].astype(jnp.float32)
    biases = small_all[:, 8:15].astype(jnp.float32)
    up_bias_all = small_all[:, 15:].reshape(-1).astype(jnp.float32)

    offset, length, frame_count = token_offsets[0], token_lengths[0], frame_counts[0]
    seq_index = lax.axis_index("seq")
    slots = jnp.arange(row_count, dtype=jnp.int32)
    positions = seq_index * row_count + slots
    positions_other = (1 - seq_index) * row_count + slots
    zero_row = jnp.zeros((model_width,), jnp.float32)
    inputs = hidden.astype(jnp.float32)
    qkv_bias = jnp.concatenate([biases[:, 0], zero_row, biases[:, 1]])
    act_one, act_far, self_query, self_pairs = self_head(
        hidden, hidden_other, gains[:, :1].T, shifts[:, :1].T, qkv_bias[None], first_all
    )
    key_pos = jnp.concatenate([positions_other, positions])[:, None]
    query_pos = positions[None, :]
    self_mask = (key_pos <= query_pos) & ((key_pos >= offset) | (key_pos == query_pos))
    self_bias = jnp.where(self_mask, 0.0, -jnp.inf)
    self_query, self_pairs, second.state, frame_mine = lax.optimization_barrier(
        (self_query, self_pairs, second.state, frame_mine)
    )
    frame_other = swap_seq(frame_mine)
    second.step()
    self_mixed, self_total = attend(self_query, self_pairs, self_bias)
    self_mixed, second.state, frame_other = lax.optimization_barrier(
        (self_mixed, second.state, frame_other)
    )
    second_all = second.result()
    self_out_all = second_all[:, :model_width]
    query_all = second_all[:, model_width : 2 * model_width]
    kv_all = second_all[:, 2 * model_width : 4 * model_width]
    cross_out_all = second_all[:, 4 * model_width :]
    after_self = inputs + dot_right(self_mixed, self_out_all) + biases[:, 2]
    normed_two, scale_two = layer_parts(after_self)
    act_two = (normed_two * gains[:, 1] + shifts[:, 1]).astype(jnp.bfloat16)
    cross_queries = (dot_right(act_two, query_all) + biases[:, 3]).astype(jnp.bfloat16)
    kv_bias = jnp.concatenate([zero_row, biases[:, 4]])
    cross_pairs = frame_pairs(frame_mine, frame_other, second_all, kv_bias[None])
    half_slots = frame_mine.shape[0]
    owner_frames = encoder.shape[1]
    gathered = jnp.arange(2 * half_slots, dtype=jnp.int32)
    half_index = (gathered // half_slots) ^ seq_index
    within = gathered % half_slots
    frame_ids = (within // owner_frames * 2 + half_index) * owner_frames + within % owner_frames
    frame_bias = jnp.broadcast_to(
        jnp.where(frame_ids < frame_count, 0.0, -jnp.inf)[:, None], (2 * half_slots, row_count)
    )
    cross_mixed, cross_total = attend(cross_queries, cross_pairs, frame_bias)
    after_cross = after_self + dot_right(cross_mixed, cross_out_all) + biases[:, 5]
    normed_three, scale_three = layer_parts(after_cross)
    act_three = (normed_three * gains[:, 2] + shifts[:, 2]).astype(jnp.bfloat16)
    corpus_match = corpus_ids[0] == jnp.arange(corpus_weights.shape[0], dtype=jnp.int32)
    seq_weight = jnp.sum(jnp.where(corpus_match, corpus_weights, 0.0))
    live_rows = (positions >= offset) & (positions < offset + length)
    live_weight = jnp.where(live_rows, seq_weight, 0.0)[:, None]
    if splits(shard_rows):
        result, grad_cross, grad_cross_in, grad_cross_mixed, table, up_sums, wide_term = feed_forward(
            act_three,
            after_cross,
            cotangent,
            live_weight,
            gains[:, 2:].T,
            shifts[:, 3:].T,
            biases[:, 6:].T,
            up_bias_all.reshape(blocks, 1, model_width),
            second_all,
            third_all,
            size,
        )
        up_bias_sum = up_sums.reshape(-1)
    else:
        down_all = third_all[:, model_width:]
        up_all = (
            third_all[:, :model_width]
            .reshape(size, blocks, shard_rows, model_width)
            .transpose(0, 2, 1, 3)
            .reshape(model_width, wide_cols)
        )
        up_value = dot_right(act_three, up_all) + up_bias_all
        gelu_value, gelu_pull = jax.vjp(partial(jax.nn.gelu, approximate=False), up_value)
        hidden_act = gelu_value.astype(jnp.bfloat16)
        after_mlp = after_cross + dot_right(hidden_act, down_all) + biases[:, 6]
        normed_last, scale_last = layer_parts(after_mlp)
        result = (normed_last * gains[:, 3] + shifts[:, 3]).astype(jnp.bfloat16)
        grad_out = cotangent.astype(jnp.float32) * live_weight
        grad_mlp, gain_last, shift_last = layer_back(grad_out, normed_last, scale_last, gains[:, 3])
        grad_down = grad_mlp.astype(jnp.bfloat16)
        down_bias = col_sum(grad_down)
        grad_act = dot_left(grad_down, down_all)
        grad_up = gelu_pull(grad_act)[0].astype(jnp.bfloat16)
        up_bias_sum = col_sum(grad_up)
        wide_term = jnp.concatenate(
            [weight_term(hidden_act, grad_down).reshape(size, -1, model_width)]
            + [
                weight_term(act_three, part).reshape(size, shard_rows, model_width)
                for part in jnp.split(grad_up, blocks, axis=1)
            ],
            axis=1,
        )
        back_three, gain_three, shift_three = layer_back(
            dot_left(grad_up, up_all), normed_three, scale_three, gains[:, 2]
        )
        grad_cross = grad_mlp + back_three
        grad_cross_in = grad_cross.astype(jnp.bfloat16)
        grad_cross_mixed = dot_left(grad_cross_in, cross_out_all).astype(jnp.bfloat16)
        table = jnp.stack(
            [
                gain_three,
                shift_three,
                gain_last,
                shift_last,
                down_bias,
                col_sum(grad_cross_in),
                col_sum(grad_cross_mixed),
                jnp.zeros_like(down_bias),
            ]
        )
    up_bias_columns = jnp.pad(
        up_bias_sum.astype(jnp.bfloat16).reshape(model_width, blocks),
        ((0, 0), (small_cols - blocks, LANES - small_cols)),
    )
    wide_term, grad_cross_mixed = lax.optimization_barrier((wide_term, grad_cross_mixed))
    wide_sum = lax.psum_scatter(wide_term, "batch", scatter_dimension=0, tiled=True)[0]
    grad_cq, frame_kept, frame_sent = attend_back(
        core, cross_queries, cross_pairs, frame_bias, cross_total, grad_cross_mixed
    )
    frame_near, frame_far = frame_back(core, frame_kept, frame_sent, second_all)
    grad_cq, frame_near, frame_far = lax.optimization_barrier((grad_cq, frame_near, frame_far))
    frame_came = swap_seq(frame_far)
    grad_self, grad_self_in, grad_self_mixed, query_table = query_back(
        grad_cq, grad_cross, after_self, gains[:, 1:2].T, second_all
    )
    cross_sum = Reduction(
        [
            ((frame_mine, frame_other), (frame_kept, frame_sent)),
            ((cross_mixed,), grad_cross_in),
            ((act_two,), grad_cq),
            ((self_mixed,), grad_self_in),
        ],
        "seq",
    )
    grad_self_mixed = advance([cross_sum], grad_self_mixed)
    grad_self_query, self_kept, self_sent = attend_back(
        core, self_query, self_pairs, self_bias, self_total, grad_self_mixed
    )
    self_pair_sum = Reduction([((act_far, act_one), (self_kept, self_sent))], "pair")
    grad_self_query, self_kept, self_sent = advance(
        [self_pair_sum], (grad_self_query, self_kept, self_sent)
    )
    norm_side, norm_far, small_term = self_tail(
        core,
        grad_self_query,
        self_kept,
        self_sent,
        first_all,
        hidden,
        hidden_other,
        query_table,
        table,
        up_bias_columns,
    )
    self_sum = Reduction([((act_one,), grad_self_query)], "seq", small_term)
    owner_grads = frame_near.astype(jnp.float32) + frame_came.astype(jnp.float32)
    norm_far, owner_grads = advance([self_sum], (norm_far, owner_grads.astype(jnp.bfloat16)))
    norm_came = swap_seq(norm_far)
    grad_encoder = lax.all_to_all(
        owner_grads.reshape(size, owner_frames, model_width),
        "batch",
        split_axis=0,
        concat_axis=0,
        tiled=True,
    )
    advance([cross_sum, self_pair_sum], after=[self_sum])
    advance([self_sum], after=[cross_sum, self_pair_sum])
    norm_came = advance([cross_sum, self_pair_sum], norm_came, after=[self_sum])
    grad_encoder, wide_sum = advance(
        [self_sum], (grad_encoder, wide_sum), after=[cross_sum, self_pair_sum]
    )
    grad_encoder = grad_encoder.astype(jnp.float32)
    grad_hidden = hidden_back(norm_side, norm_came, hidden, gains[:, :1].T, grad_self)
    wide_sum = wide_sum.astype(jnp.float32) + swap_seq(wide_sum).astype(jnp.float32)
    inner_rows = down_weight.shape[0]
    grad_up_weight = (
        wide_sum[inner_rows:]
        .reshape(blocks, shard_rows, model_width)
        .transpose(1, 0, 2)
        .reshape(shard_rows, wide_cols)
    )
    grad_cross_kv, grad_cross_out, grad_cross_query, grad_self_out = cross_sum.result()
    grad_self_keys = self_pair_sum.result()[0]
    grad_self_queries, small_sum = self_sum.result()
    return (
        result[None],
        grad_hidden[None],
        grad_encoder,
        small_sum[:, :4],
        small_sum[:, 4:8],
        jnp.concatenate([grad_self_queries, grad_self_keys], axis=1),
        grad_self_out,
        grad_cross_query,
        grad_cross_kv,
        grad_cross_out,
        small_sum[:, 8:15],
        grad_up_weight,
        small_sum[:, 15:small_cols].reshape(-1),
        wide_sum[:inner_rows],
    )


def solution(mesh):
    in_specs = (
        P("batch", "seq", None),
        P(None, ("batch", "seq"), None),
        P("batch", "seq", None),
        P("batch"),
        P("batch"),
        P("batch"),
        P("batch"),
        P(),
        P("batch", None),
        P("batch", None),
        P("batch", None),
        P("batch", None),
        P("batch", None),
        P("batch", None),
        P("batch", None),
        P("batch", None),
        P("batch", None),
        P("batch"),
        P("batch", None),
    )
    out_specs = (
        P("batch", "seq", None),
        P("batch", "seq", None),
        P(None, ("batch", "seq"), None),
        P("batch", None),
        P("batch", None),
        P("batch", None),
        P("batch", None),
        P("batch", None),
        P("batch", None),
        P("batch", None),
        P("batch", None),
        P("batch", None),
        P("batch"),
        P("batch", None),
    )
    return jax.shard_map(body, mesh=mesh, in_specs=in_specs, out_specs=out_specs, check_vma=False)
```

```python
from functools import partial

import math

import jax
import jax.numpy as jnp
from jax import lax
from jax.experimental import pallas as pl
from jax.experimental.pallas import tpu as pltpu
from jax.sharding import PartitionSpec as P

HEAD_DIM = 64
LANES = 128


EPS = 1e-05

def layer_parts(values):
    center = values - jnp.mean(values, axis=-1, keepdims=True)
    inv_std = lax.rsqrt(jnp.mean(center * center, axis=-1, keepdims=True) + EPS)
    return (center * inv_std, inv_std)


def layer_back(grad_side, normed, inv_std, gain):
    scaled = grad_side * gain
    mean_one = jnp.mean(scaled, axis=-1, keepdims=True)
    mean_two = jnp.mean(scaled * normed, axis=-1, keepdims=True)
    grad_in = inv_std * (scaled - mean_one - normed * mean_two)
    return (grad_in, jnp.sum(grad_side * normed, axis=0), jnp.sum(grad_side, axis=0))


def dot_right(left_side, weight):
    return jnp.dot(left_side, weight, preferred_element_type=jnp.float32)


def dot_left(grad_side, weight):
    return jnp.einsum("cj,ij->ci", grad_side, weight, preferred_element_type=jnp.float32)


def weight_term(left_side, grad_side):
    return jnp.einsum(
        "ci,cj->ij", left_side, grad_side, preferred_element_type=jnp.float32
    ).astype(jnp.bfloat16)


def col_sum(grad_side):
    return jnp.sum(grad_side, axis=0, dtype=jnp.float32)


def hold(steps, values):
    return lax.optimization_barrier((steps, values))

ROWS_BY_LANES = (((1,), (1,)), ((), ()))
DOWN_BOTH = (((0,), (0,)), ((), ()))
ROWS_BY_ROWS = (((1,), (0,)), ((), ()))


def head_parts(block):
    lane = lax.broadcasted_iota(jnp.int32, block.shape, 1)
    zero = jnp.zeros_like(block)
    return (
        jnp.where(lane < HEAD_DIM, block, zero),
        jnp.where(lane < HEAD_DIM, zero, block),
    )


def dot_of(left, right, dims):
    return lax.dot_general(left, right, dims, preferred_element_type=jnp.float32)


def attend_kernel(query_ref, key_ref, value_ref, bias_ref, mixed_ref, total_ref):
    score_scale = HEAD_DIM ** (-0.5)
    key, value = key_ref[...], value_ref[...]
    queries = head_parts(query_ref[...] * jnp.bfloat16(score_scale))
    scores = [dot_of(key, query, ROWS_BY_LANES) + bias_ref[...] for query in queries]
    tops = [jnp.max(item, axis=0, keepdims=True) for item in scores]
    terms = [jnp.exp(item - top) for item, top in zip(scores, tops)]
    totals = [jnp.sum(item, axis=0, keepdims=True) for item in terms]
    sides = [dot_of(value, item.astype(jnp.bfloat16), DOWN_BOTH) for item in terms]
    for head in range(2):
        total_ref[0, head : head + 1, :] = tops[head] + jnp.log(totals[head])
    mixed = [
        sides[head][head * HEAD_DIM : (head + 1) * HEAD_DIM] / totals[head] for head in range(2)
    ]
    mixed_ref[...] = jnp.concatenate(mixed, axis=0).T.astype(jnp.bfloat16)


def attend_back_kernel(
    core_ref,
    query_ref,
    key_ref,
    value_ref,
    bias_ref,
    total_ref,
    grad_ref,
    gq_ref,
    kept_ref,
    sent_ref,
):
    score_scale = HEAD_DIM ** (-0.5)
    key, value = key_ref[...], value_ref[...]
    queries = head_parts(query_ref[...] * jnp.bfloat16(score_scale))
    grads = head_parts(grad_ref[...])
    scores = [dot_of(key, query, ROWS_BY_LANES) + bias_ref[...] for query in queries]
    terms = [
        jnp.exp(item - total_ref[0, head : head + 1, :]) for head, item in enumerate(scores)
    ]
    grad_terms = [
        item * dot_of(value, grad, ROWS_BY_LANES) for item, grad in zip(terms, grads)
    ]
    row_dots = [jnp.sum(item, axis=0, keepdims=True) for item in grad_terms]
    grad_scores = [
        (grad_term - term * row_dot).astype(jnp.bfloat16)
        for grad_term, term, row_dot in zip(grad_terms, terms, row_dots)
    ]
    values = [
        jnp.dot(item.astype(jnp.bfloat16), grad, preferred_element_type=jnp.float32)
        for item, grad in zip(terms, grads)
    ]
    keys = [
        jnp.dot(item, query, preferred_element_type=jnp.float32)
        for item, query in zip(grad_scores, queries)
    ]
    sides = [dot_of(key, item, DOWN_BOTH) for item in grad_scores]
    grad_key = (keys[0] + keys[1]).astype(jnp.bfloat16)
    grad_value = (values[0] + values[1]).astype(jnp.bfloat16)

    @pl.when(core_ref[0] == 0)
    def _():
        kept_ref[...] = grad_key
        sent_ref[...] = grad_value

    @pl.when(core_ref[0] == 1)
    def _():
        kept_ref[...] = grad_value
        sent_ref[...] = grad_key

    picked = [
        sides[head][head * HEAD_DIM : (head + 1) * HEAD_DIM] * score_scale for head in range(2)
    ]
    gq_ref[...] = jnp.concatenate(picked, axis=0).T.astype(jnp.bfloat16)


def head_specs(rows, keys, blocks):
    return [
        pl.BlockSpec((rows, LANES), lambda i: (0, i)),
        pl.BlockSpec((keys, LANES), lambda i: (0, i)),
        pl.BlockSpec((keys, LANES), lambda i: (0, i + blocks)),
        pl.BlockSpec((keys, rows), lambda i: (0, 0)),
    ]


def attend(queries, pairs, bias):
    rows, width = queries.shape
    keys = pairs.shape[0]
    blocks = width // LANES
    return pl.pallas_call(
        attend_kernel,
        grid=(blocks,),
        out_shape=(
            jax.ShapeDtypeStruct((rows, width), jnp.bfloat16),
            jax.ShapeDtypeStruct((blocks, 2, rows), jnp.float32),
        ),
        in_specs=head_specs(rows, keys, blocks),
        out_specs=(
            pl.BlockSpec((rows, LANES), lambda i: (0, i)),
            pl.BlockSpec((1, 2, rows), lambda i: (i, 0, 0)),
        ),
        cost_estimate=pl.CostEstimate(flops=0, transcendentals=0, bytes_accessed=0),
        name="attend",
    )(queries, pairs, pairs, bias)


def attend_back(core, queries, pairs, bias, totals, grads):
    rows, width = queries.shape
    keys = pairs.shape[0]
    blocks = width // LANES
    return pl.pallas_call(
        attend_back_kernel,
        grid=(blocks,),
        out_shape=(
            jax.ShapeDtypeStruct((rows, width), jnp.bfloat16),
            jax.ShapeDtypeStruct((keys, width), jnp.bfloat16),
            jax.ShapeDtypeStruct((keys, width), jnp.bfloat16),
        ),
        in_specs=[pl.BlockSpec(memory_space=pltpu.SMEM)]
        + head_specs(rows, keys, blocks)
        + [
            pl.BlockSpec((1, 2, rows), lambda i: (i, 0, 0)),
            pl.BlockSpec((rows, LANES), lambda i: (0, i)),
        ],
        out_specs=(
            pl.BlockSpec((rows, LANES), lambda i: (0, i)),
            pl.BlockSpec((keys, LANES), lambda i: (0, i)),
            pl.BlockSpec((keys, LANES), lambda i: (0, i)),
        ),
        cost_estimate=pl.CostEstimate(flops=0, transcendentals=0, bytes_accessed=0),
        name="attend_back",
    )(core.reshape(1), queries, pairs, pairs, bias, totals, grads)


CORES = 2
PAIR = 2
FLIP = [(0, 1), (1, 0)]


def partners(stride, radix, step):
    pairs = []
    for i in range(lax.axis_size("batch")):
        digit = i // stride % radix
        pairs.append((i, i + ((digit ^ step) - digit) * stride))
    return pairs


def swap(block, stride, radix=2, step=1):
    return lax.ppermute(block, "batch", partners(stride, radix, step))


def swap_seq(block):
    return lax.ppermute(block, "seq", FLIP)


def place_of():
    batch = lax.axis_index("batch")
    return (
        batch // (CORES * PAIR),
        batch // CORES % PAIR,
        batch % CORES,
        lax.axis_index("seq"),
    )


def splits(rows):
    depth = lax.axis_size("batch") // (CORES * PAIR)
    return rows % 48 == 0 and depth == 4 and lax.axis_size("seq") == 2


def place_kernel(where_ref, *refs, depth, rows, half):
    pieces, out_ref, sem = refs[:8], refs[8], refs[9]
    deep, wide, core, seq = where_ref[0], where_ref[1], where_ref[2], where_ref[3]
    started = []
    for c in range(2):
        column, across, side, side_across = pieces[4 * c : 4 * c + 4]
        for w, (near, far) in enumerate(((column, side), (across, side_across))):
            for k in range(depth):
                base = (((deep ^ k) * PAIR + (wide ^ w)) * CORES + (core ^ c)) * rows
                row_span = pl.ds(pl.multiple_of(base, 16), rows)
                for source, part in ((near, seq), (far, 1 - seq)):
                    col_span = pl.ds(pl.multiple_of(part * half, LANES), half)
                    copy = pltpu.make_async_copy(
                        source.at[k], out_ref.at[row_span, col_span], sem
                    )
                    copy.start()
                    started.append(copy)
    for copy in started:
        copy.wait()


class Gather:
    def __init__(self, shard, last):
        self.rows, self.cols = shard.shape
        self.half = self.cols // 2
        self.last = last
        self.depth = lax.axis_size("batch") // (CORES * PAIR)
        self.state = (shard,)
        self.todo = (
            [self.by_depth, self.by_both, self.by_last, self.place]
            if splits(self.rows)
            else [self.plain]
        )

    def step(self):
        if self.todo:
            self.state = self.todo.pop(0)(*self.state)
        return self

    def result(self):
        while self.todo:
            self.step()
        return self.state[0]

    def plain(self, shard):
        return (lax.all_gather(shard, "batch", axis=0, tiled=True),)

    def by_depth(self, shard):
        part = lax.dynamic_slice_in_dim(shard, lax.axis_index("seq") * self.half, self.half, 1)
        came = [swap(part, CORES * PAIR, self.depth, k) for k in range(1, self.depth)]
        return (jnp.stack([part] + came),)

    def by_both(self, column):
        return column, swap(column, CORES), swap_seq(column)

    def by_last(self, column, across, side):
        far = swap_seq(across) if self.last == "seq" else swap(side, CORES)
        return column, across, side, far, swap(column, 1), swap(across, 1), swap(side, 1)

    def place(self, *pieces):
        mine, other = pieces[:4], (*pieces[4:], swap(pieces[3], 1))
        total = lax.axis_size("batch") * self.rows
        call = pl.pallas_call(
            partial(place_kernel, depth=self.depth, rows=self.rows, half=self.half),
            out_shape=jax.ShapeDtypeStruct((total, self.cols), mine[0].dtype),
            in_specs=[pl.BlockSpec(memory_space=pltpu.SMEM)]
            + [pl.BlockSpec(memory_space=pl.ANY)] * 8,
            out_specs=pl.BlockSpec(memory_space=pltpu.VMEM),
            scratch_shapes=[pltpu.SemaphoreType.DMA],
            cost_estimate=pl.CostEstimate(flops=0, transcendentals=0, bytes_accessed=0),
            name="place_rows",
        )
        return (call(jnp.stack(place_of()).astype(jnp.int32), *mine, *other),)


def narrow(values):
    return lax.reduce_precision(values, 8, 7).astype(jnp.bfloat16)


def grad_kernel(where_ref, *refs, parts, split, first, rows, blend):
    terms = []
    for count in parts:
        terms.append((refs[:count], refs[count : 2 * count], *refs[2 * count : 2 * count + 2]))
        refs = refs[2 * count + 2 :]
    extras, (kept_ref, sent_ref, total_ref) = refs[:blend], refs[blend:]
    wide, core, seq = where_ref[1], where_ref[2], where_ref[3]
    height = total_ref.shape[0]
    groups = CORES * kept_ref.shape[0] * rows // height

    def group_step(group, carry):
        start = 0
        for (lefts, far_lefts, right_ref, far_right_ref), whole in zip(terms, split):
            width = far_right_ref.shape[1]
            span = pl.ds(pl.multiple_of(group * height, LANES), height)
            if whole:
                picked = slice(None)
            else:
                picked = pl.ds(pl.multiple_of(core * width, LANES), width)
            total, at = 0.0, 0
            for left_ref, far_left_ref in zip(lefts, far_lefts):
                tokens = slice(at, at + left_ref.shape[0])
                at += left_ref.shape[0]
                total = total + dot_of(left_ref[:, span], right_ref[tokens, picked], DOWN_BOTH)
                total = total + dot_of(
                    far_left_ref[:, span], far_right_ref[tokens, :], DOWN_BOTH
                )
            total_ref[:, :width] = total
            cols = slice(start, start + width)
            for place, near, far in routes(group, height, first, rows, wide, seq):
                for out_ref, base in ((kept_ref, near), (sent_ref, far)):
                    picked = total_ref[pl.ds(pl.multiple_of(base, 16), rows), :width]
                    out_ref[place, :, cols] = picked.astype(jnp.bfloat16)
            start += width
        if blend:
            cols = slice(start, start + LANES)
            for place, near, far in routes(group, height, first, rows, wide, seq):
                for out_ref, base in ((kept_ref, near), (sent_ref, far)):
                    picked = pl.ds(pl.multiple_of(group * height + base, 16), rows)
                    out_ref[place, :, cols] = (
                        extras[0][picked, :].astype(jnp.float32)
                        + extras[1][picked, :].astype(jnp.float32)
                    ).astype(jnp.bfloat16)
        return carry

    lax.fori_loop(0, groups, group_step, 0)


def routes(group, height, first, rows, wide, seq):
    if first == "seq":
        pairs = height // (2 * rows)
        return [
            (group * pairs + i, (2 * i + seq) * rows, (2 * i + 1 - seq) * rows)
            for i in range(pairs)
        ]
    quads = height // (4 * rows)
    return [
        (
            (group * quads + i) * 2 + j,
            (4 * i + 2 * wide + j) * rows,
            (4 * i + 2 * (1 - wide) + j) * rows,
        )
        for i in range(quads)
        for j in range(2)
    ]


def back_by_norm(grad_side, normed, inv_std, gain):
    scaled = grad_side * gain
    mean_one = jnp.mean(scaled, axis=-1, keepdims=True)
    mean_two = jnp.mean(scaled * normed, axis=-1, keepdims=True)
    return inv_std * (scaled - mean_one - normed * mean_two)


def sum_rows(values):
    return jnp.sum(values, axis=0, keepdims=True)


def feed_forward_kernel(
    act_ref,
    after_ref,
    grad_ref,
    live_ref,
    gain_ref,
    shift_ref,
    bias_ref,
    up_bias_ref,
    out_weight_ref,
    weight_ref,
    result_ref,
    cross_ref,
    cross_in_ref,
    mixed_ref,
    sums_ref,
    up_sums_ref,
    wide_ref,
    up_ref,
    down_ref,
    hidden_ref,
    slope_ref,
    side_ref,
    term_ref,
    project_ref,
    in_sem,
    out_sem,
):
    blocks, width, _ = up_ref.shape
    project = pltpu.make_async_copy(
        out_weight_ref.at[:, pl.ds(out_weight_ref.shape[1] - width, width)],
        project_ref,
        in_sem.at[2 * blocks],
    )
    size = wide_ref.shape[0]
    piece = width // size
    inner = blocks * piece
    per = size // blocks
    copies = []
    for j in range(blocks):
        for b in range(size):
            copies.append(
                (
                    weight_ref.at[pl.ds(b * inner + j * piece, piece), pl.ds(0, width)],
                    up_ref.at[j, pl.ds(b * piece, piece)],
                    in_sem.at[j],
                )
            )
        copies.append(
            (
                weight_ref.at[pl.ds(j * width, width), pl.ds(width, width)],
                down_ref.at[j],
                in_sem.at[blocks + j],
            )
        )
    started = [pltpu.make_async_copy(*copy) for copy in copies]
    for copy in started:
        copy.start()
    project.start()

    def wait_up(j):
        pltpu.make_async_copy(down_ref.at[j], up_ref.at[j], in_sem.at[j]).wait()

    def wait_down(j):
        pltpu.make_async_copy(up_ref.at[j], down_ref.at[j], in_sem.at[blocks + j]).wait()

    act = act_ref[...]
    half_root, slope_scale = math.sqrt(0.5), 1.0 / math.sqrt(2.0 * math.pi)

    def rise(j, total):
        wait_up(j)
        up = dot_of(act, up_ref[j], (((1,), (0,)), ((), ()))) + up_bias_ref[j]
        level = 0.5 * (1.0 + lax.erf(up * half_root))
        hidden_ref[j] = (up * level).astype(jnp.bfloat16)
        slope_ref[j] = level + up * (slope_scale * jnp.exp(-0.5 * up * up))
        wait_down(j)
        return total + dot_of(hidden_ref[j], down_ref[j], (((1,), (0,)), ((), ())))

    after = after_ref[...]
    mlp = lax.fori_loop(0, blocks, rise, after + bias_ref[...])
    normed, inv_std = layer_parts(mlp)
    result_ref[...] = (normed * gain_ref[1:2] + shift_ref[...]).astype(jnp.bfloat16)
    grad_out = grad_ref[...].astype(jnp.float32) * live_ref[...]
    grad_mlp = back_by_norm(grad_out, normed, inv_std, gain_ref[1:2])
    grad_down = grad_mlp.astype(jnp.bfloat16)

    def fall(j, total):
        grad_act = dot_of(grad_down, down_ref[j], ROWS_BY_LANES)
        grad_up = slope_ref[j] * grad_act
        side_ref[j] = grad_up.astype(jnp.bfloat16)
        up_sums_ref[j] = sum_rows(grad_up)
        return total + dot_of(side_ref[j], up_ref[j], ROWS_BY_LANES)

    grad_three = lax.fori_loop(0, blocks, fall, jnp.zeros_like(mlp))

    def outward(j):
        return (
            pltpu.make_async_copy(
                term_ref.at[pl.ds(j * per, per), pl.ds(0, inner)],
                wide_ref.at[pl.ds(j * per, per), pl.ds(0, inner)],
                out_sem.at[j],
            ),
            pltpu.make_async_copy(
                term_ref.at[:, pl.ds(pl.multiple_of(inner + j * piece, 16), piece)],
                wide_ref.at[:, pl.ds(pl.multiple_of(inner + j * piece, 16), piece)],
                out_sem.at[blocks + j],
            ),
        )

    def weigh(j, carry):
        down = dot_of(hidden_ref[j], grad_down, DOWN_BOTH).astype(jnp.bfloat16)
        for t in range(per):
            term_ref[j * per + t, :inner] = down[t * inner : (t + 1) * inner]
        up = dot_of(act, side_ref[j], DOWN_BOTH).astype(jnp.bfloat16)
        span = pl.ds(pl.multiple_of(inner + j * piece, 16), piece)
        for b in range(size):
            term_ref[b, span] = up[b * piece : (b + 1) * piece]
        for copy in outward(j):
            copy.start()
        return carry

    lax.fori_loop(0, blocks, weigh, 0)
    normed_three, scale_three = layer_parts(after)
    grad_cross = grad_mlp + back_by_norm(grad_three, normed_three, scale_three, gain_ref[0:1])
    cross_ref[...] = grad_cross
    grad_cross_in = grad_cross.astype(jnp.bfloat16)
    cross_in_ref[...] = grad_cross_in
    project.wait()
    grad_mixed = dot_of(grad_cross_in, project_ref[...], ROWS_BY_LANES).astype(jnp.bfloat16)
    mixed_ref[...] = grad_mixed
    rows = [
        grad_three * normed_three,
        grad_three,
        grad_out * normed,
        grad_out,
        grad_down.astype(jnp.float32),
        grad_cross_in.astype(jnp.float32),
        grad_mixed.astype(jnp.float32),
    ]
    for i, item in enumerate(rows):
        sums_ref[i : i + 1] = sum_rows(item)

    def finish(j, carry):
        for copy in outward(j):
            copy.wait()
        return carry

    lax.fori_loop(0, blocks, finish, 0)


def feed_forward(act, after, grad, live, gains, shift, bias, up_bias, out_weight, weight, size):
    rows, width = act.shape
    blocks = up_bias.shape[0]
    inner = blocks * width // size
    shape = jax.ShapeDtypeStruct
    vmem = pl.BlockSpec(memory_space=pltpu.VMEM)
    return pl.pallas_call(
        feed_forward_kernel,
        out_shape=(
            shape((rows, width), jnp.bfloat16),
            shape((rows, width), jnp.float32),
            shape((rows, width), jnp.bfloat16),
            shape((rows, width), jnp.bfloat16),
            shape((8, width), jnp.float32),
            shape((blocks, 1, width), jnp.float32),
            shape((size, 2 * inner, width), jnp.bfloat16),
        ),
        in_specs=[vmem] * 8 + [pl.BlockSpec(memory_space=pl.ANY)] * 2,
        out_specs=(vmem,) * 6 + (pl.BlockSpec(memory_space=pl.ANY),),
        scratch_shapes=[
            pltpu.VMEM((blocks, width, width), jnp.bfloat16),
            pltpu.VMEM((blocks, width, width), jnp.bfloat16),
            pltpu.VMEM((blocks, rows, width), jnp.bfloat16),
            pltpu.VMEM((blocks, rows, width), jnp.float32),
            pltpu.VMEM((blocks, rows, width), jnp.bfloat16),
            pltpu.VMEM((size, 2 * inner, width), jnp.bfloat16),
            pltpu.VMEM((width, width), jnp.bfloat16),
            pltpu.SemaphoreType.DMA((2 * blocks + 1,)),
            pltpu.SemaphoreType.DMA((2 * blocks,)),
        ],
        cost_estimate=pl.CostEstimate(flops=0, transcendentals=0, bytes_accessed=0),
        name="feed_forward",
    )(act, after, grad, live, gains, shift, bias, up_bias, out_weight, weight)


def frame_pairs_kernel(near_ref, far_ref, weight_ref, bias_ref, pair_ref):
    half = pl.num_programs(0) // 2

    @pl.when(pl.program_id(0) < half)
    def _():
        pair_ref[...] = (
            dot_of(near_ref[...], weight_ref[...], ROWS_BY_ROWS) + bias_ref[...]
        ).astype(jnp.bfloat16)

    @pl.when(pl.program_id(0) >= half)
    def _():
        pair_ref[...] = (
            dot_of(far_ref[...], weight_ref[...], ROWS_BY_ROWS) + bias_ref[...]
        ).astype(jnp.bfloat16)


def frame_pairs(near, far, weight, bias):
    half, width = near.shape
    steps = half // (2 * LANES)
    return pl.pallas_call(
        frame_pairs_kernel,
        grid=(2 * steps,),
        out_shape=jax.ShapeDtypeStruct((2 * half, 2 * width), jnp.bfloat16),
        in_specs=[
            pl.BlockSpec((2 * LANES, width), lambda i: (jnp.minimum(i, steps - 1), 0)),
            pl.BlockSpec((2 * LANES, width), lambda i: (jnp.maximum(i - steps, 0), 0)),
            pl.BlockSpec((width, 2 * width), lambda i: (0, 1)),
            pl.BlockSpec((1, 2 * width), lambda i: (0, 0)),
        ],
        out_specs=pl.BlockSpec((2 * LANES, 2 * width), lambda i: (i, 0)),
        cost_estimate=pl.CostEstimate(flops=0, transcendentals=0, bytes_accessed=0),
        name="frame_pairs",
    )(near, far, weight, bias)


def frame_back_kernel(core_ref, kept_ref, sent_ref, weight_ref, far_weight_ref, near_ref, far_ref):
    half = pl.num_programs(0) // 2
    grad = dot_of(kept_ref[...], weight_ref[...], ROWS_BY_LANES) + dot_of(
        sent_ref[...], far_weight_ref[...], ROWS_BY_LANES
    )

    @pl.when(pl.program_id(0) < half)
    def _():
        near_ref[...] = grad.astype(jnp.bfloat16)

    @pl.when(pl.program_id(0) >= half)
    def _():
        far_ref[...] = grad.astype(jnp.bfloat16)


def frame_back(core, kept, sent, weight):
    keys, width = kept.shape
    steps = keys // (4 * LANES)
    shape = jax.ShapeDtypeStruct((keys // 2, width), jnp.bfloat16)
    return pl.pallas_call(
        frame_back_kernel,
        grid_spec=pltpu.PrefetchScalarGridSpec(
            num_scalar_prefetch=1,
            grid=(2 * steps,),
            in_specs=[
                pl.BlockSpec((2 * LANES, width), lambda i, core: (i, 0)),
                pl.BlockSpec((2 * LANES, width), lambda i, core: (i, 0)),
                pl.BlockSpec((width, width), lambda i, core: (0, 2 + core[0])),
                pl.BlockSpec((width, width), lambda i, core: (0, 3 - core[0])),
            ],
            out_specs=(
                pl.BlockSpec((2 * LANES, width), lambda i, core: (jnp.minimum(i, steps - 1), 0)),
                pl.BlockSpec((2 * LANES, width), lambda i, core: (jnp.maximum(i - steps, 0), 0)),
            ),
        ),
        out_shape=(shape, shape),
        cost_estimate=pl.CostEstimate(flops=0, transcendentals=0, bytes_accessed=0),
        name="frame_back",
    )(core.reshape(1), kept, sent, weight, weight)


def self_head_kernel(
    near_ref, far_ref, gain_ref, shift_ref, bias_ref, weight_ref, act_ref, far_act_ref, query_ref, pair_ref
):
    rows, width = near_ref.shape
    tile = width // 2
    for source_ref, out_ref in ((far_ref, far_act_ref), (near_ref, act_ref)):
        normed, _ = layer_parts(source_ref[...].astype(jnp.float32))
        out_ref[...] = (normed * gain_ref[...] + shift_ref[...]).astype(jnp.bfloat16)

    def project(source_ref, t):
        span = pl.ds(pl.multiple_of(t * tile, LANES), tile)
        return (
            dot_of(source_ref[...], weight_ref[:, span], ROWS_BY_ROWS) + bias_ref[:, span]
        ).astype(jnp.bfloat16)

    def query(t, carry):
        query_ref[:, pl.ds(pl.multiple_of(t * tile, LANES), tile)] = project(act_ref, t)
        return carry

    def pair(t, carry):
        span = pl.ds(pl.multiple_of(t * tile, LANES), tile)
        pair_ref[:rows, span] = project(far_act_ref, t + 2)
        pair_ref[rows:, span] = project(act_ref, t + 2)
        return carry

    lax.fori_loop(0, 2, query, 0)
    lax.fori_loop(0, 4, pair, 0)


def self_head(near, far, gain, shift, bias, weight):
    rows, width = near.shape
    shape = jax.ShapeDtypeStruct((rows, width), jnp.bfloat16)
    return pl.pallas_call(
        self_head_kernel,
        out_shape=(
            shape,
            shape,
            shape,
            jax.ShapeDtypeStruct((2 * rows, 2 * width), jnp.bfloat16),
        ),
        cost_estimate=pl.CostEstimate(flops=0, transcendentals=0, bytes_accessed=0),
        name="self_head",
    )(near, far, gain, shift, bias, weight)


def hidden_back_kernel(side_ref, came_ref, hidden_ref, gain_ref, self_ref, out_ref):
    normed, inv_std = layer_parts(hidden_ref[...].astype(jnp.float32))
    side = side_ref[...] + came_ref[...].astype(jnp.float32)
    out_ref[...] = self_ref[...] + back_by_norm(side, normed, inv_std, gain_ref[...])


def hidden_back(side, came, hidden, gain, grad_self):
    return pl.pallas_call(
        hidden_back_kernel,
        out_shape=jax.ShapeDtypeStruct(side.shape, jnp.float32),
        cost_estimate=pl.CostEstimate(flops=0, transcendentals=0, bytes_accessed=0),
        name="hidden_back",
    )(side, came, hidden, gain, grad_self)


def query_back_kernel(
    grad_ref,
    cross_ref,
    after_ref,
    gain_ref,
    weight_ref,
    self_ref,
    self_in_ref,
    mixed_ref,
    sums_ref,
    held_ref,
    sem,
):
    width = grad_ref.shape[1]
    copies = [
        pltpu.make_async_copy(
            weight_ref.at[:, pl.ds(i * width, width)], held_ref.at[i], sem.at[i]
        )
        for i in (1, 0)
    ]
    for copy in copies:
        copy.start()
    copies[0].wait()
    side = dot_of(grad_ref[...], held_ref[1], ROWS_BY_LANES)
    normed, inv_std = layer_parts(after_ref[...])
    grad_self = cross_ref[...] + back_by_norm(side, normed, inv_std, gain_ref[...])
    self_ref[...] = grad_self
    grad_self_in = grad_self.astype(jnp.bfloat16)
    self_in_ref[...] = grad_self_in
    copies[1].wait()
    grad_mixed = dot_of(grad_self_in, held_ref[0], ROWS_BY_LANES).astype(jnp.bfloat16)
    mixed_ref[...] = grad_mixed
    rows = [
        side * normed,
        side,
        grad_ref[...].astype(jnp.float32),
        grad_self_in.astype(jnp.float32),
        grad_mixed.astype(jnp.float32),
    ]
    for i, item in enumerate(rows):
        sums_ref[i : i + 1] = sum_rows(item)


def query_back(grad, cross, after, gain, weight):
    shape = jax.ShapeDtypeStruct
    rows, width = grad.shape
    return pl.pallas_call(
        query_back_kernel,
        out_shape=(
            shape((rows, width), jnp.float32),
            shape((rows, width), jnp.bfloat16),
            shape((rows, width), jnp.bfloat16),
            shape((8, width), jnp.float32),
        ),
        in_specs=[pl.BlockSpec(memory_space=pltpu.VMEM)] * 4 + [pl.BlockSpec(memory_space=pl.ANY)],
        out_specs=(pl.BlockSpec(memory_space=pltpu.VMEM),) * 4,
        scratch_shapes=[
            pltpu.VMEM((2, width, width), jnp.bfloat16),
            pltpu.SemaphoreType.DMA((2,)),
        ],
        cost_estimate=pl.CostEstimate(flops=0, transcendentals=0, bytes_accessed=0),
        name="query_back",
    )(grad, cross, after, gain, weight)


def self_tail_kernel(
    core_ref,
    query_ref,
    kept_ref,
    sent_ref,
    weight_ref,
    near_ref,
    far_ref,
    query_table_ref,
    table_ref,
    base_ref,
    side_ref,
    moved_ref,
    column_ref,
):
    rows, width = query_ref.shape
    core = core_ref[0]
    near_span = pl.ds(pl.multiple_of((1 + core) * width, LANES), width)
    far_span = pl.ds(pl.multiple_of((2 - core) * width, LANES), width)
    both = dot_of(kept_ref[...], weight_ref[:, near_span], ROWS_BY_LANES) + dot_of(
        sent_ref[...], weight_ref[:, far_span], ROWS_BY_LANES
    )
    far = both[:rows]
    side = both[rows:] + dot_of(query_ref[...], weight_ref[:, :width], ROWS_BY_LANES)
    side_ref[...] = side
    moved_ref[...] = far.astype(jnp.bfloat16)
    normed, _ = layer_parts(near_ref[...].astype(jnp.float32))
    normed_far, _ = layer_parts(far_ref[...].astype(jnp.float32))
    gain_one = sum_rows(side * normed + far * normed_far)
    shift_one = sum_rows(side + far)
    query_bias = sum_rows(query_ref[...].astype(jnp.float32))
    gain_two, shift_two, cross_query, self_out, value = [
        query_table_ref[i : i + 1] for i in range(5)
    ]
    gain_three, shift_three, gain_last, shift_last, down, cross_out, cross_value = [
        table_ref[i : i + 1] for i in range(7)
    ]
    sums = [gain_one, gain_two, gain_three, gain_last]
    sums += [shift_one, shift_two, shift_three, shift_last]
    sums += [query_bias, value, self_out, cross_query, cross_value, cross_out, down]
    lane = lax.broadcasted_iota(jnp.int32, (LANES, LANES), 1)
    blank = jnp.zeros((LANES - len(sums), LANES), jnp.float32)
    for i in range(width // LANES):
        here = slice(i * LANES, (i + 1) * LANES)
        block = jnp.concatenate([item[:, here] for item in sums] + [blank], axis=0)
        column_ref[here, :] = jnp.where(
            lane < len(sums), block.T, base_ref[here, :].astype(jnp.float32)
        ).astype(jnp.bfloat16)


def self_tail(core, query, kept, sent, weight, near, far, query_table, table, base):
    rows, width = query.shape
    return pl.pallas_call(
        self_tail_kernel,
        out_shape=(
            jax.ShapeDtypeStruct((rows, width), jnp.float32),
            jax.ShapeDtypeStruct((rows, width), jnp.bfloat16),
            jax.ShapeDtypeStruct(base.shape, jnp.bfloat16),
        ),
        in_specs=[pl.BlockSpec(memory_space=pltpu.SMEM)]
        + [pl.BlockSpec(memory_space=pltpu.VMEM)] * 9,
        cost_estimate=pl.CostEstimate(flops=0, transcendentals=0, bytes_accessed=0),
        name="self_tail",
    )(core.reshape(1), query, kept, sent, weight, near, far, query_table, table, base)


def half_of(right, which):
    width = right.shape[1] // CORES
    return lax.dynamic_slice_in_dim(right, which * width, width, 1)


class Reduction:
    def __init__(self, terms, first, extra=None):
        self.size = lax.axis_size("batch")
        self.depth = self.size // (CORES * PAIR)
        self.rows = terms[0][0][0].shape[1] // self.size
        self.first = first
        self.terms, self.extra = terms, extra
        self.fast = splits(self.rows)
        self.widths = [
            right[0].shape[1] if isinstance(right, tuple) else right.shape[1] // CORES
            for _, right in terms
        ]
        self.state = ()
        self.todo = (
            [self.begin, self.by_first, self.by_second, self.by_depth, self.by_seq, self.finish]
            if self.fast
            else [self.plain]
        )

    def step(self):
        if self.todo:
            self.state = self.todo.pop(0)(*self.state)
        return self

    def result(self):
        while self.todo:
            self.step()
            self.state = self.launch(*self.state)
        return self.state

    def plain(self):
        _, _, core, _ = place_of()
        whole = [] if self.extra is None else [self.extra]
        for left, right in reversed(self.terms):
            if isinstance(right, tuple):
                kept, sent = right
                right = jnp.concatenate(
                    [jnp.where(core == 0, kept, sent), jnp.where(core == 0, sent, kept)], axis=1
                )
            whole.insert(0, weight_term(jnp.concatenate(left, axis=0), right))
        mine = lax.psum_scatter(
            jnp.concatenate(whole, axis=1), "batch", scatter_dimension=0, tiled=True
        )
        mine = lax.psum(mine, "seq").astype(jnp.float32)
        ends = [0]
        for item in whole:
            ends.append(ends[-1] + item.shape[1])
        return tuple(mine[:, i:j] for i, j in zip(ends, ends[1:]))

    def begin(self):
        self.sender = self.along_seq if self.first == "seq" else self.along_pair
        where = jnp.stack(place_of()).astype(jnp.int32)
        operands = [where]
        for left, right in self.terms:
            if isinstance(right, tuple):
                kept, sent = right
            else:
                kept, sent = right, half_of(right, 1 - where[2])
            operands += [*left, *[swap(part, 1) for part in left], kept, swap(sent, 1)]
        if self.extra is not None:
            operands += [self.extra, swap(self.extra, 1)]
        blend = 0 if self.extra is None else 2
        total = sum(self.widths) + (LANES if blend else 0)
        shape = jax.ShapeDtypeStruct((self.depth * PAIR, self.rows, total), jnp.bfloat16)
        height = 3 * LANES
        return tuple(
            pl.pallas_call(
                partial(
                    grad_kernel,
                    parts=[len(left) for left, _ in self.terms],
                    split=[isinstance(right, tuple) for _, right in self.terms],
                    first=self.first,
                    rows=self.rows,
                    blend=blend,
                ),
                out_shape=(shape, shape),
                in_specs=[pl.BlockSpec(memory_space=pltpu.SMEM)]
                + [pl.BlockSpec(memory_space=pltpu.VMEM)] * (len(operands) - 1),
                out_specs=(pl.BlockSpec(memory_space=pltpu.VMEM),) * 2,
                scratch_shapes=[pltpu.VMEM((height, max(self.widths)), jnp.float32)],
                cost_estimate=pl.CostEstimate(flops=0, transcendentals=0, bytes_accessed=0),
                name="grad_blocks",
            )(*operands)
        )

    def launch(self, kept, *sent):
        if not self.fast:
            return (kept, *sent)
        return (kept, *self.sender(*sent))

    def along_seq(self, block):
        return (swap_seq(block),)

    def along_pair(self, block):
        return (swap(block, CORES),)

    def along_depth(self, *blocks):
        return tuple(
            swap(block, CORES * PAIR, self.depth, k) for k, block in enumerate(blocks, 1)
        )

    def along_core(self, block):
        return (swap(block, 1),)

    def by_first(self, kept, came):
        _, wide, _, seq = place_of()
        self.sender = self.along_pair if self.first == "seq" else self.along_seq
        kept = kept.astype(jnp.float32) + came.astype(jnp.float32)
        kept = kept.reshape(self.depth, 2, self.rows, -1)
        which = wide if self.first == "seq" else seq
        return tuple(
            lax.dynamic_index_in_dim(kept, i, 1, keepdims=False).astype(jnp.bfloat16)
            for i in (which, 1 - which)
        )

    def by_second(self, kept, came):
        deep, _, _, _ = place_of()
        self.sender = self.along_depth
        kept = kept.astype(jnp.float32) + came.astype(jnp.float32)
        return tuple(
            lax.dynamic_index_in_dim(kept, deep ^ k, 0, keepdims=False).astype(jnp.bfloat16)
            for k in range(self.depth)
        )

    def by_depth(self, kept, *came):
        total = kept.astype(jnp.float32)
        for block in came:
            total = total + block.astype(jnp.float32)
        self.sender = self.along_seq
        total = narrow(total)
        return total, total

    def by_seq(self, mine, came):
        _, _, core, seq = place_of()
        same = seq == core
        self.sender = self.along_core
        return jnp.where(same, mine, came), jnp.where(same, came, mine)

    def finish(self, mine, came):
        _, _, core, _ = place_of()
        self.fast = False
        low = jnp.where(core == 0, mine, came).astype(jnp.float32)
        high = jnp.where(core == 0, came, mine).astype(jnp.float32)
        results, start = [], 0
        for width in self.widths:
            cols = slice(start, start + width)
            results.append(jnp.concatenate([low[:, cols], high[:, cols]], axis=1))
            start += width
        if self.extra is not None:
            results.append(mine[:, start:].astype(jnp.float32))
        return tuple(results)


def advance(works, values=(), after=()):
    for work in works:
        work.step()
    states = [work.state for work in works]
    heads = [work.state[0] for work in after]
    states, heads, values = lax.optimization_barrier((states, heads, values))
    for work, state in zip(works, states):
        work.state = work.launch(*state)
    for work, head in zip(after, heads):
        work.state = (head, *work.state[1:])
    return values


def body(
    hidden,
    encoder,
    cotangent,
    token_offsets,
    token_lengths,
    frame_counts,
    corpus_ids,
    corpus_weights,
    norm_gains,
    norm_shifts,
    self_in,
    self_out,
    cross_query,
    cross_kv,
    cross_out,
    proj_bias,
    up_weight,
    up_bias,
    down_weight,
):
    hidden, cotangent = hidden[0], cotangent[0]
    row_count, model_width = hidden.shape
    shard_rows = norm_gains.shape[0]
    wide_cols = up_weight.shape[1]
    blocks = wide_cols // model_width
    size = lax.axis_size("batch")

    tail_width = 2 * LANES
    core = place_of()[2].astype(jnp.int32)
    small = jnp.concatenate(
        [norm_gains, norm_shifts, proj_bias, up_bias.reshape(shard_rows, blocks)], axis=1
    )
    small_cols = small.shape[1]
    small = jnp.pad(small, ((0, 0), (0, tail_width - small_cols)))
    first = Gather(jnp.concatenate([self_in, small], axis=1), "seq")
    second = Gather(jnp.concatenate([self_out, cross_query, cross_kv, cross_out], axis=1), "pair")
    up_blocks = up_weight.reshape(shard_rows, blocks, model_width).transpose(1, 0, 2)
    third = jnp.concatenate([up_blocks.reshape(-1, model_width), down_weight], axis=1)
    hidden_other = swap_seq(hidden)
    first.step()
    second.state, encoder, first.state, hidden_other = lax.optimization_barrier(
        (second.state, encoder, first.state, hidden_other)
    )
    frame_mine = lax.all_to_all(encoder, "batch", split_axis=0, concat_axis=0, tiled=True)
    frame_mine = frame_mine.reshape(-1, model_width)
    first.step()
    second.step()
    first.state, second.state, third = lax.optimization_barrier(
        (first.state, second.state, third)
    )
    first.step()
    second.step()
    third_all = lax.all_gather(third, "batch", axis=0, tiled=True)
    first_all = first.result()

    small_all = first_all[:, 3 * model_width : 3 * model_width + small_cols]
    gains = small_all[:, :4].astype(jnp.float32)
    shifts = small_all[:, 4:8].astype(jnp.float32)
    biases = small_all[:, 8:15].astype(jnp.float32)
    up_bias_all = small_all[:, 15:].reshape(-1).astype(jnp.float32)

    offset, length, frame_count = token_offsets[0], token_lengths[0], frame_counts[0]
    seq_index = lax.axis_index("seq")
    slots = jnp.arange(row_count, dtype=jnp.int32)
    positions = seq_index * row_count + slots
    positions_other = (1 - seq_index) * row_count + slots
    zero_row = jnp.zeros((model_width,), jnp.float32)
    inputs = hidden.astype(jnp.float32)
    qkv_bias = jnp.concatenate([biases[:, 0], zero_row, biases[:, 1]])
    act_one, act_far, self_query, self_pairs = self_head(
        hidden, hidden_other, gains[:, :1].T, shifts[:, :1].T, qkv_bias[None], first_all
    )
    key_pos = jnp.concatenate([positions_other, positions])[:, None]
    query_pos = positions[None, :]
    self_mask = (key_pos <= query_pos) & ((key_pos >= offset) | (key_pos == query_pos))
    self_bias = jnp.where(self_mask, 0.0, -jnp.inf)
    self_query, self_pairs, second.state = lax.optimization_barrier(
        (self_query, self_pairs, second.state)
    )
    second.step()
    half_slots = frame_mine.shape[0]
    owner_frames = encoder.shape[1]
    gathered = jnp.arange(2 * half_slots, dtype=jnp.int32)
    half_index = (gathered // half_slots) ^ seq_index
    within = gathered % half_slots
    frame_ids = (within // owner_frames * 2 + half_index) * owner_frames + within % owner_frames
    frame_bias = jnp.broadcast_to(
        jnp.where(frame_ids < frame_count, 0.0, -jnp.inf)[:, None], (2 * half_slots, row_count)
    )
    corpus_match = corpus_ids[0] == jnp.arange(corpus_weights.shape[0], dtype=jnp.int32)
    seq_weight = jnp.sum(jnp.where(corpus_match, corpus_weights, 0.0))
    live_rows = (positions >= offset) & (positions < offset + length)
    live_weight = jnp.where(live_rows, seq_weight, 0.0)[:, None]
    up_bias_blocks = up_bias_all.reshape(blocks, 1, model_width)
    kv_bias = jnp.concatenate([zero_row, biases[:, 4]])[None]
    side_rows = (
        gains[:, :1].T,
        gains[:, 1:2].T,
        gains[:, 2:].T,
        shifts[:, 3:].T,
        biases[:, 6:].T,
        biases[:, 2][None],
        biases[:, 3][None],
        biases[:, 5][None],
        shifts[:, 1][None],
        gains[:, 2][None],
        shifts[:, 2][None],
    )
    self_query, self_pairs, frame_mine, side_rows, frame_bias, live_weight, up_bias_blocks, kv_bias = (
        lax.optimization_barrier(
            (
                self_query,
                self_pairs,
                frame_mine,
                side_rows,
                frame_bias,
                live_weight,
                up_bias_blocks,
                kv_bias,
            )
        )
    )
    (
        gain_self,
        gain_query,
        gain_end,
        shift_end,
        bias_down,
        bias_self_out,
        bias_query,
        bias_cross_out,
        shift_query,
        gain_up,
        shift_up,
    ) = side_rows
    frame_other = swap_seq(frame_mine)
    self_mixed, self_total = attend(self_query, self_pairs, self_bias)
    self_mixed, second.state, frame_other = lax.optimization_barrier(
        (self_mixed, second.state, frame_other)
    )
    second_all = second.result()
    self_out_all = second_all[:, :model_width]
    query_all = second_all[:, model_width : 2 * model_width]
    kv_all = second_all[:, 2 * model_width : 4 * model_width]
    cross_out_all = second_all[:, 4 * model_width :]
    after_self = inputs + dot_right(self_mixed, self_out_all) + bias_self_out
    normed_two, scale_two = layer_parts(after_self)
    act_two = (normed_two * gain_query + shift_query).astype(jnp.bfloat16)
    cross_queries = (dot_right(act_two, query_all) + bias_query).astype(jnp.bfloat16)
    cross_pairs = frame_pairs(frame_mine, frame_other, second_all, kv_bias)
    cross_mixed, cross_total = attend(cross_queries, cross_pairs, frame_bias)
    after_cross = after_self + dot_right(cross_mixed, cross_out_all) + bias_cross_out
    normed_three, scale_three = layer_parts(after_cross)
    act_three = (normed_three * gain_up + shift_up).astype(jnp.bfloat16)
    if splits(shard_rows):
        result, grad_cross, grad_cross_in, grad_cross_mixed, table, up_sums, wide_term = feed_forward(
            act_three,
            after_cross,
            cotangent,
            live_weight,
            gain_end,
            shift_end,
            bias_down,
            up_bias_blocks,
            second_all,
            third_all,
            size,
        )
        up_bias_sum = up_sums.reshape(-1)
    else:
        down_all = third_all[:, model_width:]
        up_all = (
            third_all[:, :model_width]
            .reshape(size, blocks, shard_rows, model_width)
            .transpose(0, 2, 1, 3)
            .reshape(model_width, wide_cols)
        )
        up_value = dot_right(act_three, up_all) + up_bias_all
        gelu_value, gelu_pull = jax.vjp(partial(jax.nn.gelu, approximate=False), up_value)
        hidden_act = gelu_value.astype(jnp.bfloat16)
        after_mlp = after_cross + dot_right(hidden_act, down_all) + biases[:, 6]
        normed_last, scale_last = layer_parts(after_mlp)
        result = (normed_last * gains[:, 3] + shifts[:, 3]).astype(jnp.bfloat16)
        grad_out = cotangent.astype(jnp.float32) * live_weight
        grad_mlp, gain_last, shift_last = layer_back(grad_out, normed_last, scale_last, gains[:, 3])
        grad_down = grad_mlp.astype(jnp.bfloat16)
        down_bias = col_sum(grad_down)
        grad_act = dot_left(grad_down, down_all)
        grad_up = gelu_pull(grad_act)[0].astype(jnp.bfloat16)
        up_bias_sum = col_sum(grad_up)
        wide_term = jnp.concatenate(
            [weight_term(hidden_act, grad_down).reshape(size, -1, model_width)]
            + [
                weight_term(act_three, part).reshape(size, shard_rows, model_width)
                for part in jnp.split(grad_up, blocks, axis=1)
            ],
            axis=1,
        )
        back_three, gain_three, shift_three = layer_back(
            dot_left(grad_up, up_all), normed_three, scale_three, gains[:, 2]
        )
        grad_cross = grad_mlp + back_three
        grad_cross_in = grad_cross.astype(jnp.bfloat16)
        grad_cross_mixed = dot_left(grad_cross_in, cross_out_all).astype(jnp.bfloat16)
        table = jnp.stack(
            [
                gain_three,
                shift_three,
                gain_last,
                shift_last,
                down_bias,
                col_sum(grad_cross_in),
                col_sum(grad_cross_mixed),
                jnp.zeros_like(down_bias),
            ]
        )
    up_bias_columns = jnp.pad(
        up_bias_sum.astype(jnp.bfloat16).reshape(model_width, blocks),
        ((0, 0), (small_cols - blocks, LANES - small_cols)),
    )
    wide_term, grad_cross_mixed = lax.optimization_barrier((wide_term, grad_cross_mixed))
    wide_sum = lax.psum_scatter(wide_term, "batch", scatter_dimension=0, tiled=True)[0]
    grad_cq, frame_kept, frame_sent = attend_back(
        core, cross_queries, cross_pairs, frame_bias, cross_total, grad_cross_mixed
    )
    frame_near, frame_far = frame_back(core, frame_kept, frame_sent, second_all)
    grad_cq, frame_near, frame_far = lax.optimization_barrier((grad_cq, frame_near, frame_far))
    frame_came = swap_seq(frame_far)
    grad_self, grad_self_in, grad_self_mixed, query_table = query_back(
        grad_cq, grad_cross, after_self, gain_query, second_all
    )
    cross_sum = Reduction(
        [
            ((frame_mine, frame_other), (frame_kept, frame_sent)),
            ((cross_mixed,), grad_cross_in),
            ((act_two,), grad_cq),
            ((self_mixed,), grad_self_in),
        ],
        "seq",
    )
    grad_self_mixed = advance([cross_sum], grad_self_mixed)
    grad_self_query, self_kept, self_sent = attend_back(
        core, self_query, self_pairs, self_bias, self_total, grad_self_mixed
    )
    self_pair_sum = Reduction([((act_far, act_one), (self_kept, self_sent))], "pair")
    grad_self_query, self_kept, self_sent = advance(
        [self_pair_sum], (grad_self_query, self_kept, self_sent)
    )
    norm_side, norm_far, small_term = self_tail(
        core,
        grad_self_query,
        self_kept,
        self_sent,
        first_all,
        hidden,
        hidden_other,
        query_table,
        table,
        up_bias_columns,
    )
    self_sum = Reduction([((act_one,), grad_self_query)], "seq", small_term)
    owner_grads = frame_near.astype(jnp.float32) + frame_came.astype(jnp.float32)
    norm_far, owner_grads = advance([self_sum], (norm_far, owner_grads.astype(jnp.bfloat16)))
    norm_came = swap_seq(norm_far)
    grad_encoder = lax.all_to_all(
        owner_grads.reshape(size, owner_frames, model_width),
        "batch",
        split_axis=0,
        concat_axis=0,
        tiled=True,
    )
    advance([cross_sum, self_pair_sum], after=[self_sum])
    advance([self_sum], after=[cross_sum, self_pair_sum])
    norm_came = advance([cross_sum, self_pair_sum], norm_came, after=[self_sum])
    grad_encoder, wide_sum = advance(
        [self_sum], (grad_encoder, wide_sum), after=[cross_sum, self_pair_sum]
    )
    grad_encoder = grad_encoder.astype(jnp.float32)
    grad_hidden = hidden_back(norm_side, norm_came, hidden, gain_self, grad_self)
    wide_sum = wide_sum.astype(jnp.float32) + swap_seq(wide_sum).astype(jnp.float32)
    inner_rows = down_weight.shape[0]
    grad_up_weight = (
        wide_sum[inner_rows:]
        .reshape(blocks, shard_rows, model_width)
        .transpose(1, 0, 2)
        .reshape(shard_rows, wide_cols)
    )
    grad_cross_kv, grad_cross_out, grad_cross_query, grad_self_out = cross_sum.result()
    grad_self_keys = self_pair_sum.result()[0]
    grad_self_queries, small_sum = self_sum.result()
    return (
        result[None],
        grad_hidden[None],
        grad_encoder,
        small_sum[:, :4],
        small_sum[:, 4:8],
        jnp.concatenate([grad_self_queries, grad_self_keys], axis=1),
        grad_self_out,
        grad_cross_query,
        grad_cross_kv,
        grad_cross_out,
        small_sum[:, 8:15],
        grad_up_weight,
        small_sum[:, 15:small_cols].reshape(-1),
        wide_sum[:inner_rows],
    )


def solution(mesh):
    in_specs = (
        P("batch", "seq", None),
        P(None, ("batch", "seq"), None),
        P("batch", "seq", None),
        P("batch"),
        P("batch"),
        P("batch"),
        P("batch"),
        P(),
        P("batch", None),
        P("batch", None),
        P("batch", None),
        P("batch", None),
        P("batch", None),
        P("batch", None),
        P("batch", None),
        P("batch", None),
        P("batch", None),
        P("batch"),
        P("batch", None),
    )
    out_specs = (
        P("batch", "seq", None),
        P("batch", "seq", None),
        P(None, ("batch", "seq"), None),
        P("batch", None),
        P("batch", None),
        P("batch", None),
        P("batch", None),
        P("batch", None),
        P("batch", None),
        P("batch", None),
        P("batch", None),
        P("batch", None),
        P("batch"),
        P("batch", None),
    )
    return jax.shard_map(body, mesh=mesh, in_specs=in_specs, out_specs=out_specs, check_vma=False)
```
